512 devices in a mesh: dp: 32 (over z_lo, y), mp: 16 (over z_hi, x, core).
Axes of the slice: x: 4, y: 4, z: 16 (z_hi: 2, z_lo: 8; z = z_hi * 8 + z_lo), core: 2. Of those that a mesh axis runs over, the one named last changes fastest.
Arguments:
- hidden_in: bfloat16 [12288, 2048], P(('dp', 'mp')), may hold values from -12 to 12
- segment_ids: int32 [32, 384], P('dp'), may hold values from 0 to 7, never falling along the last dimension, each value on 1 to 192 neighbouring positions
- page_table: int32 [32, 3], P('dp'), may hold values from 0 to 2, each once within a row
- qkv_master: float32 [2048, 6144], P(('dp', 'mp')), may hold values from -0.3 to 0.3
- up_master: float32 [2048, 8192], P(('dp', 'mp')), may hold values from -0.125 to 0.125
- dense_weight: bfloat16 [2048, 2048], P('mp'), may hold values from -0.125 to 0.125
Outputs:
- hidden_out: bfloat16 [12288, 2048], P(('dp', 'mp'))
- activated: bfloat16 [12288, 8192], P('dp', 'mp')
- cache_pages: bfloat16 [96, 2, 16, 128, 128], P('dp', None, 'mp')
The draws below stay inside these ranges and needn't reach their ends.
Inputs may be any that keep to these rules, and one draw needn't show every extreme that they name: `segment_ids`: within a group segment ids never fall; each request holds 1 to 192 tokens and one holds exactly that many. `page_table`: each row names every slot of its group once.
All inputs are finite; a program needn't handle non-finite values.
Results may differ from the reference program's by a relative error of at most 0.015.
Values may be sent and summed in bfloat16 or wider, within the bound.
A program may use at most 64 MiB of HBM per device.

```python
import math
import jax
import jax.numpy as jnp
import numpy as np
from jax import lax

D = 2048
H = 16
HD = 128
FF = 8192
PAGE = 128
PAGES_GRP = 3
SEGS = 8
TOK_GRP = 384
TOKENS = 12288
PAGES = 96
N_DP = 32
N_MP = 16


def shared_signs(key):
    row_signs = jax.random.rademacher(jax.random.fold_in(key, 11), (D,), dtype=jnp.int32).astype(jnp.float32)
    head_signs = jax.random.rademacher(jax.random.fold_in(key, 12), (H, HD), dtype=jnp.int32).astype(jnp.float32)
    return (row_signs, head_signs)


def draw_hidden_in(key, part):
    cluster_len = 6
    groups = TOKENS // TOK_GRP
    noise = jax.random.normal(jax.random.fold_in(key, 31), (groups, TOK_GRP, D), jnp.float32)
    starts = jax.random.randint(jax.random.fold_in(key, 32), (groups, 1), 0, TOK_GRP - cluster_len + 1)
    strength = jax.random.uniform(jax.random.fold_in(key, 33), (groups, 1, 1), jnp.float32, 1.0, 2.0)
    places = jnp.arange(TOK_GRP)[None, :]
    inside = ((places >= starts) & (places < starts + cluster_len)).astype(jnp.float32)[:, :, None]
    row_signs, head_signs = shared_signs(key)
    values = noise + inside * strength * row_signs[None, None, :]
    values = jnp.clip(values, -12.0, 12.0)
    return values.reshape(TOKENS, D).astype(jnp.bfloat16)


def draw_qkv_master(key, part):
    scale = 1.0 / math.sqrt(D)
    base = jax.random.normal(jax.random.fold_in(key, 41), (D, H, 3, HD), jnp.float32) * scale
    row_signs, head_signs = shared_signs(key)
    amplitude = math.sqrt(450.0 * math.sqrt(HD) / D) / (math.sqrt(D) * math.sqrt(HD))
    extra = amplitude * row_signs[:, None, None] * head_signs[None, :, :]
    zeros = jnp.zeros_like(extra)
    added = jnp.stack([extra, extra, zeros], 2)
    values = jnp.clip(base + added, -0.3, 0.3)
    return values.reshape(D, 3 * D)


def steps_of(own_key, shape, cuts, smallest, high):
    loudness, own = 1.0, jax.random.fold_in(own_key, 6)
    for position, shards_of in cuts:
        draws = jnp.exp(jax.random.uniform(jax.random.fold_in(own, position), (shards_of,), jnp.float32, smallest / len(cuts), high / len(cuts)))
        loudness = loudness * jnp.repeat(draws, shape[position] // shards_of).reshape([-1 if axis == position else 1 for axis in range(len(shape))])
    return loudness


def length_profile(count, total, limit, lean):
    portions = [(1 << 20) // math.isqrt(standing ** lean) + 1 for standing in range(2, count + 1)]
    spare, holding = total - limit - (count - 1), [1] * (count - 1)
    while spare > 0:
        movable = [i for i in range(count - 1) if holding[i] < limit]
        mass, budget = sum([portions[i] for i in movable]), spare
        for i in movable:
            more = min(limit - holding[i], max(1, budget * portions[i] // mass), spare)
            holding[i] = holding[i] + more
            spare = spare - more
    return np.array([limit] + holding)


def uneven_parts(key, number_of, total, bound, skew):
    if number_of == 2:
        one = jax.random.randint(key, (), max(1, total - bound), min(bound, total - 1) + 1)
        return jnp.stack([one, total - one])
    tallies = jnp.asarray(length_profile(number_of, total, bound, skew), jnp.int32)
    pairs = (number_of - 1) // 2
    donor, taker = tallies[1:1 + 2 * pairs:2], tallies[2:2 + 2 * pairs:2]
    slack = jnp.minimum(donor - 1, bound - taker)
    moved = jax.random.randint(jax.random.fold_in(key, 1), (pairs,), 0, 1 << 20) % (slack + 1)
    tallies = tallies.at[1:1 + 2 * pairs:2].set(donor - moved).at[2:2 + 2 * pairs:2].set(taker + moved)
    return tallies[jax.random.permutation(jax.random.fold_in(key, 2), number_of)]


def centred(own_key, extent, deviation, most, cuts=(), kind=jnp.bfloat16):
    loudness = steps_of(own_key, extent, cuts, -0.22, 0.18) if cuts else 1.0
    values = jax.random.normal(own_key, extent, jnp.float32) * deviation * loudness
    return jnp.minimum(jnp.maximum(values, -most), most).astype(kind)


def setup_inputs(seed: int = 0) -> dict:
    seeds = jax.random.split(jax.random.key(seed), 7)
    return {
        "hidden_in": draw_hidden_in(jax.random.fold_in(seeds[6], 71), 0),
        "segment_ids": jax.vmap(lambda own: jnp.searchsorted(jnp.cumsum(uneven_parts(own, SEGS, TOK_GRP, TOK_GRP // 2, 2)), jnp.arange(TOK_GRP), side="right"))(jax.random.split(seeds[1], N_DP)).reshape((N_DP, TOK_GRP)).astype(jnp.int32),
        "page_table": jax.vmap(lambda own: jax.random.permutation(own, PAGES_GRP))(jax.random.split(seeds[2], N_DP)).reshape((N_DP, PAGES_GRP)).astype(jnp.int32),
        "qkv_master": draw_qkv_master(jax.random.fold_in(seeds[6], 71), 0),
        "up_master": centred(seeds[4], (D, FF), D ** -0.5, 0.125, ((0, 512),), jnp.float32),
        "dense_weight": centred(seeds[5], (D, D), D ** -0.5, 0.125, ((0, 16),)),
    }


def layer_norm(values):
    mean_val = lax.optimization_barrier(jnp.mean(values, -1, keepdims=True))
    centered = values - mean_val
    variance = lax.optimization_barrier(jnp.mean(centered * centered, -1, keepdims=True))
    return centered * lax.rsqrt(variance + 1e-05)

def reference(hidden_in, segment_ids, page_table, qkv_master, up_master, dense_weight):
    qkv_w = qkv_master.astype(jnp.bfloat16)
    up_w = up_master.astype(jnp.bfloat16)
    slopes = jnp.exp2(-8.0 * (jnp.arange(H) + 1).astype(jnp.float32) / H)
    positions = jnp.arange(TOK_GRP)
    distance = (positions[:, None] - positions[None, :]).astype(jnp.float32)
    dense_blocks = dense_weight.reshape(N_MP, D // N_MP, D).astype(jnp.float32)

    def one_group(inputs):
        tokens, segment, table = inputs
        normed = layer_norm(tokens.astype(jnp.float32)).astype(jnp.bfloat16)
        joined = jnp.dot(normed, qkv_w, preferred_element_type=jnp.float32).astype(jnp.bfloat16)
        joined = joined.reshape(TOK_GRP, H, 3, HD)
        query = joined[:, :, 0].transpose(1, 0, 2)
        keys = joined[:, :, 1].transpose(1, 0, 2)
        vals = joined[:, :, 2].transpose(1, 0, 2)
        allowed = (segment[:, None] == segment[None, :]) & (distance >= 0)

        def one_head(head_in):
            head_query, head_keys, head_vals, slope = head_in
            scores = jnp.dot(head_query, head_keys.T, preferred_element_type=jnp.float32) / jnp.sqrt(jnp.float32(HD))
            scores = jnp.where(allowed, scores - slope * distance, -jnp.inf)
            probs = jax.nn.softmax(scores, axis=-1).astype(jnp.bfloat16)
            return jnp.dot(probs, head_vals, preferred_element_type=jnp.float32).astype(jnp.bfloat16)
        context = lax.map(one_head, (query, keys, vals, slopes))
        context = context.transpose(1, 0, 2).reshape(TOK_GRP, D)
        blocks = context.reshape(TOK_GRP, N_MP, D // N_MP).astype(jnp.float32)
        terms = jnp.einsum('tgc,gce->gte', blocks, dense_blocks)
        terms = lax.optimization_barrier(terms.astype(jnp.bfloat16)).astype(jnp.float32)
        stream = tokens.astype(jnp.float32) + lax.optimization_barrier(jnp.sum(terms, 0))
        normed_two = layer_norm(stream).astype(jnp.bfloat16)
        upper = jnp.dot(normed_two, up_w, preferred_element_type=jnp.float32)
        activated = jax.nn.gelu(upper, approximate=True).astype(jnp.bfloat16)
        key_vals = jnp.stack([joined[:, :, 1], joined[:, :, 2]], 1)
        key_vals = key_vals.reshape(PAGES_GRP, PAGE, 2, H, HD).transpose(0, 2, 3, 1, 4)
        cache = jnp.zeros((PAGES_GRP, 2, H, PAGE, HD), jnp.bfloat16).at[table].set(key_vals)
        return (stream.astype(jnp.bfloat16), activated, cache)
    grouped = hidden_in.reshape(N_DP, TOK_GRP, D)
    hidden_out, activated, cache = lax.map(one_group, (grouped, segment_ids, page_table))
    return (hidden_out.reshape(TOKENS, D), activated.reshape(TOKENS, FF), cache.reshape(PAGES, 2, H, PAGE, HD))
```

```python
import jax
import jax.numpy as jnp
from jax import lax
from jax.sharding import PartitionSpec as P

H = 16
HD = 128
PAGE = 128


def layer_norm(values):
    mean_val = jnp.mean(values, -1, keepdims=True)
    centered = values - mean_val
    variance = jnp.mean(centered * centered, -1, keepdims=True)
    return centered * lax.rsqrt(variance + 1e-05)


def gather_rows(x, axis):
    n = lax.axis_size(axis)
    tiled = jnp.concatenate([x] * n, axis=0)
    return lax.all_to_all(tiled, axis, split_axis=0, concat_axis=0, tiled=True)


def attend(normed, qkv_w, segment, table, mp_index):
    group_rows = normed.shape[0]
    heads_dev = qkv_w.shape[1] // (3 * HD)
    joined = jnp.dot(normed, qkv_w, preferred_element_type=jnp.float32).astype(jnp.bfloat16)
    joined = joined.reshape(group_rows, heads_dev, 3, HD)
    query = joined[:, :, 0]
    keys = joined[:, :, 1]
    vals = joined[:, :, 2]
    head_ids = mp_index * heads_dev + jnp.arange(heads_dev)
    slopes = jnp.exp2(-8.0 * (head_ids + 1).astype(jnp.float32) / H)
    positions = jnp.arange(group_rows)
    distance = (positions[:, None] - positions[None, :]).astype(jnp.float32)
    allowed = (segment[:, None] == segment[None, :]) & (distance >= 0)
    scores = jnp.einsum("thd,shd->hts", query, keys, preferred_element_type=jnp.float32) / jnp.sqrt(
        jnp.float32(HD)
    )
    scores = scores - slopes[:, None, None] * distance[None]
    scores = jnp.where(allowed[None], scores, -jnp.inf)
    probs = jax.nn.softmax(scores, axis=-1).astype(jnp.bfloat16)
    context = jnp.einsum("hts,shd->thd", probs, vals, preferred_element_type=jnp.float32).astype(
        jnp.bfloat16
    )
    context = context.reshape(group_rows, heads_dev * HD)
    key_vals = jnp.stack([keys, vals], 1)
    pages_here = group_rows // PAGE
    key_vals = key_vals.reshape(pages_here, PAGE, 2, heads_dev, HD).transpose(0, 2, 3, 1, 4)
    cache = jnp.zeros((pages_here, 2, heads_dev, PAGE, HD), jnp.bfloat16).at[table].set(key_vals)
    return (context, cache)


def local(hidden_in, segment_ids, page_table, qkv_master, up_master, dense_weight):
    mp_count = lax.axis_size("mp")
    mp_index = lax.axis_index("mp")
    qkv_bf = qkv_master.astype(jnp.bfloat16)
    up_bf = up_master.astype(jnp.bfloat16)
    qkv_w = gather_rows(
        lax.all_to_all(qkv_bf, "mp", split_axis=1, concat_axis=0, tiled=True), "dp"
    )
    up_w = gather_rows(
        lax.all_to_all(up_bf, "mp", split_axis=1, concat_axis=0, tiled=True), "dp"
    )
    normed_own = layer_norm(hidden_in.astype(jnp.float32)).astype(jnp.bfloat16)
    normed = gather_rows(normed_own, "mp")
    context, cache = attend(normed, qkv_w, segment_ids[0], page_table[0], mp_index)
    partial = jnp.dot(context, dense_weight, preferred_element_type=jnp.float32).astype(jnp.bfloat16)
    parts = lax.all_to_all(partial, "mp", split_axis=0, concat_axis=0, tiled=True)
    rows = hidden_in.shape[0]
    share = jnp.sum(parts.reshape(mp_count, rows, -1).astype(jnp.float32), axis=0)
    stream_own = hidden_in.astype(jnp.float32) + share
    normed_two = gather_rows(layer_norm(stream_own).astype(jnp.bfloat16), "mp")
    upper = jnp.dot(normed_two, up_w, preferred_element_type=jnp.float32)
    activated = jax.nn.gelu(upper, approximate=True).astype(jnp.bfloat16)
    return (stream_own.astype(jnp.bfloat16), activated, cache)


def solution(mesh):
    placed = (
        P(("dp", "mp"), None),
        P("dp", None),
        P("dp", None),
        P(("dp", "mp"), None),
        P(("dp", "mp"), None),
        P("mp", None),
    )
    return jax.shard_map(
        local,
        mesh=mesh,
        in_specs=placed,
        out_specs=(P(("dp", "mp"), None), P("dp", "mp"), P("dp", None, "mp", None, None)),
        check_vma=False,
    )
```

```python
import functools

import jax
import jax.numpy as jnp
from jax import lax
from jax.experimental import pallas as pl
from jax.experimental.pallas import tpu as pltpu
from jax.sharding import PartitionSpec as P

H = 16
HD = 128
PAGE = 128
MESH = pl.DeviceIdType.MESH


def layer_norm(values):
    mean_val = jnp.mean(values, -1, keepdims=True)
    centered = values - mean_val
    variance = jnp.mean(centered * centered, -1, keepdims=True)
    return centered * lax.rsqrt(variance + 1e-05)


def exchange_kernel(n, axis, spread, count, *refs):
    ins, outs = refs[:count], refs[count:2 * count]
    send_sem, recv_sem = refs[2 * count], refs[2 * count + 1]
    me = lax.axis_index(axis)
    barrier = pltpu.get_barrier_semaphore()
    for step in range(1, n):
        peer = lax.rem(me + step, n)
        pl.semaphore_signal(barrier, inc=1, device_id={axis: peer}, device_id_type=MESH)
    pl.semaphore_wait(barrier, n - 1)
    copies = []
    for a in range(count):
        for step in range(1, n):
            peer = lax.rem(me + step, n)
            src = ins[a].at[peer] if spread else ins[a]
            slot = a * (n - 1) + step - 1
            copy = pltpu.make_async_remote_copy(
                src_ref=src,
                dst_ref=outs[a].at[me],
                send_sem=send_sem.at[slot],
                recv_sem=recv_sem.at[slot],
                device_id={axis: peer},
                device_id_type=MESH,
            )
            copy.start()
            copies.append(copy)
    for a in range(count):
        outs[a][me] = ins[a][me] if spread else ins[a][...]
    for copy in copies:
        copy.wait()


def exchange(xs, axis, spread, cid):
    n = lax.axis_size(axis)
    count = len(xs)
    outs = [
        jax.ShapeDtypeStruct((n,) + (x.shape[1:] if spread else x.shape), x.dtype) for x in xs
    ]
    return pl.pallas_call(
        functools.partial(exchange_kernel, n, axis, spread, count),
        out_shape=outs,
        in_specs=[pl.BlockSpec(memory_space=pltpu.VMEM)] * count,
        out_specs=[pl.BlockSpec(memory_space=pltpu.VMEM)] * count,
        scratch_shapes=[
            pltpu.SemaphoreType.DMA((count * (n - 1),)),
            pltpu.SemaphoreType.DMA((count * (n - 1),)),
        ],
        compiler_params=pltpu.CompilerParams(collective_id=cid, has_side_effects=True),
    )(*xs)


def attend(normed, qkv_w, segment, table, mp_index):
    group_rows = normed.shape[0]
    heads_dev = qkv_w.shape[1] // (3 * HD)
    joined = jnp.dot(normed, qkv_w, preferred_element_type=jnp.float32).astype(jnp.bfloat16)
    joined = joined.reshape(group_rows, heads_dev, 3, HD)
    query = joined[:, :, 0]
    keys = joined[:, :, 1]
    vals = joined[:, :, 2]
    head_ids = mp_index * heads_dev + jnp.arange(heads_dev)
    slopes = jnp.exp2(-8.0 * (head_ids + 1).astype(jnp.float32) / H)
    positions = jnp.arange(group_rows)
    distance = (positions[:, None] - positions[None, :]).astype(jnp.float32)
    allowed = (segment[:, None] == segment[None, :]) & (distance >= 0)
    scores = jnp.einsum("thd,shd->hts", query, keys, preferred_element_type=jnp.float32) / jnp.sqrt(
        jnp.float32(HD)
    )
    scores = scores - slopes[:, None, None] * distance[None]
    scores = jnp.where(allowed[None], scores, -jnp.inf)
    probs = jax.nn.softmax(scores, axis=-1).astype(jnp.bfloat16)
    context = jnp.einsum("hts,shd->thd", probs, vals, preferred_element_type=jnp.float32).astype(
        jnp.bfloat16
    )
    context = context.reshape(group_rows, heads_dev * HD)
    key_vals = jnp.stack([keys, vals], 1)
    pages_here = group_rows // PAGE
    key_vals = key_vals.reshape(pages_here, PAGE, 2, heads_dev, HD).transpose(0, 2, 3, 1, 4)
    cache = jnp.zeros((pages_here, 2, heads_dev, PAGE, HD), jnp.bfloat16).at[table].set(key_vals)
    return (context, cache)


def local(hidden_in, segment_ids, page_table, qkv_master, up_master, dense_weight):
    mp_count = lax.axis_size("mp")
    mp_index = lax.axis_index("mp")
    rows_w = qkv_master.shape[0]
    qkv_t = qkv_master.astype(jnp.bfloat16).reshape(rows_w, mp_count, -1).transpose(1, 0, 2)
    up_t = up_master.astype(jnp.bfloat16).reshape(rows_w, mp_count, -1).transpose(1, 0, 2)
    qkv_blk, up_blk = exchange([qkv_t, up_t], "mp", True, 0)
    qkv_g, up_g = exchange(
        [qkv_blk.reshape(mp_count * rows_w, -1), up_blk.reshape(mp_count * rows_w, -1)],
        "dp",
        False,
        1,
    )
    qkv_w = qkv_g.reshape(-1, qkv_g.shape[-1])
    up_w = up_g.reshape(-1, up_g.shape[-1])
    rows = hidden_in.shape[0]
    normed_own = layer_norm(hidden_in.astype(jnp.float32)).astype(jnp.bfloat16)
    normed = exchange([normed_own], "mp", False, 2)[0].reshape(mp_count * rows, -1)
    context, cache = attend(normed, qkv_w, segment_ids[0], page_table[0], mp_index)
    partial = jnp.dot(context, dense_weight, preferred_element_type=jnp.float32).astype(jnp.bfloat16)
    parts = exchange([partial.reshape(mp_count, rows, -1)], "mp", True, 3)[0]
    share = jnp.sum(parts.astype(jnp.float32), axis=0)
    stream_own = hidden_in.astype(jnp.float32) + share
    normed_two = exchange([layer_norm(stream_own).astype(jnp.bfloat16)], "mp", False, 4)[0]
    normed_two = normed_two.reshape(mp_count * rows, -1)
    upper = jnp.dot(normed_two, up_w, preferred_element_type=jnp.float32)
    activated = jax.nn.gelu(upper, approximate=True).astype(jnp.bfloat16)
    return (stream_own.astype(jnp.bfloat16), activated, cache)


def solution(mesh):
    placed = (
        P(("dp", "mp"), None),
        P("dp", None),
        P("dp", None),
        P(("dp", "mp"), None),
        P(("dp", "mp"), None),
        P("mp", None),
    )
    return jax.shard_map(
        local,
        mesh=mesh,
        in_specs=placed,
        out_specs=(P(("dp", "mp"), None), P("dp", "mp"), P("dp", None, "mp", None, None)),
        check_vma=False,
    )
```

```python
import functools

import jax
import jax.numpy as jnp
from jax import lax
from jax.experimental import pallas as pl
from jax.experimental.pallas import tpu as pltpu
from jax.sharding import PartitionSpec as P

H = 16
HD = 128
PAGE = 128
MESH = pl.DeviceIdType.MESH
RING = 4


def layer_norm(values):
    mean_val = jnp.mean(values, -1, keepdims=True)
    centered = values - mean_val
    variance = jnp.mean(centered * centered, -1, keepdims=True)
    return centered * lax.rsqrt(variance + 1e-05)


def exchange_kernel(n, axis, spread, count, *refs):
    ins, outs = refs[:count], refs[count:2 * count]
    send_sem, recv_sem = refs[2 * count], refs[2 * count + 1]
    me = lax.axis_index(axis)
    barrier = pltpu.get_barrier_semaphore()
    for step in range(1, n):
        peer = lax.rem(me + step, n)
        pl.semaphore_signal(barrier, inc=1, device_id={axis: peer}, device_id_type=MESH)
    pl.semaphore_wait(barrier, n - 1)
    copies = []
    for a in range(count):
        for step in range(1, n):
            peer = lax.rem(me + step, n)
            src = ins[a].at[peer] if spread else ins[a]
            slot = a * (n - 1) + step - 1
            copy = pltpu.make_async_remote_copy(
                src_ref=src,
                dst_ref=outs[a].at[me],
                send_sem=send_sem.at[slot],
                recv_sem=recv_sem.at[slot],
                device_id={axis: peer},
                device_id_type=MESH,
            )
            copy.start()
            copies.append(copy)
    for a in range(count):
        outs[a][me] = ins[a][me] if spread else ins[a][...]
    for copy in copies:
        copy.wait()


def exchange(xs, axis, spread, cid):
    n = lax.axis_size(axis)
    count = len(xs)
    outs = [
        jax.ShapeDtypeStruct((n,) + (x.shape[1:] if spread else x.shape), x.dtype) for x in xs
    ]
    return pl.pallas_call(
        functools.partial(exchange_kernel, n, axis, spread, count),
        out_shape=outs,
        in_specs=[pl.BlockSpec(memory_space=pltpu.VMEM)] * count,
        out_specs=[pl.BlockSpec(memory_space=pltpu.VMEM)] * count,
        scratch_shapes=[
            pltpu.SemaphoreType.DMA((count * (n - 1),)),
            pltpu.SemaphoreType.DMA((count * (n - 1),)),
        ],
        compiler_params=pltpu.CompilerParams(collective_id=cid, has_side_effects=True),
    )(*xs)


def _remote(src, dst, send_sem, recv_sem, axis, peer):
    return pltpu.make_async_remote_copy(
        src_ref=src,
        dst_ref=dst,
        send_sem=send_sem,
        recv_sem=recv_sem,
        device_id={axis: peer},
        device_id_type=MESH,
    )


def dp_gather_kernel(lines, ring, x_ref, o_ref, send_sem, recv_sem):
    me = lax.axis_index("dp")
    z, y = me // ring, me % ring
    barrier = pltpu.get_barrier_semaphore()
    has_left, has_right = z > 0, z < lines - 1

    def signal(peer):
        pl.semaphore_signal(barrier, inc=1, device_id={"dp": peer}, device_id_type=MESH)

    pl.when(has_left)(lambda: signal(me - ring))
    pl.when(has_right)(lambda: signal(me + ring))
    for k in range(1, ring):
        signal(z * ring + (y + k) % ring)
    n_line = has_left.astype(jnp.int32) + has_right.astype(jnp.int32)
    pl.semaphore_wait(barrier, n_line + (ring - 1))

    sends = []
    counter = [0]

    def send(cond, src, src_z, peer):
        slot = src_z * ring + y
        copy = _remote(src, o_ref.at[src_z, y], send_sem.at[counter[0]], recv_sem.at[slot], "dp", peer)
        counter[0] += 1
        pl.when(cond)(copy.start)
        sends.append((cond, copy))

    def spread(cond, src, src_z):
        for k in range(1, ring):
            send(cond, src, src_z, z * ring + (y + k) % ring)

    def arrive(cond, src_z, peer):
        slot = src_z * ring + y
        copy = _remote(o_ref.at[src_z, y], o_ref.at[src_z, y], send_sem.at[0], recv_sem.at[slot], "dp", peer)
        pl.when(cond)(copy.wait_recv)

    true = z >= 0
    send(has_right, x_ref, z, me + ring)
    send(has_left, x_ref, z, me - ring)
    spread(true, x_ref, z)
    o_ref[z, y] = x_ref[...]
    for s in range(1, lines):
        from_left = z - s >= 0
        src_l = jnp.maximum(z - s, 0)
        arrive(from_left, src_l, me - ring)
        send(from_left & has_right, o_ref.at[src_l, y], src_l, me + ring)
        spread(from_left, o_ref.at[src_l, y], src_l)
        from_right = z + s <= lines - 1
        src_r = jnp.minimum(z + s, lines - 1)
        arrive(from_right, src_r, me + ring)
        send(from_right & has_left, o_ref.at[src_r, y], src_r, me - ring)
        spread(from_right, o_ref.at[src_r, y], src_r)
    for k in range(1, ring):
        yy = (y + k) % ring
        for zz in range(lines):
            slot = zz * ring + yy
            copy = _remote(o_ref.at[zz, yy], o_ref.at[zz, yy], send_sem.at[0], recv_sem.at[slot], "dp", z * ring + yy)
            copy.wait_recv()
    for cond, copy in sends:
        pl.when(cond)(copy.wait_send)


def dp_gather(x, lines, ring, cid):
    n_sends = 1 + ring + (lines - 1) * 2 * ring
    return pl.pallas_call(
        functools.partial(dp_gather_kernel, lines, ring),
        out_shape=jax.ShapeDtypeStruct((lines, ring) + x.shape, x.dtype),
        in_specs=[pl.BlockSpec(memory_space=pltpu.VMEM)],
        out_specs=pl.BlockSpec(memory_space=pltpu.VMEM),
        scratch_shapes=[
            pltpu.SemaphoreType.DMA((n_sends,)),
            pltpu.SemaphoreType.DMA((lines * ring,)),
        ],
        compiler_params=pltpu.CompilerParams(collective_id=cid, has_side_effects=True),
    )(x)


def mp_gather_kernel(halves, chips, cores, x_ref, o_ref, send_sem, recv_sem):
    me = lax.axis_index("mp")
    h, c, k = me // (chips * cores), (me // cores) % chips, me % cores
    per_half = chips * cores
    barrier = pltpu.get_barrier_semaphore()
    far = (1 - h) * per_half + c * cores + k
    twin = h * per_half + c * cores + (1 - k)
    mates = [h * per_half + ((c + j) % chips) * cores + k for j in range(1, chips)]
    for peer in [far, twin] + mates:
        pl.semaphore_signal(barrier, inc=1, device_id={"mp": peer}, device_id_type=MESH)
    pl.semaphore_wait(barrier, 2 + len(mates))

    sends = []

    def send(src, hh, cc, kk, peer):
        slot = (hh * chips + cc) * cores + kk
        copy = _remote(src, o_ref.at[hh, cc, kk], send_sem.at[len(sends)], recv_sem.at[slot], "mp", peer)
        copy.start()
        sends.append(copy)

    def arrive(hh, cc, kk, peer):
        slot = (hh * chips + cc) * cores + kk
        copy = _remote(o_ref.at[hh, cc, kk], o_ref.at[hh, cc, kk], send_sem.at[0], recv_sem.at[slot], "mp", peer)
        copy.wait_recv()

    send(x_ref, h, c, k, far)
    for peer in mates:
        send(x_ref, h, c, k, peer)
    send(x_ref, h, c, k, twin)
    o_ref[h, c, k] = x_ref[...]
    arrive(1 - h, c, k, far)
    for peer in mates:
        send(o_ref.at[1 - h, c, k], 1 - h, c, k, peer)
    send(o_ref.at[1 - h, c, k], 1 - h, c, k, twin)
    for j in range(1, chips):
        cc = (c + j) % chips
        for hh in (h, 1 - h):
            arrive(hh, cc, k, mates[j - 1])
            send(o_ref.at[hh, cc, k], hh, cc, k, twin)
    for hh in range(2):
        for cc in range(chips):
            arrive(hh, cc, 1 - k, twin)
    for copy in sends:
        copy.wait_send()


def mp_gather(x, chips, cid):
    return pl.pallas_call(
        functools.partial(mp_gather_kernel, 2, chips, 2),
        out_shape=jax.ShapeDtypeStruct((2, chips, 2) + x.shape, x.dtype),
        in_specs=[pl.BlockSpec(memory_space=pltpu.VMEM)],
        out_specs=pl.BlockSpec(memory_space=pltpu.VMEM),
        scratch_shapes=[
            pltpu.SemaphoreType.DMA((2 * chips * 2,)),
            pltpu.SemaphoreType.DMA((2 * chips * 2,)),
        ],
        compiler_params=pltpu.CompilerParams(collective_id=cid, has_side_effects=True),
    )(x)


def attend(normed, qkv_w, segment, table, mp_index):
    group_rows = normed.shape[0]
    heads_dev = qkv_w.shape[1] // (3 * HD)
    joined = jnp.dot(normed, qkv_w, preferred_element_type=jnp.float32).astype(jnp.bfloat16)
    joined = joined.reshape(group_rows, heads_dev, 3, HD)
    query = joined[:, :, 0]
    keys = joined[:, :, 1]
    vals = joined[:, :, 2]
    head_ids = mp_index * heads_dev + jnp.arange(heads_dev)
    slopes = jnp.exp2(-8.0 * (head_ids + 1).astype(jnp.float32) / H)
    positions = jnp.arange(group_rows)
    distance = (positions[:, None] - positions[None, :]).astype(jnp.float32)
    allowed = (segment[:, None] == segment[None, :]) & (distance >= 0)
    scores = jnp.einsum("thd,shd->hts", query, keys, preferred_element_type=jnp.float32) / jnp.sqrt(
        jnp.float32(HD)
    )
    scores = scores - slopes[:, None, None] * distance[None]
    scores = jnp.where(allowed[None], scores, -jnp.inf)
    probs = jax.nn.softmax(scores, axis=-1).astype(jnp.bfloat16)
    context = jnp.einsum("hts,shd->thd", probs, vals, preferred_element_type=jnp.float32).astype(
        jnp.bfloat16
    )
    context = context.reshape(group_rows, heads_dev * HD)
    key_vals = jnp.stack([keys, vals], 1)
    pages_here = group_rows // PAGE
    key_vals = key_vals.reshape(pages_here, PAGE, 2, heads_dev, HD).transpose(0, 2, 3, 1, 4)
    cache = jnp.zeros((pages_here, 2, heads_dev, PAGE, HD), jnp.bfloat16).at[table].set(key_vals)
    return (context, cache)


def local(hidden_in, segment_ids, page_table, qkv_master, up_master, dense_weight):
    mp_count = lax.axis_size("mp")
    mp_index = lax.axis_index("mp")
    rows_w = qkv_master.shape[0]
    qkv_t = qkv_master.astype(jnp.bfloat16).reshape(rows_w, mp_count, -1).transpose(1, 0, 2)
    up_t = up_master.astype(jnp.bfloat16).reshape(rows_w, mp_count, -1).transpose(1, 0, 2)
    qkv_blk, up_blk = exchange([qkv_t, up_t], "mp", True, 0)
    dp_count = lax.axis_size("dp")
    width = qkv_t.shape[-1]
    both = jnp.concatenate(
        [qkv_blk.reshape(mp_count * rows_w, -1), up_blk.reshape(mp_count * rows_w, -1)], axis=1
    )
    gathered = dp_gather(both, dp_count // RING, RING, 1)
    gathered = gathered.reshape(-1, gathered.shape[-1])
    qkv_w = gathered[:, :width]
    up_w = gathered[:, width:]
    rows = hidden_in.shape[0]
    normed_own = layer_norm(hidden_in.astype(jnp.float32)).astype(jnp.bfloat16)
    normed = mp_gather(normed_own, mp_count // 4, 2).reshape(mp_count * rows, -1)
    context, cache = attend(normed, qkv_w, segment_ids[0], page_table[0], mp_index)
    partial = jnp.dot(context, dense_weight, preferred_element_type=jnp.float32).astype(jnp.bfloat16)
    parts = exchange([partial.reshape(mp_count, rows, -1)], "mp", True, 3)[0]
    share = jnp.sum(parts.astype(jnp.float32), axis=0)
    stream_own = hidden_in.astype(jnp.float32) + share
    normed_two = mp_gather(layer_norm(stream_own).astype(jnp.bfloat16), mp_count // 4, 4)
    normed_two = normed_two.reshape(mp_count * rows, -1)
    upper = jnp.dot(normed_two, up_w, preferred_element_type=jnp.float32)
    activated = jax.nn.gelu(upper, approximate=True).astype(jnp.bfloat16)
    return (stream_own.astype(jnp.bfloat16), activated, cache)


def solution(mesh):
    placed = (
        P(("dp", "mp"), None),
        P("dp", None),
        P("dp", None),
        P(("dp", "mp"), None),
        P(("dp", "mp"), None),
        P("mp", None),
    )
    return jax.shard_map(
        local,
        mesh=mesh,
        in_specs=placed,
        out_specs=(P(("dp", "mp"), None), P("dp", "mp"), P("dp", None, "mp", None, None)),
        check_vma=False,
    )
```

```python
import functools

import jax
import jax.numpy as jnp
from jax import lax
from jax.experimental import pallas as pl
from jax.experimental.pallas import tpu as pltpu
from jax.sharding import PartitionSpec as P

H = 16
HD = 128
PAGE = 128
MESH = pl.DeviceIdType.MESH
RING = 4


def layer_norm(values):
    mean_val = jnp.mean(values, -1, keepdims=True)
    centered = values - mean_val
    variance = jnp.mean(centered * centered, -1, keepdims=True)
    return centered * lax.rsqrt(variance + 1e-05)


def exchange_kernel(n, axis, spread, count, *refs):
    ins, outs = refs[:count], refs[count:2 * count]
    send_sem, recv_sem = refs[2 * count], refs[2 * count + 1]
    me = lax.axis_index(axis)
    barrier = pltpu.get_barrier_semaphore()
    for step in range(1, n):
        peer = lax.rem(me + step, n)
        pl.semaphore_signal(barrier, inc=1, device_id={axis: peer}, device_id_type=MESH)
    pl.semaphore_wait(barrier, n - 1)
    copies = []
    for a in range(count):
        for step in range(1, n):
            peer = lax.rem(me + step, n)
            src = ins[a].at[peer] if spread else ins[a]
            slot = a * (n - 1) + step - 1
            copy = pltpu.make_async_remote_copy(
                src_ref=src,
                dst_ref=outs[a].at[me],
                send_sem=send_sem.at[slot],
                recv_sem=recv_sem.at[slot],
                device_id={axis: peer},
                device_id_type=MESH,
            )
            copy.start()
            copies.append(copy)
    for a in range(count):
        outs[a][me] = ins[a][me] if spread else ins[a][...]
    for copy in copies:
        copy.wait()


def exchange(xs, axis, spread, cid):
    n = lax.axis_size(axis)
    count = len(xs)
    outs = [
        jax.ShapeDtypeStruct((n,) + (x.shape[1:] if spread else x.shape), x.dtype) for x in xs
    ]
    return pl.pallas_call(
        functools.partial(exchange_kernel, n, axis, spread, count),
        out_shape=outs,
        in_specs=[pl.BlockSpec(memory_space=pltpu.VMEM)] * count,
        out_specs=[pl.BlockSpec(memory_space=pltpu.VMEM)] * count,
        scratch_shapes=[
            pltpu.SemaphoreType.DMA((count * (n - 1),)),
            pltpu.SemaphoreType.DMA((count * (n - 1),)),
        ],
        compiler_params=pltpu.CompilerParams(collective_id=cid, has_side_effects=True),
    )(*xs)


def _remote(src, dst, send_sem, recv_sem, axis, peer):
    return pltpu.make_async_remote_copy(
        src_ref=src,
        dst_ref=dst,
        send_sem=send_sem,
        recv_sem=recv_sem,
        device_id={axis: peer},
        device_id_type=MESH,
    )


def dp_gather_kernel(lines, ring, x_ref, o_ref, send_sem, recv_sem):
    me = lax.axis_index("dp")
    z, y = me // ring, me % ring
    barrier = pltpu.get_barrier_semaphore()
    has_left, has_right = z > 0, z < lines - 1

    def signal(peer):
        pl.semaphore_signal(barrier, inc=1, device_id={"dp": peer}, device_id_type=MESH)

    pl.when(has_left)(lambda: signal(me - ring))
    pl.when(has_right)(lambda: signal(me + ring))
    for k in range(1, ring):
        signal(z * ring + (y + k) % ring)
    n_line = has_left.astype(jnp.int32) + has_right.astype(jnp.int32)
    pl.semaphore_wait(barrier, n_line + (ring - 1))

    sends = []
    counter = [0]

    def send(cond, src, src_z, peer):
        slot = src_z * ring + y
        copy = _remote(src, o_ref.at[src_z, y], send_sem.at[counter[0]], recv_sem.at[slot], "dp", peer)
        counter[0] += 1
        pl.when(cond)(copy.start)
        sends.append((cond, copy))

    def spread(cond, src, src_z):
        for k in range(1, ring):
            send(cond, src, src_z, z * ring + (y + k) % ring)

    def arrive(cond, src_z, peer):
        slot = src_z * ring + y
        copy = _remote(o_ref.at[src_z, y], o_ref.at[src_z, y], send_sem.at[0], recv_sem.at[slot], "dp", peer)
        pl.when(cond)(copy.wait_recv)

    true = z >= 0
    send(has_right, x_ref, z, me + ring)
    send(has_left, x_ref, z, me - ring)
    spread(true, x_ref, z)
    o_ref[z, y] = x_ref[...]
    for s in range(1, lines):
        from_left = z - s >= 0
        src_l = jnp.maximum(z - s, 0)
        arrive(from_left, src_l, me - ring)
        send(from_left & has_right, o_ref.at[src_l, y], src_l, me + ring)
        spread(from_left, o_ref.at[src_l, y], src_l)
        from_right = z + s <= lines - 1
        src_r = jnp.minimum(z + s, lines - 1)
        arrive(from_right, src_r, me + ring)
        send(from_right & has_left, o_ref.at[src_r, y], src_r, me - ring)
        spread(from_right, o_ref.at[src_r, y], src_r)
    for k in range(1, ring):
        yy = (y + k) % ring
        for zz in range(lines):
            slot = zz * ring + yy
            copy = _remote(o_ref.at[zz, yy], o_ref.at[zz, yy], send_sem.at[0], recv_sem.at[slot], "dp", z * ring + yy)
            copy.wait_recv()
    for cond, copy in sends:
        pl.when(cond)(copy.wait_send)


def dp_gather(x, lines, ring, cid):
    n_sends = 1 + ring + (lines - 1) * 2 * ring
    return pl.pallas_call(
        functools.partial(dp_gather_kernel, lines, ring),
        out_shape=jax.ShapeDtypeStruct((lines, ring) + x.shape, x.dtype),
        in_specs=[pl.BlockSpec(memory_space=pltpu.VMEM)],
        out_specs=pl.BlockSpec(memory_space=pltpu.VMEM),
        scratch_shapes=[
            pltpu.SemaphoreType.DMA((n_sends,)),
            pltpu.SemaphoreType.DMA((lines * ring,)),
        ],
        compiler_params=pltpu.CompilerParams(collective_id=cid, has_side_effects=True),
    )(x)


def mp_gather_kernel(halves, chips, cores, x_ref, o_ref, send_sem, recv_sem):
    me = lax.axis_index("mp")
    h, c, k = me // (chips * cores), (me // cores) % chips, me % cores
    per_half = chips * cores
    barrier = pltpu.get_barrier_semaphore()
    far = (1 - h) * per_half + c * cores + k
    twin = h * per_half + c * cores + (1 - k)
    mates = [h * per_half + ((c + j) % chips) * cores + k for j in range(1, chips)]
    for peer in [far, twin] + mates:
        pl.semaphore_signal(barrier, inc=1, device_id={"mp": peer}, device_id_type=MESH)
    pl.semaphore_wait(barrier, 2 + len(mates))

    sends = []

    def send(src, hh, cc, kk, peer):
        slot = (hh * chips + cc) * cores + kk
        copy = _remote(src, o_ref.at[hh, cc, kk], send_sem.at[len(sends)], recv_sem.at[slot], "mp", peer)
        copy.start()
        sends.append(copy)

    def arrive(hh, cc, kk, peer):
        slot = (hh * chips + cc) * cores + kk
        copy = _remote(o_ref.at[hh, cc, kk], o_ref.at[hh, cc, kk], send_sem.at[0], recv_sem.at[slot], "mp", peer)
        copy.wait_recv()

    send(x_ref, h, c, k, far)
    for peer in mates:
        send(x_ref, h, c, k, peer)
    send(x_ref, h, c, k, twin)
    o_ref[h, c, k] = x_ref[...]
    arrive(1 - h, c, k, far)
    for peer in mates:
        send(o_ref.at[1 - h, c, k], 1 - h, c, k, peer)
    send(o_ref.at[1 - h, c, k], 1 - h, c, k, twin)
    for j in range(1, chips):
        cc = (c + j) % chips
        for hh in (h, 1 - h):
            arrive(hh, cc, k, mates[j - 1])
            send(o_ref.at[hh, cc, k], hh, cc, k, twin)
    for hh in range(2):
        for cc in range(chips):
            arrive(hh, cc, 1 - k, twin)
    for copy in sends:
        copy.wait_send()


def mp_gather(x, chips, cid):
    return pl.pallas_call(
        functools.partial(mp_gather_kernel, 2, chips, 2),
        out_shape=jax.ShapeDtypeStruct((2, chips, 2) + x.shape, x.dtype),
        in_specs=[pl.BlockSpec(memory_space=pltpu.VMEM)],
        out_specs=pl.BlockSpec(memory_space=pltpu.VMEM),
        scratch_shapes=[
            pltpu.SemaphoreType.DMA((2 * chips * 2,)),
            pltpu.SemaphoreType.DMA((2 * chips * 2,)),
        ],
        compiler_params=pltpu.CompilerParams(collective_id=cid, has_side_effects=True),
    )(x)


def mp_sum_kernel(chips, p_ref, o_ref, twin_in, pair, mate_in, far_out, far_in, acc, send_sem, recv_sem):
    me = lax.axis_index("mp")
    per_half = chips * 2
    h, c, k = me // per_half, (me // 2) % chips, me % 2
    far = (1 - h) * per_half + c * 2 + k
    twin = h * per_half + c * 2 + (1 - k)
    mates = [h * per_half + ((c + j) % chips) * 2 + k for j in range(1, chips)]
    barrier = pltpu.get_barrier_semaphore()
    for peer in [far, twin] + mates:
        pl.semaphore_signal(barrier, inc=1, device_id={"mp": peer}, device_id_type=MESH)
    pl.semaphore_wait(barrier, 2 + len(mates))

    sends = []

    def send(src, dst, slot, peer):
        copy = _remote(src, dst, send_sem.at[len(sends)], recv_sem.at[slot], "mp", peer)
        copy.start()
        sends.append(copy)

    def arrive(dst, slot, peer):
        _remote(dst, dst, send_sem.at[0], recv_sem.at[slot], "mp", peer).wait_recv()

    for hh in range(2):
        for cc in range(chips):
            send(p_ref.at[hh, cc, 1 - k], twin_in.at[hh, cc], hh * chips + cc, twin)
    for j in range(1, chips):
        cc = (c + j) % chips
        for hh in range(2):
            arrive(twin_in.at[hh, cc], hh * chips + cc, twin)
            pair[hh, cc] = (
                p_ref[hh, cc, k].astype(jnp.float32) + twin_in[hh, cc].astype(jnp.float32)
            ).astype(pair.dtype)
            send(pair.at[hh, cc], mate_in.at[c, hh], 2 * chips + c * 2 + hh, mates[j - 1])
    for hh in range(2):
        arrive(twin_in.at[hh, c], hh * chips + c, twin)
        acc[hh] = p_ref[hh, c, k].astype(jnp.float32) + twin_in[hh, c].astype(jnp.float32)
    for j in range(1, chips):
        cc = (c + j) % chips
        for hh in range(2):
            arrive(mate_in.at[cc, hh], 2 * chips + cc * 2 + hh, mates[j - 1])
            acc[hh] = acc[hh] + mate_in[cc, hh].astype(jnp.float32)
    far_out[...] = acc[1 - h].astype(far_out.dtype)
    send(far_out, far_in, 4 * chips, far)
    arrive(far_in, 4 * chips, far)
    o_ref[...] = acc[h] + far_in[...].astype(jnp.float32)
    for copy in sends:
        copy.wait_send()


def mp_sum(parts, chips, cid):
    rows, cols = parts.shape[-2:]
    dt = parts.dtype
    return pl.pallas_call(
        functools.partial(mp_sum_kernel, chips),
        out_shape=jax.ShapeDtypeStruct((rows, cols), jnp.float32),
        in_specs=[pl.BlockSpec(memory_space=pltpu.VMEM)],
        out_specs=pl.BlockSpec(memory_space=pltpu.VMEM),
        scratch_shapes=[
            pltpu.VMEM((2, chips, rows, cols), dt),
            pltpu.VMEM((2, chips, rows, cols), dt),
            pltpu.VMEM((chips, 2, rows, cols), dt),
            pltpu.VMEM((rows, cols), dt),
            pltpu.VMEM((rows, cols), dt),
            pltpu.VMEM((2, rows, cols), jnp.float32),
            pltpu.SemaphoreType.DMA((4 * chips + 1,)),
            pltpu.SemaphoreType.DMA((4 * chips + 1,)),
        ],
        compiler_params=pltpu.CompilerParams(collective_id=cid, has_side_effects=True),
    )(parts)


def attend(normed, qkv_w, segment, table, mp_index):
    group_rows = normed.shape[0]
    heads_dev = qkv_w.shape[1] // (3 * HD)
    joined = jnp.dot(normed, qkv_w, preferred_element_type=jnp.float32).astype(jnp.bfloat16)
    joined = joined.reshape(group_rows, heads_dev, 3, HD)
    query = joined[:, :, 0]
    keys = joined[:, :, 1]
    vals = joined[:, :, 2]
    head_ids = mp_index * heads_dev + jnp.arange(heads_dev)
    slopes = jnp.exp2(-8.0 * (head_ids + 1).astype(jnp.float32) / H)
    positions = jnp.arange(group_rows)
    distance = (positions[:, None] - positions[None, :]).astype(jnp.float32)
    allowed = (segment[:, None] == segment[None, :]) & (distance >= 0)
    scores = jnp.einsum("thd,shd->hts", query, keys, preferred_element_type=jnp.float32) / jnp.sqrt(
        jnp.float32(HD)
    )
    scores = scores - slopes[:, None, None] * distance[None]
    scores = jnp.where(allowed[None], scores, -jnp.inf)
    probs = jax.nn.softmax(scores, axis=-1).astype(jnp.bfloat16)
    context = jnp.einsum("hts,shd->thd", probs, vals, preferred_element_type=jnp.float32).astype(
        jnp.bfloat16
    )
    context = context.reshape(group_rows, heads_dev * HD)
    key_vals = jnp.stack([keys, vals], 1)
    pages_here = group_rows // PAGE
    key_vals = key_vals.reshape(pages_here, PAGE, 2, heads_dev, HD).transpose(0, 2, 3, 1, 4)
    cache = jnp.zeros((pages_here, 2, heads_dev, PAGE, HD), jnp.bfloat16).at[table].set(key_vals)
    return (context, cache)


def local(hidden_in, segment_ids, page_table, qkv_master, up_master, dense_weight):
    mp_count = lax.axis_size("mp")
    mp_index = lax.axis_index("mp")
    rows_w = qkv_master.shape[0]
    qkv_t = qkv_master.astype(jnp.bfloat16).reshape(rows_w, mp_count, -1).transpose(1, 0, 2)
    up_t = up_master.astype(jnp.bfloat16).reshape(rows_w, mp_count, -1).transpose(1, 0, 2)
    qkv_blk, up_blk = exchange([qkv_t, up_t], "mp", True, 0)
    dp_count = lax.axis_size("dp")
    width = qkv_t.shape[-1]
    both = jnp.concatenate(
        [qkv_blk.reshape(mp_count * rows_w, -1), up_blk.reshape(mp_count * rows_w, -1)], axis=1
    )
    gathered = dp_gather(both, dp_count // RING, RING, 1)
    gathered = gathered.reshape(-1, gathered.shape[-1])
    qkv_w = gathered[:, :width]
    up_w = gathered[:, width:]
    rows = hidden_in.shape[0]
    normed_own = layer_norm(hidden_in.astype(jnp.float32)).astype(jnp.bfloat16)
    normed = mp_gather(normed_own, mp_count // 4, 2).reshape(mp_count * rows, -1)
    context, cache = attend(normed, qkv_w, segment_ids[0], page_table[0], mp_index)
    partial = jnp.dot(context, dense_weight, preferred_element_type=jnp.float32).astype(jnp.bfloat16)
    share = mp_sum(partial.reshape(2, mp_count // 4, 2, rows, -1), mp_count // 4, 3)
    stream_own = hidden_in.astype(jnp.float32) + share
    normed_two = mp_gather(layer_norm(stream_own).astype(jnp.bfloat16), mp_count // 4, 4)
    normed_two = normed_two.reshape(mp_count * rows, -1)
    upper = jnp.dot(normed_two, up_w, preferred_element_type=jnp.float32)
    activated = jax.nn.gelu(upper, approximate=True).astype(jnp.bfloat16)
    return (stream_own.astype(jnp.bfloat16), activated, cache)


def solution(mesh):
    placed = (
        P(("dp", "mp"), None),
        P("dp", None),
        P("dp", None),
        P(("dp", "mp"), None),
        P(("dp", "mp"), None),
        P("mp", None),
    )
    return jax.shard_map(
        local,
        mesh=mesh,
        in_specs=placed,
        out_specs=(P(("dp", "mp"), None), P("dp", "mp"), P("dp", None, "mp", None, None)),
        check_vma=False,
    )
```

```python
import functools

import jax
import jax.numpy as jnp
from jax import lax
from jax.experimental import pallas as pl
from jax.experimental.pallas import tpu as pltpu
from jax.sharding import PartitionSpec as P

H = 16
HD = 128
PAGE = 128
RING = 4
MESH = pl.DeviceIdType.MESH


def layer_norm(values):
    mean_val = jnp.mean(values, -1, keepdims=True)
    centered = values - mean_val
    variance = jnp.mean(centered * centered, -1, keepdims=True)
    return centered * lax.rsqrt(variance + 1e-05)


def _remote(src, dst, send_sem, recv_sem, axis, peer):
    return pltpu.make_async_remote_copy(
        src_ref=src,
        dst_ref=dst,
        send_sem=send_sem,
        recv_sem=recv_sem,
        device_id={axis: peer},
        device_id_type=MESH,
    )


def mp_places(chips):
    me = lax.axis_index("mp")
    per_half = chips * 2
    h, c, k = me // per_half, (me // 2) % chips, me % 2
    far = (1 - h) * per_half + c * 2 + k
    twin = h * per_half + c * 2 + (1 - k)
    mates = [h * per_half + ((c + j) % chips) * 2 + k for j in range(1, chips)]
    return h, c, k, far, twin, mates


def exchange_peers(n, axis):
    me = lax.axis_index(axis)
    return [(None, axis, lax.rem(me + step, n)) for step in range(1, n)]


def exchange_body(n, axis, ins, outs, scratch):
    send_sem, recv_sem, local_sem = scratch
    me = lax.axis_index(axis)
    copies, locals_ = [], []
    for a in range(len(ins)):
        for step in range(1, n):
            peer = lax.rem(me + step, n)
            slot = a * (n - 1) + step - 1
            copy = _remote(ins[a].at[peer], outs[a].at[me], send_sem.at[slot], recv_sem.at[slot], axis, peer)
            copy.start()
            copies.append(copy)
        own = pltpu.make_async_copy(ins[a].at[me], outs[a].at[me], local_sem.at[a])
        own.start()
        locals_.append(own)
    yield
    for own in locals_:
        own.wait()
    for copy in copies:
        copy.wait()


def exchange_scratch(n, count):
    return [
        pltpu.SemaphoreType.DMA((count * (n - 1),)),
        pltpu.SemaphoreType.DMA((count * (n - 1),)),
        pltpu.SemaphoreType.DMA((count,)),
    ]


def dp_peers(lines, ring):
    me = lax.axis_index("dp")
    z, y = me // ring, me % ring
    out = [(z > 0, "dp", me - ring), (z < lines - 1, "dp", me + ring)]
    return out + [(None, "dp", z * ring + (y + k) % ring) for k in range(1, ring)]


def dp_gather_body(lines, ring, ins, outs, scratch):
    (x_ref,), (o_ref,), (send_sem, recv_sem) = ins, outs, scratch
    me = lax.axis_index("dp")
    z, y = me // ring, me % ring
    has_left, has_right = z > 0, z < lines - 1
    sends = []

    def send(cond, src, src_z, peer):
        slot = src_z * ring + y
        copy = _remote(src, o_ref.at[src_z, y], send_sem.at[len(sends)], recv_sem.at[slot], "dp", peer)
        pl.when(cond)(copy.start)
        sends.append((cond, copy))

    def spread(cond, src, src_z):
        for k in range(1, ring):
            send(cond, src, src_z, z * ring + (y + k) % ring)

    def arrive(cond, src_z, peer):
        slot = src_z * ring + y
        copy = _remote(o_ref.at[src_z, y], o_ref.at[src_z, y], send_sem.at[0], recv_sem.at[slot], "dp", peer)
        pl.when(cond)(copy.wait_recv)

    send(has_right, x_ref, z, me + ring)
    send(has_left, x_ref, z, me - ring)
    spread(z >= 0, x_ref, z)
    o_ref[z, y] = x_ref[...]
    yield
    for s in range(1, lines):
        from_left = z - s >= 0
        src_l = jnp.maximum(z - s, 0)
        arrive(from_left, src_l, me - ring)
        send(from_left & has_right, o_ref.at[src_l, y], src_l, me + ring)
        spread(from_left, o_ref.at[src_l, y], src_l)
        from_right = z + s <= lines - 1
        src_r = jnp.minimum(z + s, lines - 1)
        arrive(from_right, src_r, me + ring)
        send(from_right & has_left, o_ref.at[src_r, y], src_r, me - ring)
        spread(from_right, o_ref.at[src_r, y], src_r)
        yield
    for k in range(1, ring):
        yy = (y + k) % ring
        for zz in range(lines):
            slot = zz * ring + yy
            copy = _remote(o_ref.at[zz, yy], o_ref.at[zz, yy], send_sem.at[0], recv_sem.at[slot], "dp", z * ring + yy)
            copy.wait_recv()
    for cond, copy in sends:
        pl.when(cond)(copy.wait_send)


def dp_scratch(lines, ring):
    return [
        pltpu.SemaphoreType.DMA((1 + ring + (lines - 1) * 2 * ring,)),
        pltpu.SemaphoreType.DMA((lines * ring,)),
    ]


def mp_peers(chips):
    _, _, _, far, twin, mates = mp_places(chips)
    return [(None, "mp", peer) for peer in [far, twin] + mates]


def mp_gather_body(chips, ins, outs, scratch):
    (x_ref,), (o_ref,), (send_sem, recv_sem) = ins, outs, scratch
    h, c, k, far, twin, mates = mp_places(chips)
    sends = []

    def send(src, hh, cc, kk, peer):
        slot = (hh * chips + cc) * 2 + kk
        copy = _remote(src, o_ref.at[hh, cc, kk], send_sem.at[len(sends)], recv_sem.at[slot], "mp", peer)
        copy.start()
        sends.append(copy)

    def arrive(hh, cc, kk, peer):
        slot = (hh * chips + cc) * 2 + kk
        copy = _remote(o_ref.at[hh, cc, kk], o_ref.at[hh, cc, kk], send_sem.at[0], recv_sem.at[slot], "mp", peer)
        copy.wait_recv()

    send(x_ref, h, c, k, far)
    for peer in mates:
        send(x_ref, h, c, k, peer)
    send(x_ref, h, c, k, twin)
    o_ref[h, c, k] = x_ref[...]
    yield
    arrive(1 - h, c, k, far)
    for peer in mates:
        send(o_ref.at[1 - h, c, k], 1 - h, c, k, peer)
    send(o_ref.at[1 - h, c, k], 1 - h, c, k, twin)
    yield
    for j in range(1, chips):
        cc = (c + j) % chips
        for hh in (h, 1 - h):
            arrive(hh, cc, k, mates[j - 1])
            send(o_ref.at[hh, cc, k], hh, cc, k, twin)
    yield
    for hh in range(2):
        for cc in range(chips):
            arrive(hh, cc, 1 - k, twin)
    for copy in sends:
        copy.wait_send()


def mp_gather_scratch(chips):
    return [pltpu.SemaphoreType.DMA((4 * chips,)), pltpu.SemaphoreType.DMA((4 * chips,))]


def mp_sum_body(chips, ins, outs, scratch):
    (p_ref,), (o_ref,) = ins, outs
    twin_in, pair, mate_in, far_out, far_in, acc, send_sem, recv_sem = scratch
    h, c, k, far, twin, mates = mp_places(chips)
    sends = []

    def send(src, dst, slot, peer):
        copy = _remote(src, dst, send_sem.at[len(sends)], recv_sem.at[slot], "mp", peer)
        copy.start()
        sends.append(copy)

    def arrive(dst, slot, peer):
        _remote(dst, dst, send_sem.at[0], recv_sem.at[slot], "mp", peer).wait_recv()

    for hh in range(2):
        for cc in range(chips):
            send(p_ref.at[hh, cc, 1 - k], twin_in.at[hh, cc], hh * chips + cc, twin)
    yield
    for j in range(1, chips):
        cc = (c + j) % chips
        for hh in range(2):
            arrive(twin_in.at[hh, cc], hh * chips + cc, twin)
            pair[hh, cc] = (
                p_ref[hh, cc, k].astype(jnp.float32) + twin_in[hh, cc].astype(jnp.float32)
            ).astype(pair.dtype)
            send(pair.at[hh, cc], mate_in.at[c, hh], 2 * chips + c * 2 + hh, mates[j - 1])
    for hh in range(2):
        arrive(twin_in.at[hh, c], hh * chips + c, twin)
        acc[hh] = p_ref[hh, c, k].astype(jnp.float32) + twin_in[hh, c].astype(jnp.float32)
    yield
    for j in range(1, chips):
        cc = (c + j) % chips
        for hh in range(2):
            arrive(mate_in.at[cc, hh], 2 * chips + cc * 2 + hh, mates[j - 1])
            acc[hh] = acc[hh] + mate_in[cc, hh].astype(jnp.float32)
    far_out[...] = acc[1 - h].astype(far_out.dtype)
    send(far_out, far_in, 4 * chips, far)
    yield
    arrive(far_in, 4 * chips, far)
    o_ref[...] = acc[h] + far_in[...].astype(jnp.float32)
    for copy in sends:
        copy.wait_send()


def mp_sum_scratch(chips, rows, cols, dt):
    return [
        pltpu.VMEM((2, chips, rows, cols), dt),
        pltpu.VMEM((2, chips, rows, cols), dt),
        pltpu.VMEM((chips, 2, rows, cols), dt),
        pltpu.VMEM((rows, cols), dt),
        pltpu.VMEM((rows, cols), dt),
        pltpu.VMEM((2, rows, cols), jnp.float32),
        pltpu.SemaphoreType.DMA((4 * chips + 1,)),
        pltpu.SemaphoreType.DMA((4 * chips + 1,)),
    ]


def combined_kernel(parts, *refs):
    n_in = sum(p[2] for p in parts)
    n_out = sum(p[3] for p in parts)
    ins, outs, scratch = refs[:n_in], refs[n_in:n_in + n_out], refs[n_in + n_out:]
    barrier = pltpu.get_barrier_semaphore()
    total = 0
    for peers, _, _, _, _ in parts:
        for cond, axis, peer in peers():
            def signal(axis=axis, peer=peer):
                pl.semaphore_signal(barrier, inc=1, device_id={axis: peer}, device_id_type=MESH)
            if cond is None:
                signal()
                total = total + 1
            else:
                pl.when(cond)(signal)
                total = total + cond.astype(jnp.int32)
    pl.semaphore_wait(barrier, total)
    gens = []
    for _, body, pi, po, ps in parts:
        gens.append(body(ins[:pi], outs[:po], scratch[:ps]))
        ins, outs, scratch = ins[pi:], outs[po:], scratch[ps:]
    while gens:
        for gen in list(gens):
            try:
                next(gen)
            except StopIteration:
                gens.remove(gen)


def combined(parts, inputs, out_shapes, scratch_shapes, cid):
    return pl.pallas_call(
        functools.partial(combined_kernel, parts),
        out_shape=out_shapes,
        in_specs=[pl.BlockSpec(memory_space=pltpu.VMEM)] * len(inputs),
        out_specs=[pl.BlockSpec(memory_space=pltpu.VMEM)] * len(out_shapes),
        scratch_shapes=scratch_shapes,
        compiler_params=pltpu.CompilerParams(collective_id=cid, has_side_effects=True),
    )(*inputs)


def attend(normed, qkv_w, segment, table, mp_index):
    group_rows = normed.shape[0]
    heads_dev = qkv_w.shape[1] // (3 * HD)
    joined = jnp.dot(normed, qkv_w, preferred_element_type=jnp.float32).astype(jnp.bfloat16)
    joined = joined.reshape(group_rows, heads_dev, 3, HD)
    query = joined[:, :, 0]
    keys = joined[:, :, 1]
    vals = joined[:, :, 2]
    head_ids = mp_index * heads_dev + jnp.arange(heads_dev)
    slopes = jnp.exp2(-8.0 * (head_ids + 1).astype(jnp.float32) / H)
    positions = jnp.arange(group_rows)
    distance = (positions[:, None] - positions[None, :]).astype(jnp.float32)
    allowed = (segment[:, None] == segment[None, :]) & (distance >= 0)
    scores = jnp.einsum("thd,shd->hts", query, keys, preferred_element_type=jnp.float32) / jnp.sqrt(
        jnp.float32(HD)
    )
    scores = scores - slopes[:, None, None] * distance[None]
    scores = jnp.where(allowed[None], scores, -jnp.inf)
    probs = jax.nn.softmax(scores, axis=-1).astype(jnp.bfloat16)
    context = jnp.einsum("hts,shd->thd", probs, vals, preferred_element_type=jnp.float32).astype(
        jnp.bfloat16
    )
    context = context.reshape(group_rows, heads_dev * HD)
    key_vals = jnp.stack([keys, vals], 1)
    pages_here = group_rows // PAGE
    key_vals = key_vals.reshape(pages_here, PAGE, 2, heads_dev, HD).transpose(0, 2, 3, 1, 4)
    cache = jnp.zeros((pages_here, 2, heads_dev, PAGE, HD), jnp.bfloat16).at[table].set(key_vals)
    return (context, cache)


def local(hidden_in, segment_ids, page_table, qkv_master, up_master, dense_weight):
    mp_count = lax.axis_size("mp")
    dp_count = lax.axis_size("dp")
    mp_index = lax.axis_index("mp")
    chips = mp_count // 4
    lines = dp_count // RING
    rows = hidden_in.shape[0]
    rows_w = qkv_master.shape[0]
    bf = jnp.bfloat16
    qkv_t = qkv_master.astype(bf).reshape(rows_w, mp_count, -1).transpose(1, 0, 2)
    up_t = up_master.astype(bf).reshape(rows_w, mp_count, -1).transpose(1, 0, 2)
    normed_own = layer_norm(hidden_in.astype(jnp.float32)).astype(bf)
    sd = jax.ShapeDtypeStruct
    qkv_blk, up_blk, normed = combined(
        [
            (
                functools.partial(exchange_peers, mp_count, "mp"),
                functools.partial(exchange_body, mp_count, "mp"),
                2, 2, 3,
            ),
            (functools.partial(mp_peers, chips), functools.partial(mp_gather_body, chips), 1, 1, 2),
        ],
        [qkv_t, up_t, normed_own],
        [sd(qkv_t.shape, bf), sd(up_t.shape, bf), sd((2, chips, 2) + normed_own.shape, bf)],
        exchange_scratch(mp_count, 2) + mp_gather_scratch(chips),
        0,
    )
    normed = normed.reshape(mp_count * rows, -1)
    qkv_piece = qkv_blk.reshape(mp_count * rows_w, -1)
    up_piece = up_blk.reshape(mp_count * rows_w, -1)
    (qkv_w,) = combined(
        [(functools.partial(dp_peers, lines, RING), functools.partial(dp_gather_body, lines, RING), 1, 1, 2)],
        [qkv_piece],
        [sd((lines, RING) + qkv_piece.shape, bf)],
        dp_scratch(lines, RING),
        1,
    )
    qkv_w = qkv_w.reshape(-1, qkv_piece.shape[-1])
    context, cache = attend(normed, qkv_w, segment_ids[0], page_table[0], mp_index)
    partial = jnp.dot(context, dense_weight, preferred_element_type=jnp.float32).astype(bf)
    share, up_w = combined(
        [
            (functools.partial(mp_peers, chips), functools.partial(mp_sum_body, chips), 1, 1, 8),
            (functools.partial(dp_peers, lines, RING), functools.partial(dp_gather_body, lines, RING), 1, 1, 2),
        ],
        [partial.reshape(2, chips, 2, rows, -1), up_piece],
        [sd((rows, partial.shape[-1]), jnp.float32), sd((lines, RING) + up_piece.shape, bf)],
        mp_sum_scratch(chips, rows, partial.shape[-1], bf) + dp_scratch(lines, RING),
        2,
    )
    up_w = up_w.reshape(-1, up_piece.shape[-1])
    stream_own = hidden_in.astype(jnp.float32) + share
    normed_two_own = layer_norm(stream_own).astype(bf)
    (normed_two,) = combined(
        [(functools.partial(mp_peers, chips), functools.partial(mp_gather_body, chips), 1, 1, 2)],
        [normed_two_own],
        [sd((2, chips, 2) + normed_two_own.shape, bf)],
        mp_gather_scratch(chips),
        3,
    )
    normed_two = normed_two.reshape(mp_count * rows, -1)
    upper = jnp.dot(normed_two, up_w, preferred_element_type=jnp.float32)
    activated = jax.nn.gelu(upper, approximate=True).astype(bf)
    return (stream_own.astype(bf), activated, cache)


def solution(mesh):
    placed = (
        P(("dp", "mp"), None),
        P("dp", None),
        P("dp", None),
        P(("dp", "mp"), None),
        P(("dp", "mp"), None),
        P("mp", None),
    )
    return jax.shard_map(
        local,
        mesh=mesh,
        in_specs=placed,
        out_specs=(P(("dp", "mp"), None), P("dp", "mp"), P("dp", None, "mp", None, None)),
        check_vma=False,
    )
```

```python
import functools

import jax
import jax.numpy as jnp
from jax import lax
from jax.experimental import pallas as pl
from jax.experimental.pallas import tpu as pltpu
from jax.sharding import PartitionSpec as P

H = 16
HD = 128
PAGE = 128
RING = 4
MESH = pl.DeviceIdType.MESH


def layer_norm(values):
    mean_val = jnp.mean(values, -1, keepdims=True)
    centered = values - mean_val
    variance = jnp.mean(centered * centered, -1, keepdims=True)
    return centered * lax.rsqrt(variance + 1e-05)


def _remote(src, dst, send_sem, recv_sem, axis, peer):
    return pltpu.make_async_remote_copy(
        src_ref=src,
        dst_ref=dst,
        send_sem=send_sem,
        recv_sem=recv_sem,
        device_id={axis: peer},
        device_id_type=MESH,
    )


def mp_places(chips):
    me = lax.axis_index("mp")
    per_half = chips * 2
    h, c, k = me // per_half, (me // 2) % chips, me % 2
    far = (1 - h) * per_half + c * 2 + k
    twin = h * per_half + c * 2 + (1 - k)
    mates = [h * per_half + ((c + j) % chips) * 2 + k for j in range(1, chips)]
    return h, c, k, far, twin, mates


def exchange_peers(n, axis):
    me = lax.axis_index(axis)
    return [(None, axis, lax.rem(me + step, n)) for step in range(1, n)]


def exchange_body(n, axis, ins, outs, scratch):
    send_sem, recv_sem, local_sem = scratch
    me = lax.axis_index(axis)
    copies, locals_ = [], []
    for a in range(len(ins)):
        for step in range(1, n):
            peer = lax.rem(me + step, n)
            slot = a * (n - 1) + step - 1
            copy = _remote(ins[a].at[peer], outs[a].at[me], send_sem.at[slot], recv_sem.at[slot], axis, peer)
            copy.start()
            copies.append(copy)
        own = pltpu.make_async_copy(ins[a].at[me], outs[a].at[me], local_sem.at[a])
        own.start()
        locals_.append(own)
    yield
    for own in locals_:
        own.wait()
    for copy in copies:
        copy.wait()


def exchange_scratch(n, count):
    return [
        pltpu.SemaphoreType.DMA((count * (n - 1),)),
        pltpu.SemaphoreType.DMA((count * (n - 1),)),
        pltpu.SemaphoreType.DMA((count,)),
    ]


def dp_peers(lines, ring):
    me = lax.axis_index("dp")
    z, y = me // ring, me % ring
    out = [(z > 0, "dp", me - ring), (z < lines - 1, "dp", me + ring)]
    return out + [(None, "dp", z * ring + (y + k) % ring) for k in range(1, ring)]


def dp_gather_body(lines, ring, ins, outs, scratch):
    (x_ref,), (o_ref,), (send_sem, recv_sem) = ins, outs, scratch
    me = lax.axis_index("dp")
    z, y = me // ring, me % ring
    has_left, has_right = z > 0, z < lines - 1
    sends = []

    def send(cond, src, src_z, peer):
        slot = src_z * ring + y
        copy = _remote(src, o_ref.at[src_z, y], send_sem.at[len(sends)], recv_sem.at[slot], "dp", peer)
        pl.when(cond)(copy.start)
        sends.append((cond, copy))

    def spread(cond, src, src_z):
        for k in range(1, ring):
            send(cond, src, src_z, z * ring + (y + k) % ring)

    def arrive(cond, src_z, peer):
        slot = src_z * ring + y
        copy = _remote(o_ref.at[src_z, y], o_ref.at[src_z, y], send_sem.at[0], recv_sem.at[slot], "dp", peer)
        pl.when(cond)(copy.wait_recv)

    send(has_right, x_ref, z, me + ring)
    send(has_left, x_ref, z, me - ring)
    spread(z >= 0, x_ref, z)
    o_ref[z, y] = x_ref[...]
    yield
    for s in range(1, lines):
        from_left = z - s >= 0
        src_l = jnp.maximum(z - s, 0)
        arrive(from_left, src_l, me - ring)
        send(from_left & has_right, o_ref.at[src_l, y], src_l, me + ring)
        spread(from_left, o_ref.at[src_l, y], src_l)
        from_right = z + s <= lines - 1
        src_r = jnp.minimum(z + s, lines - 1)
        arrive(from_right, src_r, me + ring)
        send(from_right & has_left, o_ref.at[src_r, y], src_r, me - ring)
        spread(from_right, o_ref.at[src_r, y], src_r)
        yield
    for k in range(1, ring):
        yy = (y + k) % ring
        for zz in range(lines):
            slot = zz * ring + yy
            copy = _remote(o_ref.at[zz, yy], o_ref.at[zz, yy], send_sem.at[0], recv_sem.at[slot], "dp", z * ring + yy)
            copy.wait_recv()
    for cond, copy in sends:
        pl.when(cond)(copy.wait_send)


def dp_scratch(lines, ring):
    return [
        pltpu.SemaphoreType.DMA((1 + ring + (lines - 1) * 2 * ring,)),
        pltpu.SemaphoreType.DMA((lines * ring,)),
    ]


def dp_direct_peers(lines, ring):
    me = lax.axis_index("dp")
    z, y = me // ring, me % ring
    out = []
    for d in range(1, lines):
        out += [(z + d < lines, "dp", me + d * ring), (z - d >= 0, "dp", me - d * ring)]
    return out + [(None, "dp", z * ring + (y + k) % ring) for k in range(1, ring)]


def dp_direct_body(lines, ring, ins, outs, scratch):
    (x_ref,), (o_ref,), (send_sem, recv_sem) = ins, outs, scratch
    me = lax.axis_index("dp")
    z, y = me // ring, me % ring
    sends = []

    def send(cond, src, src_z, peer):
        slot = src_z * ring + y
        copy = _remote(src, o_ref.at[src_z, y], send_sem.at[len(sends)], recv_sem.at[slot], "dp", peer)
        pl.when(cond)(copy.start)
        sends.append((cond, copy))

    def spread(cond, src, src_z):
        for k in range(1, ring):
            send(cond, src, src_z, z * ring + (y + k) % ring)

    def arrive(cond, src_z, peer):
        slot = src_z * ring + y
        copy = _remote(o_ref.at[src_z, y], o_ref.at[src_z, y], send_sem.at[0], recv_sem.at[slot], "dp", peer)
        pl.when(cond)(copy.wait_recv)

    always = z >= 0
    spread(always, x_ref, z)
    for d in range(1, lines):
        send(z + d < lines, x_ref, z, me + d * ring)
        send(z - d >= 0, x_ref, z, me - d * ring)
    o_ref[z, y] = x_ref[...]
    yield
    for d in range(1, lines):
        for sign in (1, -1):
            cond = (z + sign * d < lines) & (z + sign * d >= 0)
            src_z = jnp.clip(z + sign * d, 0, lines - 1)
            arrive(cond, src_z, src_z * ring + y)
            spread(cond, o_ref.at[src_z, y], src_z)
        yield
    for k in range(1, ring):
        yy = (y + k) % ring
        for zz in range(lines):
            slot = zz * ring + yy
            copy = _remote(o_ref.at[zz, yy], o_ref.at[zz, yy], send_sem.at[0], recv_sem.at[slot], "dp", z * ring + yy)
            copy.wait_recv()
    for cond, copy in sends:
        pl.when(cond)(copy.wait_send)


def dp_direct_scratch(lines, ring):
    return [
        pltpu.SemaphoreType.DMA((ring - 1 + 2 * (lines - 1) * ring,)),
        pltpu.SemaphoreType.DMA((lines * ring,)),
    ]


def mp_peers(chips):
    _, _, _, far, twin, mates = mp_places(chips)
    return [(None, "mp", peer) for peer in [far, twin] + mates]


def mp_gather_body(chips, ins, outs, scratch):
    (x_ref,), (o_ref,), (send_sem, recv_sem) = ins, outs, scratch
    h, c, k, far, twin, mates = mp_places(chips)
    sends = []

    def send(src, hh, cc, kk, peer):
        slot = (hh * chips + cc) * 2 + kk
        copy = _remote(src, o_ref.at[hh, cc, kk], send_sem.at[len(sends)], recv_sem.at[slot], "mp", peer)
        copy.start()
        sends.append(copy)

    def arrive(hh, cc, kk, peer):
        slot = (hh * chips + cc) * 2 + kk
        copy = _remote(o_ref.at[hh, cc, kk], o_ref.at[hh, cc, kk], send_sem.at[0], recv_sem.at[slot], "mp", peer)
        copy.wait_recv()

    send(x_ref, h, c, k, far)
    for peer in mates:
        send(x_ref, h, c, k, peer)
    send(x_ref, h, c, k, twin)
    o_ref[h, c, k] = x_ref[...]
    yield
    arrive(1 - h, c, k, far)
    for peer in mates:
        send(o_ref.at[1 - h, c, k], 1 - h, c, k, peer)
    send(o_ref.at[1 - h, c, k], 1 - h, c, k, twin)
    yield
    for j in range(1, chips):
        cc = (c + j) % chips
        for hh in (h, 1 - h):
            arrive(hh, cc, k, mates[j - 1])
            send(o_ref.at[hh, cc, k], hh, cc, k, twin)
    yield
    for hh in range(2):
        for cc in range(chips):
            arrive(hh, cc, 1 - k, twin)
    for copy in sends:
        copy.wait_send()


def mp_gather_scratch(chips):
    return [pltpu.SemaphoreType.DMA((4 * chips,)), pltpu.SemaphoreType.DMA((4 * chips,))]


def mp_sum_body(chips, ins, outs, scratch):
    (p_ref,), (o_ref,) = ins, outs
    twin_in, pair, mate_in, far_out, far_in, acc, send_sem, recv_sem = scratch
    h, c, k, far, twin, mates = mp_places(chips)
    sends = []

    def send(src, dst, slot, peer):
        copy = _remote(src, dst, send_sem.at[len(sends)], recv_sem.at[slot], "mp", peer)
        copy.start()
        sends.append(copy)

    def arrive(dst, slot, peer):
        _remote(dst, dst, send_sem.at[0], recv_sem.at[slot], "mp", peer).wait_recv()

    for hh in range(2):
        for cc in range(chips):
            send(p_ref.at[hh, cc, 1 - k], twin_in.at[hh, cc], hh * chips + cc, twin)
    yield
    for j in range(1, chips):
        cc = (c + j) % chips
        for hh in range(2):
            arrive(twin_in.at[hh, cc], hh * chips + cc, twin)
            pair[hh, cc] = (
                p_ref[hh, cc, k].astype(jnp.float32) + twin_in[hh, cc].astype(jnp.float32)
            ).astype(pair.dtype)
            send(pair.at[hh, cc], mate_in.at[c, hh], 2 * chips + c * 2 + hh, mates[j - 1])
    for hh in range(2):
        arrive(twin_in.at[hh, c], hh * chips + c, twin)
        acc[hh] = p_ref[hh, c, k].astype(jnp.float32) + twin_in[hh, c].astype(jnp.float32)
    yield
    for j in range(1, chips):
        cc = (c + j) % chips
        for hh in range(2):
            arrive(mate_in.at[cc, hh], 2 * chips + cc * 2 + hh, mates[j - 1])
            acc[hh] = acc[hh] + mate_in[cc, hh].astype(jnp.float32)
    far_out[...] = acc[1 - h].astype(far_out.dtype)
    send(far_out, far_in, 4 * chips, far)
    yield
    arrive(far_in, 4 * chips, far)
    o_ref[...] = acc[h] + far_in[...].astype(jnp.float32)
    for copy in sends:
        copy.wait_send()


def mp_sum_scratch(chips, rows, cols, dt):
    return [
        pltpu.VMEM((2, chips, rows, cols), dt),
        pltpu.VMEM((2, chips, rows, cols), dt),
        pltpu.VMEM((chips, 2, rows, cols), dt),
        pltpu.VMEM((rows, cols), dt),
        pltpu.VMEM((rows, cols), dt),
        pltpu.VMEM((2, rows, cols), jnp.float32),
        pltpu.SemaphoreType.DMA((4 * chips + 1,)),
        pltpu.SemaphoreType.DMA((4 * chips + 1,)),
    ]


def combined_kernel(parts, *refs):
    n_in = sum(p[2] for p in parts)
    n_out = sum(p[3] for p in parts)
    ins, outs, scratch = refs[:n_in], refs[n_in:n_in + n_out], refs[n_in + n_out:]
    barrier = pltpu.get_barrier_semaphore()
    total = 0
    for peers, _, _, _, _ in parts:
        for cond, axis, peer in peers():
            def signal(axis=axis, peer=peer):
                pl.semaphore_signal(barrier, inc=1, device_id={axis: peer}, device_id_type=MESH)
            if cond is None:
                signal()
                total = total + 1
            else:
                pl.when(cond)(signal)
                total = total + cond.astype(jnp.int32)
    pl.semaphore_wait(barrier, total)
    gens = []
    for _, body, pi, po, ps in parts:
        gens.append(body(ins[:pi], outs[:po], scratch[:ps]))
        ins, outs, scratch = ins[pi:], outs[po:], scratch[ps:]
    while gens:
        for gen in list(gens):
            try:
                next(gen)
            except StopIteration:
                gens.remove(gen)


def combined(parts, inputs, out_shapes, scratch_shapes, cid):
    return pl.pallas_call(
        functools.partial(combined_kernel, parts),
        out_shape=out_shapes,
        in_specs=[pl.BlockSpec(memory_space=pltpu.VMEM)] * len(inputs),
        out_specs=[pl.BlockSpec(memory_space=pltpu.VMEM)] * len(out_shapes),
        scratch_shapes=scratch_shapes,
        compiler_params=pltpu.CompilerParams(collective_id=cid, has_side_effects=True),
    )(*inputs)


def attend(normed, qkv_w, segment, table, mp_index):
    group_rows = normed.shape[0]
    heads_dev = qkv_w.shape[1] // (3 * HD)
    joined = jnp.dot(normed, qkv_w, preferred_element_type=jnp.float32).astype(jnp.bfloat16)
    joined = joined.reshape(group_rows, heads_dev, 3, HD)
    query = joined[:, :, 0]
    keys = joined[:, :, 1]
    vals = joined[:, :, 2]
    head_ids = mp_index * heads_dev + jnp.arange(heads_dev)
    slopes = jnp.exp2(-8.0 * (head_ids + 1).astype(jnp.float32) / H)
    positions = jnp.arange(group_rows)
    distance = (positions[:, None] - positions[None, :]).astype(jnp.float32)
    allowed = (segment[:, None] == segment[None, :]) & (distance >= 0)
    scores = jnp.einsum("thd,shd->hts", query, keys, preferred_element_type=jnp.float32) / jnp.sqrt(
        jnp.float32(HD)
    )
    scores = scores - slopes[:, None, None] * distance[None]
    scores = jnp.where(allowed[None], scores, -jnp.inf)
    probs = jax.nn.softmax(scores, axis=-1).astype(jnp.bfloat16)
    context = jnp.einsum("hts,shd->thd", probs, vals, preferred_element_type=jnp.float32).astype(
        jnp.bfloat16
    )
    context = context.reshape(group_rows, heads_dev * HD)
    key_vals = jnp.stack([keys, vals], 1)
    pages_here = group_rows // PAGE
    key_vals = key_vals.reshape(pages_here, PAGE, 2, heads_dev, HD).transpose(0, 2, 3, 1, 4)
    cache = jnp.zeros((pages_here, 2, heads_dev, PAGE, HD), jnp.bfloat16).at[table].set(key_vals)
    return (context, cache)


def local(hidden_in, segment_ids, page_table, qkv_master, up_master, dense_weight):
    mp_count = lax.axis_size("mp")
    dp_count = lax.axis_size("dp")
    mp_index = lax.axis_index("mp")
    chips = mp_count // 4
    lines = dp_count // RING
    rows = hidden_in.shape[0]
    rows_w = qkv_master.shape[0]
    bf = jnp.bfloat16
    qkv_t = qkv_master.astype(bf).reshape(rows_w, mp_count, -1).transpose(1, 0, 2)
    up_t = up_master.astype(bf).reshape(rows_w, mp_count, -1).transpose(1, 0, 2)
    normed_own = layer_norm(hidden_in.astype(jnp.float32)).astype(bf)
    sd = jax.ShapeDtypeStruct
    qkv_blk, up_blk, normed = combined(
        [
            (
                functools.partial(exchange_peers, mp_count, "mp"),
                functools.partial(exchange_body, mp_count, "mp"),
                2, 2, 3,
            ),
            (functools.partial(mp_peers, chips), functools.partial(mp_gather_body, chips), 1, 1, 2),
        ],
        [qkv_t, up_t, normed_own],
        [sd(qkv_t.shape, bf), sd(up_t.shape, bf), sd((2, chips, 2) + normed_own.shape, bf)],
        exchange_scratch(mp_count, 2) + mp_gather_scratch(chips),
        0,
    )
    normed = normed.reshape(mp_count * rows, -1)
    qkv_piece = qkv_blk.reshape(mp_count * rows_w, -1)
    up_piece = up_blk.reshape(mp_count * rows_w, -1)
    (qkv_w,) = combined(
        [(functools.partial(dp_direct_peers, lines, RING), functools.partial(dp_direct_body, lines, RING), 1, 1, 2)],
        [qkv_piece],
        [sd((lines, RING) + qkv_piece.shape, bf)],
        dp_direct_scratch(lines, RING),
        1,
    )
    qkv_w = qkv_w.reshape(-1, qkv_piece.shape[-1])
    context, cache = attend(normed, qkv_w, segment_ids[0], page_table[0], mp_index)
    partial = jnp.dot(context, dense_weight, preferred_element_type=jnp.float32).astype(bf)
    share, up_w = combined(
        [
            (functools.partial(mp_peers, chips), functools.partial(mp_sum_body, chips), 1, 1, 8),
            (functools.partial(dp_direct_peers, lines, RING), functools.partial(dp_direct_body, lines, RING), 1, 1, 2),
        ],
        [partial.reshape(2, chips, 2, rows, -1), up_piece],
        [sd((rows, partial.shape[-1]), jnp.float32), sd((lines, RING) + up_piece.shape, bf)],
        mp_sum_scratch(chips, rows, partial.shape[-1], bf) + dp_direct_scratch(lines, RING),
        2,
    )
    up_w = up_w.reshape(-1, up_piece.shape[-1])
    stream_own = hidden_in.astype(jnp.float32) + share
    normed_two_own = layer_norm(stream_own).astype(bf)
    (normed_two,) = combined(
        [(functools.partial(mp_peers, chips), functools.partial(mp_gather_body, chips), 1, 1, 2)],
        [normed_two_own],
        [sd((2, chips, 2) + normed_two_own.shape, bf)],
        mp_gather_scratch(chips),
        3,
    )
    normed_two = normed_two.reshape(mp_count * rows, -1)
    upper = jnp.dot(normed_two, up_w, preferred_element_type=jnp.float32)
    activated = jax.nn.gelu(upper, approximate=True).astype(bf)
    return (stream_own.astype(bf), activated, cache)


def solution(mesh):
    placed = (
        P(("dp", "mp"), None),
        P("dp", None),
        P("dp", None),
        P(("dp", "mp"), None),
        P(("dp", "mp"), None),
        P("mp", None),
    )
    return jax.shard_map(
        local,
        mesh=mesh,
        in_specs=placed,
        out_specs=(P(("dp", "mp"), None), P("dp", "mp"), P("dp", None, "mp", None, None)),
        check_vma=False,
    )
```

```python
import functools

import jax
import jax.numpy as jnp
from jax import lax
from jax.experimental import pallas as pl
from jax.experimental.pallas import tpu as pltpu
from jax.sharding import PartitionSpec as P

H = 16
HD = 128
PAGE = 128
RING = 4
MESH = pl.DeviceIdType.MESH


def layer_norm(values):
    mean_val = jnp.mean(values, -1, keepdims=True)
    centered = values - mean_val
    variance = jnp.mean(centered * centered, -1, keepdims=True)
    return centered * lax.rsqrt(variance + 1e-05)


def _remote(src, dst, send_sem, recv_sem, axis, peer):
    return pltpu.make_async_remote_copy(
        src_ref=src,
        dst_ref=dst,
        send_sem=send_sem,
        recv_sem=recv_sem,
        device_id={axis: peer},
        device_id_type=MESH,
    )


def mp_places(chips):
    me = lax.axis_index("mp")
    per_half = chips * 2
    h, c, k = me // per_half, (me // 2) % chips, me % 2
    far = (1 - h) * per_half + c * 2 + k
    twin = h * per_half + c * 2 + (1 - k)
    mates = [h * per_half + ((c + j) % chips) * 2 + k for j in range(1, chips)]
    return h, c, k, far, twin, mates


def exchange_peers(n, axis):
    me = lax.axis_index(axis)
    return [(None, axis, lax.rem(me + step, n)) for step in range(1, n)]


def exchange_body(n, axis, ins, outs, scratch):
    send_sem, recv_sem, local_sem = scratch
    me = lax.axis_index(axis)
    copies, locals_ = [], []
    for a in range(len(ins)):
        for step in range(1, n):
            peer = lax.rem(me + step, n)
            slot = a * (n - 1) + step - 1
            copy = _remote(ins[a].at[peer], outs[a].at[me], send_sem.at[slot], recv_sem.at[slot], axis, peer)
            copy.start()
            copies.append(copy)
        own = pltpu.make_async_copy(ins[a].at[me], outs[a].at[me], local_sem.at[a])
        own.start()
        locals_.append(own)
    yield
    for own in locals_:
        own.wait()
    for copy in copies:
        copy.wait()


def exchange_scratch(n, count):
    return [
        pltpu.SemaphoreType.DMA((count * (n - 1),)),
        pltpu.SemaphoreType.DMA((count * (n - 1),)),
        pltpu.SemaphoreType.DMA((count,)),
    ]


def dp_peers(lines, ring):
    me = lax.axis_index("dp")
    z, y = me // ring, me % ring
    out = [(z > 0, "dp", me - ring), (z < lines - 1, "dp", me + ring)]
    return out + [(None, "dp", z * ring + (y + k) % ring) for k in range(1, ring)]


def dp_gather_body(lines, ring, ins, outs, scratch):
    (x_ref,), (o_ref,), (send_sem, recv_sem) = ins, outs, scratch
    me = lax.axis_index("dp")
    z, y = me // ring, me % ring
    has_left, has_right = z > 0, z < lines - 1
    sends = []

    def send(cond, src, src_z, peer):
        slot = src_z * ring + y
        copy = _remote(src, o_ref.at[src_z, y], send_sem.at[len(sends)], recv_sem.at[slot], "dp", peer)
        pl.when(cond)(copy.start)
        sends.append((cond, copy))

    def spread(cond, src, src_z):
        for k in range(1, ring):
            send(cond, src, src_z, z * ring + (y + k) % ring)

    def arrive(cond, src_z, peer):
        slot = src_z * ring + y
        copy = _remote(o_ref.at[src_z, y], o_ref.at[src_z, y], send_sem.at[0], recv_sem.at[slot], "dp", peer)
        pl.when(cond)(copy.wait_recv)

    send(has_right, x_ref, z, me + ring)
    send(has_left, x_ref, z, me - ring)
    spread(z >= 0, x_ref, z)
    o_ref[z, y] = x_ref[...]
    yield
    for s in range(1, lines):
        from_left = z - s >= 0
        src_l = jnp.maximum(z - s, 0)
        arrive(from_left, src_l, me - ring)
        send(from_left & has_right, o_ref.at[src_l, y], src_l, me + ring)
        spread(from_left, o_ref.at[src_l, y], src_l)
        from_right = z + s <= lines - 1
        src_r = jnp.minimum(z + s, lines - 1)
        arrive(from_right, src_r, me + ring)
        send(from_right & has_left, o_ref.at[src_r, y], src_r, me - ring)
        spread(from_right, o_ref.at[src_r, y], src_r)
        yield
    for k in range(1, ring):
        yy = (y + k) % ring
        for zz in range(lines):
            slot = zz * ring + yy
            copy = _remote(o_ref.at[zz, yy], o_ref.at[zz, yy], send_sem.at[0], recv_sem.at[slot], "dp", z * ring + yy)
            copy.wait_recv()
    for cond, copy in sends:
        pl.when(cond)(copy.wait_send)


def dp_scratch(lines, ring):
    return [
        pltpu.SemaphoreType.DMA((1 + ring + (lines - 1) * 2 * ring,)),
        pltpu.SemaphoreType.DMA((lines * ring,)),
    ]


def dp_direct_peers(lines, ring):
    me = lax.axis_index("dp")
    z, y = me // ring, me % ring
    out = []
    for d in range(1, lines):
        out += [(z + d < lines, "dp", me + d * ring), (z - d >= 0, "dp", me - d * ring)]
    return out + [(None, "dp", z * ring + (y + k) % ring) for k in range(1, ring)]


def dp_direct_body(lines, ring, ins, outs, scratch):
    (x_ref,), (o_ref,), (send_sem, recv_sem) = ins, outs, scratch
    me = lax.axis_index("dp")
    z, y = me // ring, me % ring
    sends = []

    def send(cond, src, src_z, peer):
        slot = src_z * ring + y
        copy = _remote(src, o_ref.at[src_z, y], send_sem.at[len(sends)], recv_sem.at[slot], "dp", peer)
        pl.when(cond)(copy.start)
        sends.append((cond, copy))

    def spread(cond, src, src_z):
        for k in range(1, ring):
            send(cond, src, src_z, z * ring + (y + k) % ring)

    def arrive(cond, src_z, peer):
        slot = src_z * ring + y
        copy = _remote(o_ref.at[src_z, y], o_ref.at[src_z, y], send_sem.at[0], recv_sem.at[slot], "dp", peer)
        pl.when(cond)(copy.wait_recv)

    always = z >= 0
    spread(always, x_ref, z)
    for d in range(1, lines):
        send(z + d < lines, x_ref, z, me + d * ring)
        send(z - d >= 0, x_ref, z, me - d * ring)
    o_ref[z, y] = x_ref[...]
    yield
    for d in range(1, lines):
        for sign in (1, -1):
            cond = (z + sign * d < lines) & (z + sign * d >= 0)
            src_z = jnp.clip(z + sign * d, 0, lines - 1)
            arrive(cond, src_z, src_z * ring + y)
            spread(cond, o_ref.at[src_z, y], src_z)
        yield
    for k in range(1, ring):
        yy = (y + k) % ring
        for zz in range(lines):
            slot = zz * ring + yy
            copy = _remote(o_ref.at[zz, yy], o_ref.at[zz, yy], send_sem.at[0], recv_sem.at[slot], "dp", z * ring + yy)
            copy.wait_recv()
    for cond, copy in sends:
        pl.when(cond)(copy.wait_send)


def dp_direct_scratch(lines, ring):
    return [
        pltpu.SemaphoreType.DMA((ring - 1 + 2 * (lines - 1) * ring,)),
        pltpu.SemaphoreType.DMA((lines * ring,)),
    ]


def mp_peers(chips):
    _, _, _, far, twin, mates = mp_places(chips)
    return [(None, "mp", peer) for peer in [far, twin] + mates]


def mp_gather_body(chips, ins, outs, scratch):
    (x_ref,), (o_ref,), (send_sem, recv_sem) = ins, outs, scratch
    h, c, k, far, twin, mates = mp_places(chips)
    sends = []

    def send(src, hh, cc, kk, peer):
        slot = (hh * chips + cc) * 2 + kk
        copy = _remote(src, o_ref.at[hh, cc, kk], send_sem.at[len(sends)], recv_sem.at[slot], "mp", peer)
        copy.start()
        sends.append(copy)

    def arrive(hh, cc, kk, peer):
        slot = (hh * chips + cc) * 2 + kk
        copy = _remote(o_ref.at[hh, cc, kk], o_ref.at[hh, cc, kk], send_sem.at[0], recv_sem.at[slot], "mp", peer)
        copy.wait_recv()

    send(x_ref, h, c, k, far)
    for peer in mates:
        send(x_ref, h, c, k, peer)
    send(x_ref, h, c, k, twin)
    o_ref[h, c, k] = x_ref[...]
    yield
    arrive(1 - h, c, k, far)
    for peer in mates:
        send(o_ref.at[1 - h, c, k], 1 - h, c, k, peer)
    send(o_ref.at[1 - h, c, k], 1 - h, c, k, twin)
    yield
    for j in range(1, chips):
        cc = (c + j) % chips
        for hh in (h, 1 - h):
            arrive(hh, cc, k, mates[j - 1])
            send(o_ref.at[hh, cc, k], hh, cc, k, twin)
    yield
    for hh in range(2):
        for cc in range(chips):
            arrive(hh, cc, 1 - k, twin)
    for copy in sends:
        copy.wait_send()


def mp_gather_scratch(chips):
    return [pltpu.SemaphoreType.DMA((4 * chips,)), pltpu.SemaphoreType.DMA((4 * chips,))]


def mp_sum_body(chips, ins, outs, scratch):
    (p_ref,), (o_ref,) = ins, outs
    twin_in, pair, mate_in, far_out, far_in, acc, send_sem, recv_sem = scratch
    h, c, k, far, twin, mates = mp_places(chips)
    sends = []

    def send(src, dst, slot, peer):
        copy = _remote(src, dst, send_sem.at[len(sends)], recv_sem.at[slot], "mp", peer)
        copy.start()
        sends.append(copy)

    def arrive(dst, slot, peer):
        _remote(dst, dst, send_sem.at[0], recv_sem.at[slot], "mp", peer).wait_recv()

    for hh in range(2):
        for cc in range(chips):
            send(p_ref.at[hh, cc, 1 - k], twin_in.at[hh, cc], hh * chips + cc, twin)
    yield
    for j in range(1, chips):
        cc = (c + j) % chips
        for hh in range(2):
            arrive(twin_in.at[hh, cc], hh * chips + cc, twin)
            pair[hh, cc] = (
                p_ref[hh, cc, k].astype(jnp.float32) + twin_in[hh, cc].astype(jnp.float32)
            ).astype(pair.dtype)
            send(pair.at[hh, cc], mate_in.at[c, hh], 2 * chips + c * 2 + hh, mates[j - 1])
    for hh in range(2):
        arrive(twin_in.at[hh, c], hh * chips + c, twin)
        acc[hh] = p_ref[hh, c, k].astype(jnp.float32) + twin_in[hh, c].astype(jnp.float32)
    yield
    for j in range(1, chips):
        cc = (c + j) % chips
        for hh in range(2):
            arrive(mate_in.at[cc, hh], 2 * chips + cc * 2 + hh, mates[j - 1])
            acc[hh] = acc[hh] + mate_in[cc, hh].astype(jnp.float32)
    far_out[...] = acc[1 - h].astype(far_out.dtype)
    send(far_out, far_in, 4 * chips, far)
    yield
    arrive(far_in, 4 * chips, far)
    o_ref[...] = acc[h] + far_in[...].astype(jnp.float32)
    for copy in sends:
        copy.wait_send()


def mp_sum_scratch(chips, rows, cols, dt):
    return [
        pltpu.VMEM((2, chips, rows, cols), dt),
        pltpu.VMEM((2, chips, rows, cols), dt),
        pltpu.VMEM((chips, 2, rows, cols), dt),
        pltpu.VMEM((rows, cols), dt),
        pltpu.VMEM((rows, cols), dt),
        pltpu.VMEM((2, rows, cols), jnp.float32),
        pltpu.SemaphoreType.DMA((4 * chips + 1,)),
        pltpu.SemaphoreType.DMA((4 * chips + 1,)),
    ]


def combined_kernel(parts, *refs):
    n_in = sum(p[2] for p in parts)
    n_out = sum(p[3] for p in parts)
    ins, outs, scratch = refs[:n_in], refs[n_in:n_in + n_out], refs[n_in + n_out:]
    barrier = pltpu.get_barrier_semaphore()
    total = 0
    for peers, _, _, _, _ in parts:
        for cond, axis, peer in peers():
            def signal(axis=axis, peer=peer):
                pl.semaphore_signal(barrier, inc=1, device_id={axis: peer}, device_id_type=MESH)
            if cond is None:
                signal()
                total = total + 1
            else:
                pl.when(cond)(signal)
                total = total + cond.astype(jnp.int32)
    pl.semaphore_wait(barrier, total)
    gens = []
    for _, body, pi, po, ps in parts:
        gens.append(body(ins[:pi], outs[:po], scratch[:ps]))
        ins, outs, scratch = ins[pi:], outs[po:], scratch[ps:]
    while gens:
        for gen in list(gens):
            try:
                next(gen)
            except StopIteration:
                gens.remove(gen)


def combined(parts, inputs, out_shapes, scratch_shapes, cid):
    return pl.pallas_call(
        functools.partial(combined_kernel, parts),
        out_shape=out_shapes,
        in_specs=[pl.BlockSpec(memory_space=pltpu.VMEM)] * len(inputs),
        out_specs=[pl.BlockSpec(memory_space=pltpu.VMEM)] * len(out_shapes),
        scratch_shapes=scratch_shapes,
        compiler_params=pltpu.CompilerParams(collective_id=cid, has_side_effects=True),
    )(*inputs)


def attend(normed, qkv_w, segment, table, mp_index):
    group_rows = normed.shape[0]
    heads_dev = qkv_w.shape[1] // (3 * HD)
    joined = jnp.dot(normed, qkv_w, preferred_element_type=jnp.float32).astype(jnp.bfloat16)
    joined = joined.reshape(group_rows, heads_dev, 3, HD)
    query = joined[:, :, 0]
    keys = joined[:, :, 1]
    vals = joined[:, :, 2]
    head_ids = mp_index * heads_dev + jnp.arange(heads_dev)
    slopes = jnp.exp2(-8.0 * (head_ids + 1).astype(jnp.float32) / H)
    positions = jnp.arange(group_rows)
    distance = (positions[:, None] - positions[None, :]).astype(jnp.float32)
    allowed = (segment[:, None] == segment[None, :]) & (distance >= 0)
    scores = jnp.einsum("thd,shd->hts", query, keys, preferred_element_type=jnp.float32) / jnp.sqrt(
        jnp.float32(HD)
    )
    scores = scores - slopes[:, None, None] * distance[None]
    scores = jnp.where(allowed[None], scores, -jnp.inf)
    probs = jax.nn.softmax(scores, axis=-1).astype(jnp.bfloat16)
    context = jnp.einsum("hts,shd->thd", probs, vals, preferred_element_type=jnp.float32).astype(
        jnp.bfloat16
    )
    context = context.reshape(group_rows, heads_dev * HD)
    key_vals = jnp.stack([keys, vals], 1)
    pages_here = group_rows // PAGE
    key_vals = key_vals.reshape(pages_here, PAGE, 2, heads_dev, HD).transpose(0, 2, 3, 1, 4)
    cache = jnp.zeros((pages_here, 2, heads_dev, PAGE, HD), jnp.bfloat16).at[table].set(key_vals)
    return (context, cache)


def local(hidden_in, segment_ids, page_table, qkv_master, up_master, dense_weight):
    mp_count = lax.axis_size("mp")
    dp_count = lax.axis_size("dp")
    mp_index = lax.axis_index("mp")
    chips = mp_count // 4
    lines = dp_count // RING
    rows = hidden_in.shape[0]
    rows_w = qkv_master.shape[0]
    bf = jnp.bfloat16
    qkv_t = qkv_master.astype(bf).reshape(rows_w, mp_count, -1).transpose(1, 0, 2)
    up_t = up_master.astype(bf).reshape(rows_w, mp_count, -1).transpose(1, 0, 2)
    normed_own = layer_norm(hidden_in.astype(jnp.float32)).astype(bf)
    sd = jax.ShapeDtypeStruct
    qkv_blk, up_blk = combined(
        [
            (
                functools.partial(exchange_peers, mp_count, "mp"),
                functools.partial(exchange_body, mp_count, "mp"),
                2, 2, 3,
            ),
        ],
        [qkv_t, up_t],
        [sd(qkv_t.shape, bf), sd(up_t.shape, bf)],
        exchange_scratch(mp_count, 2),
        0,
    )
    qkv_piece = qkv_blk.reshape(mp_count * rows_w, -1)
    up_piece = up_blk.reshape(mp_count * rows_w, -1)
    qkv_w, normed = combined(
        [
            (functools.partial(dp_peers, lines, RING), functools.partial(dp_gather_body, lines, RING), 1, 1, 2),
            (functools.partial(mp_peers, chips), functools.partial(mp_gather_body, chips), 1, 1, 2),
        ],
        [qkv_piece, normed_own],
        [sd((lines, RING) + qkv_piece.shape, bf), sd((2, chips, 2) + normed_own.shape, bf)],
        dp_scratch(lines, RING) + mp_gather_scratch(chips),
        1,
    )
    normed = normed.reshape(mp_count * rows, -1)
    qkv_w = qkv_w.reshape(-1, qkv_piece.shape[-1])
    context, cache = attend(normed, qkv_w, segment_ids[0], page_table[0], mp_index)
    partial = jnp.dot(context, dense_weight, preferred_element_type=jnp.float32).astype(bf)
    share, up_w = combined(
        [
            (functools.partial(mp_peers, chips), functools.partial(mp_sum_body, chips), 1, 1, 8),
            (functools.partial(dp_peers, lines, RING), functools.partial(dp_gather_body, lines, RING), 1, 1, 2),
        ],
        [partial.reshape(2, chips, 2, rows, -1), up_piece],
        [sd((rows, partial.shape[-1]), jnp.float32), sd((lines, RING) + up_piece.shape, bf)],
        mp_sum_scratch(chips, rows, partial.shape[-1], bf) + dp_scratch(lines, RING),
        2,
    )
    up_w = up_w.reshape(-1, up_piece.shape[-1])
    stream_own = hidden_in.astype(jnp.float32) + share
    normed_two_own = layer_norm(stream_own).astype(bf)
    (normed_two,) = combined(
        [(functools.partial(mp_peers, chips), functools.partial(mp_gather_body, chips), 1, 1, 2)],
        [normed_two_own],
        [sd((2, chips, 2) + normed_two_own.shape, bf)],
        mp_gather_scratch(chips),
        3,
    )
    normed_two = normed_two.reshape(mp_count * rows, -1)
    upper = jnp.dot(normed_two, up_w, preferred_element_type=jnp.float32)
    activated = jax.nn.gelu(upper, approximate=True).astype(bf)
    return (stream_own.astype(bf), activated, cache)


def solution(mesh):
    placed = (
        P(("dp", "mp"), None),
        P("dp", None),
        P("dp", None),
        P(("dp", "mp"), None),
        P(("dp", "mp"), None),
        P("mp", None),
    )
    return jax.shard_map(
        local,
        mesh=mesh,
        in_specs=placed,
        out_specs=(P(("dp", "mp"), None), P("dp", "mp"), P("dp", None, "mp", None, None)),
        check_vma=False,
    )
```

```python
import functools

import jax
import jax.numpy as jnp
from jax import lax
from jax.experimental import pallas as pl
from jax.experimental.pallas import tpu as pltpu
from jax.sharding import PartitionSpec as P

H = 16
HD = 128
PAGE = 128
RING = 4
MESH = pl.DeviceIdType.MESH


def layer_norm(values):
    mean_val = jnp.mean(values, -1, keepdims=True)
    centered = values - mean_val
    variance = jnp.mean(centered * centered, -1, keepdims=True)
    return centered * lax.rsqrt(variance + 1e-05)


def _remote(src, dst, send_sem, recv_sem, axis, peer):
    return pltpu.make_async_remote_copy(
        src_ref=src,
        dst_ref=dst,
        send_sem=send_sem,
        recv_sem=recv_sem,
        device_id={axis: peer},
        device_id_type=MESH,
    )


def mp_places(chips):
    me = lax.axis_index("mp")
    per_half = chips * 2
    h, c, k = me // per_half, (me // 2) % chips, me % 2
    far = (1 - h) * per_half + c * 2 + k
    twin = h * per_half + c * 2 + (1 - k)
    mates = [h * per_half + ((c + j) % chips) * 2 + k for j in range(1, chips)]
    return h, c, k, far, twin, mates


def exchange_peers(n, axis):
    me = lax.axis_index(axis)
    return [(None, axis, lax.rem(me + step, n)) for step in range(1, n)]


def exchange_body(n, axis, ins, outs, scratch):
    send_sem, recv_sem, local_sem = scratch
    me = lax.axis_index(axis)
    copies, locals_ = [], []
    for a in range(len(ins)):
        for step in range(1, n):
            peer = lax.rem(me + step, n)
            slot = a * (n - 1) + step - 1
            copy = _remote(ins[a].at[peer], outs[a].at[me], send_sem.at[slot], recv_sem.at[slot], axis, peer)
            copy.start()
            copies.append(copy)
        own = pltpu.make_async_copy(ins[a].at[me], outs[a].at[me], local_sem.at[a])
        own.start()
        locals_.append(own)
    yield
    for own in locals_:
        own.wait()
    for copy in copies:
        copy.wait()


def exchange_scratch(n, count):
    return [
        pltpu.SemaphoreType.DMA((count * (n - 1),)),
        pltpu.SemaphoreType.DMA((count * (n - 1),)),
        pltpu.SemaphoreType.DMA((count,)),
    ]


def dp_peers(lines, ring):
    me = lax.axis_index("dp")
    z, y = me // ring, me % ring
    out = [(z > 0, "dp", me - ring), (z < lines - 1, "dp", me + ring)]
    return out + [(None, "dp", z * ring + (y + k) % ring) for k in range(1, ring)]


def dp_gather_body(lines, ring, ins, outs, scratch):
    (x_ref,), (o_ref,), (send_sem, recv_sem) = ins, outs, scratch
    me = lax.axis_index("dp")
    z, y = me // ring, me % ring
    has_left, has_right = z > 0, z < lines - 1
    sends = []

    def send(cond, src, src_z, peer):
        slot = src_z * ring + y
        copy = _remote(src, o_ref.at[src_z, y], send_sem.at[len(sends)], recv_sem.at[slot], "dp", peer)
        pl.when(cond)(copy.start)
        sends.append((cond, copy))

    def spread(cond, src, src_z):
        for k in range(1, ring):
            send(cond, src, src_z, z * ring + (y + k) % ring)

    def arrive(cond, src_z, peer):
        slot = src_z * ring + y
        copy = _remote(o_ref.at[src_z, y], o_ref.at[src_z, y], send_sem.at[0], recv_sem.at[slot], "dp", peer)
        pl.when(cond)(copy.wait_recv)

    send(has_right, x_ref, z, me + ring)
    send(has_left, x_ref, z, me - ring)
    spread(z >= 0, x_ref, z)
    o_ref[z, y] = x_ref[...]
    yield
    for s in range(1, lines):
        from_left = z - s >= 0
        src_l = jnp.maximum(z - s, 0)
        arrive(from_left, src_l, me - ring)
        send(from_left & has_right, o_ref.at[src_l, y], src_l, me + ring)
        spread(from_left, o_ref.at[src_l, y], src_l)
        from_right = z + s <= lines - 1
        src_r = jnp.minimum(z + s, lines - 1)
        arrive(from_right, src_r, me + ring)
        send(from_right & has_left, o_ref.at[src_r, y], src_r, me - ring)
        spread(from_right, o_ref.at[src_r, y], src_r)
        yield
    for k in range(1, ring):
        yy = (y + k) % ring
        for zz in range(lines):
            slot = zz * ring + yy
            copy = _remote(o_ref.at[zz, yy], o_ref.at[zz, yy], send_sem.at[0], recv_sem.at[slot], "dp", z * ring + yy)
            copy.wait_recv()
    for cond, copy in sends:
        pl.when(cond)(copy.wait_send)


def dp_scratch(lines, ring):
    return [
        pltpu.SemaphoreType.DMA((1 + ring + (lines - 1) * 2 * ring,)),
        pltpu.SemaphoreType.DMA((lines * ring,)),
    ]


def dp_direct_peers(lines, ring):
    me = lax.axis_index("dp")
    z, y = me // ring, me % ring
    out = []
    for d in range(1, lines):
        out += [(z + d < lines, "dp", me + d * ring), (z - d >= 0, "dp", me - d * ring)]
    return out + [(None, "dp", z * ring + (y + k) % ring) for k in range(1, ring)]


def dp_direct_body(lines, ring, ins, outs, scratch):
    (x_ref,), (o_ref,), (send_sem, recv_sem) = ins, outs, scratch
    me = lax.axis_index("dp")
    z, y = me // ring, me % ring
    sends = []

    def send(cond, src, src_z, peer):
        slot = src_z * ring + y
        copy = _remote(src, o_ref.at[src_z, y], send_sem.at[len(sends)], recv_sem.at[slot], "dp", peer)
        pl.when(cond)(copy.start)
        sends.append((cond, copy))

    def spread(cond, src, src_z):
        for k in range(1, ring):
            send(cond, src, src_z, z * ring + (y + k) % ring)

    def arrive(cond, src_z, peer):
        slot = src_z * ring + y
        copy = _remote(o_ref.at[src_z, y], o_ref.at[src_z, y], send_sem.at[0], recv_sem.at[slot], "dp", peer)
        pl.when(cond)(copy.wait_recv)

    always = z >= 0
    spread(always, x_ref, z)
    for d in range(1, lines):
        send(z + d < lines, x_ref, z, me + d * ring)
        send(z - d >= 0, x_ref, z, me - d * ring)
    o_ref[z, y] = x_ref[...]
    yield
    for d in range(1, lines):
        for sign in (1, -1):
            cond = (z + sign * d < lines) & (z + sign * d >= 0)
            src_z = jnp.clip(z + sign * d, 0, lines - 1)
            arrive(cond, src_z, src_z * ring + y)
            spread(cond, o_ref.at[src_z, y], src_z)
        yield
    for k in range(1, ring):
        yy = (y + k) % ring
        for zz in range(lines):
            slot = zz * ring + yy
            copy = _remote(o_ref.at[zz, yy], o_ref.at[zz, yy], send_sem.at[0], recv_sem.at[slot], "dp", z * ring + yy)
            copy.wait_recv()
    for cond, copy in sends:
        pl.when(cond)(copy.wait_send)


def dp_direct_scratch(lines, ring):
    return [
        pltpu.SemaphoreType.DMA((ring - 1 + 2 * (lines - 1) * ring,)),
        pltpu.SemaphoreType.DMA((lines * ring,)),
    ]


def dp_yfirst_body(lines, ring, ins, outs, scratch):
    (x_ref,), (o_ref,), (send_sem, recv_sem, local_sem) = ins, outs, scratch
    me = lax.axis_index("dp")
    z, y = me // ring, me % ring
    has_left, has_right = z > 0, z < lines - 1
    sends = []

    def send(cond, src, dst, slot, peer):
        copy = _remote(src, dst, send_sem.at[len(sends)], recv_sem.at[slot], "dp", peer)
        pl.when(cond)(copy.start)
        sends.append((cond, copy))

    def arrive(cond, dst, slot, peer):
        copy = _remote(dst, dst, send_sem.at[0], recv_sem.at[slot], "dp", peer)
        pl.when(cond)(copy.wait_recv)

    always = z >= 0
    for k in range(1, ring):
        send(always, x_ref, o_ref.at[z, y], lines + y, z * ring + (y + k) % ring)
    own = pltpu.make_async_copy(x_ref, o_ref.at[z, y], local_sem.at[0])
    own.start()
    yield
    for k in range(1, ring):
        yy = (y + k) % ring
        arrive(always, o_ref.at[z, yy], lines + yy, z * ring + yy)
    own.wait()
    send(has_right, o_ref.at[z], o_ref.at[z], z, me + ring)
    send(has_left, o_ref.at[z], o_ref.at[z], z, me - ring)
    yield
    for s in range(1, lines):
        from_left = z - s >= 0
        src_l = jnp.maximum(z - s, 0)
        arrive(from_left, o_ref.at[src_l], src_l, me - ring)
        send(from_left & has_right, o_ref.at[src_l], o_ref.at[src_l], src_l, me + ring)
        from_right = z + s <= lines - 1
        src_r = jnp.minimum(z + s, lines - 1)
        arrive(from_right, o_ref.at[src_r], src_r, me + ring)
        send(from_right & has_left, o_ref.at[src_r], o_ref.at[src_r], src_r, me - ring)
        yield
    for cond, copy in sends:
        pl.when(cond)(copy.wait_send)


def dp_yfirst_scratch(lines, ring):
    return [
        pltpu.SemaphoreType.DMA((ring - 1 + 2 * lines,)),
        pltpu.SemaphoreType.DMA((lines + ring,)),
        pltpu.SemaphoreType.DMA((1,)),
    ]


def dp_split_parts(lines, ring):
    return [
        (functools.partial(dp_peers, lines, ring), functools.partial(dp_gather_body, lines, ring), 1, 1, 2),
        (functools.partial(dp_peers, lines, ring), functools.partial(dp_yfirst_body, lines, ring), 1, 1, 3),
    ]


def dp_split_scratch(lines, ring):
    return dp_scratch(lines, ring) + dp_yfirst_scratch(lines, ring)


def dp_split_join(first, second):
    return jnp.concatenate([first, second], axis=2).reshape(-1, first.shape[-1])


def mp_peers(chips):
    _, _, _, far, twin, mates = mp_places(chips)
    return [(None, "mp", peer) for peer in [far, twin] + mates]


def mp_gather_body(chips, ins, outs, scratch):
    (x_ref,), (o_ref,), (send_sem, recv_sem) = ins, outs, scratch
    h, c, k, far, twin, mates = mp_places(chips)
    sends = []

    def send(src, hh, cc, kk, peer):
        slot = (hh * chips + cc) * 2 + kk
        copy = _remote(src, o_ref.at[hh, cc, kk], send_sem.at[len(sends)], recv_sem.at[slot], "mp", peer)
        copy.start()
        sends.append(copy)

    def arrive(hh, cc, kk, peer):
        slot = (hh * chips + cc) * 2 + kk
        copy = _remote(o_ref.at[hh, cc, kk], o_ref.at[hh, cc, kk], send_sem.at[0], recv_sem.at[slot], "mp", peer)
        copy.wait_recv()

    send(x_ref, h, c, k, far)
    for peer in mates:
        send(x_ref, h, c, k, peer)
    send(x_ref, h, c, k, twin)
    o_ref[h, c, k] = x_ref[...]
    yield
    arrive(1 - h, c, k, far)
    for peer in mates:
        send(o_ref.at[1 - h, c, k], 1 - h, c, k, peer)
    send(o_ref.at[1 - h, c, k], 1 - h, c, k, twin)
    yield
    for j in range(1, chips):
        cc = (c + j) % chips
        for hh in (h, 1 - h):
            arrive(hh, cc, k, mates[j - 1])
            send(o_ref.at[hh, cc, k], hh, cc, k, twin)
    yield
    for hh in range(2):
        for cc in range(chips):
            arrive(hh, cc, 1 - k, twin)
    for copy in sends:
        copy.wait_send()


def mp_gather_scratch(chips):
    return [pltpu.SemaphoreType.DMA((4 * chips,)), pltpu.SemaphoreType.DMA((4 * chips,))]


def mp_sum_body(chips, ins, outs, scratch):
    (p_ref,), (o_ref,) = ins, outs
    twin_in, pair, mate_in, far_out, far_in, acc, send_sem, recv_sem = scratch
    h, c, k, far, twin, mates = mp_places(chips)
    sends = []

    def send(src, dst, slot, peer):
        copy = _remote(src, dst, send_sem.at[len(sends)], recv_sem.at[slot], "mp", peer)
        copy.start()
        sends.append(copy)

    def arrive(dst, slot, peer):
        _remote(dst, dst, send_sem.at[0], recv_sem.at[slot], "mp", peer).wait_recv()

    for hh in range(2):
        for cc in range(chips):
            send(p_ref.at[hh, cc, 1 - k], twin_in.at[hh, cc], hh * chips + cc, twin)
    yield
    for j in range(1, chips):
        cc = (c + j) % chips
        for hh in range(2):
            arrive(twin_in.at[hh, cc], hh * chips + cc, twin)
            pair[hh, cc] = (
                p_ref[hh, cc, k].astype(jnp.float32) + twin_in[hh, cc].astype(jnp.float32)
            ).astype(pair.dtype)
            send(pair.at[hh, cc], mate_in.at[c, hh], 2 * chips + c * 2 + hh, mates[j - 1])
    for hh in range(2):
        arrive(twin_in.at[hh, c], hh * chips + c, twin)
        acc[hh] = p_ref[hh, c, k].astype(jnp.float32) + twin_in[hh, c].astype(jnp.float32)
    yield
    for j in range(1, chips):
        cc = (c + j) % chips
        for hh in range(2):
            arrive(mate_in.at[cc, hh], 2 * chips + cc * 2 + hh, mates[j - 1])
            acc[hh] = acc[hh] + mate_in[cc, hh].astype(jnp.float32)
    far_out[...] = acc[1 - h].astype(far_out.dtype)
    send(far_out, far_in, 4 * chips, far)
    yield
    arrive(far_in, 4 * chips, far)
    o_ref[...] = acc[h] + far_in[...].astype(jnp.float32)
    for copy in sends:
        copy.wait_send()


def mp_sum_scratch(chips, rows, cols, dt):
    return [
        pltpu.VMEM((2, chips, rows, cols), dt),
        pltpu.VMEM((2, chips, rows, cols), dt),
        pltpu.VMEM((chips, 2, rows, cols), dt),
        pltpu.VMEM((rows, cols), dt),
        pltpu.VMEM((rows, cols), dt),
        pltpu.VMEM((2, rows, cols), jnp.float32),
        pltpu.SemaphoreType.DMA((4 * chips + 1,)),
        pltpu.SemaphoreType.DMA((4 * chips + 1,)),
    ]


def combined_kernel(parts, *refs):
    n_in = sum(p[2] for p in parts)
    n_out = sum(p[3] for p in parts)
    ins, outs, scratch = refs[:n_in], refs[n_in:n_in + n_out], refs[n_in + n_out:]
    barrier = pltpu.get_barrier_semaphore()
    total = 0
    for peers, _, _, _, _ in parts:
        for cond, axis, peer in peers():
            def signal(axis=axis, peer=peer):
                pl.semaphore_signal(barrier, inc=1, device_id={axis: peer}, device_id_type=MESH)
            if cond is None:
                signal()
                total = total + 1
            else:
                pl.when(cond)(signal)
                total = total + cond.astype(jnp.int32)
    pl.semaphore_wait(barrier, total)
    gens = []
    for _, body, pi, po, ps in parts:
        gens.append(body(ins[:pi], outs[:po], scratch[:ps]))
        ins, outs, scratch = ins[pi:], outs[po:], scratch[ps:]
    while gens:
        for gen in list(gens):
            try:
                next(gen)
            except StopIteration:
                gens.remove(gen)


def combined(parts, inputs, out_shapes, scratch_shapes, cid):
    return pl.pallas_call(
        functools.partial(combined_kernel, parts),
        out_shape=out_shapes,
        in_specs=[pl.BlockSpec(memory_space=pltpu.VMEM)] * len(inputs),
        out_specs=[pl.BlockSpec(memory_space=pltpu.VMEM)] * len(out_shapes),
        scratch_shapes=scratch_shapes,
        compiler_params=pltpu.CompilerParams(collective_id=cid, has_side_effects=True),
    )(*inputs)


def attend(normed, qkv_w, segment, table, mp_index):
    group_rows = normed.shape[0]
    heads_dev = qkv_w.shape[1] // (3 * HD)
    joined = jnp.dot(normed, qkv_w, preferred_element_type=jnp.float32).astype(jnp.bfloat16)
    joined = joined.reshape(group_rows, heads_dev, 3, HD)
    query = joined[:, :, 0]
    keys = joined[:, :, 1]
    vals = joined[:, :, 2]
    head_ids = mp_index * heads_dev + jnp.arange(heads_dev)
    slopes = jnp.exp2(-8.0 * (head_ids + 1).astype(jnp.float32) / H)
    positions = jnp.arange(group_rows)
    distance = (positions[:, None] - positions[None, :]).astype(jnp.float32)
    allowed = (segment[:, None] == segment[None, :]) & (distance >= 0)
    scores = jnp.einsum("thd,shd->hts", query, keys, preferred_element_type=jnp.float32) / jnp.sqrt(
        jnp.float32(HD)
    )
    scores = scores - slopes[:, None, None] * distance[None]
    scores = jnp.where(allowed[None], scores, -jnp.inf)
    probs = jax.nn.softmax(scores, axis=-1).astype(jnp.bfloat16)
    context = jnp.einsum("hts,shd->thd", probs, vals, preferred_element_type=jnp.float32).astype(
        jnp.bfloat16
    )
    context = context.reshape(group_rows, heads_dev * HD)
    key_vals = jnp.stack([keys, vals], 1)
    pages_here = group_rows // PAGE
    key_vals = key_vals.reshape(pages_here, PAGE, 2, heads_dev, HD).transpose(0, 2, 3, 1, 4)
    cache = jnp.zeros((pages_here, 2, heads_dev, PAGE, HD), jnp.bfloat16).at[table].set(key_vals)
    return (context, cache)


def local(hidden_in, segment_ids, page_table, qkv_master, up_master, dense_weight):
    mp_count = lax.axis_size("mp")
    dp_count = lax.axis_size("dp")
    mp_index = lax.axis_index("mp")
    chips = mp_count // 4
    lines = dp_count // RING
    rows = hidden_in.shape[0]
    rows_w = qkv_master.shape[0]
    bf = jnp.bfloat16
    qkv_t = qkv_master.astype(bf).reshape(rows_w, mp_count, -1).transpose(1, 0, 2)
    up_t = up_master.astype(bf).reshape(rows_w, mp_count, -1).transpose(1, 0, 2)
    normed_own = layer_norm(hidden_in.astype(jnp.float32)).astype(bf)
    sd = jax.ShapeDtypeStruct
    qkv_blk, up_blk = combined(
        [
            (
                functools.partial(exchange_peers, mp_count, "mp"),
                functools.partial(exchange_body, mp_count, "mp"),
                2, 2, 3,
            ),
        ],
        [qkv_t, up_t],
        [sd(qkv_t.shape, bf), sd(up_t.shape, bf)],
        exchange_scratch(mp_count, 2),
        0,
    )
    qkv_piece = qkv_blk.reshape(mp_count * rows_w, -1)
    up_piece = up_blk.reshape(mp_count * rows_w, -1)
    half = qkv_piece.shape[0] // 2
    qkv_a, qkv_b, normed = combined(
        dp_split_parts(lines, RING)
        + [(functools.partial(mp_peers, chips), functools.partial(mp_gather_body, chips), 1, 1, 2)],
        [qkv_piece[:half], qkv_piece[half:], normed_own],
        [
            sd((lines, RING, half, qkv_piece.shape[-1]), bf),
            sd((lines, RING, half, qkv_piece.shape[-1]), bf),
            sd((2, chips, 2) + normed_own.shape, bf),
        ],
        dp_split_scratch(lines, RING) + mp_gather_scratch(chips),
        1,
    )
    normed = normed.reshape(mp_count * rows, -1)
    qkv_w = dp_split_join(qkv_a, qkv_b)
    context, cache = attend(normed, qkv_w, segment_ids[0], page_table[0], mp_index)
    partial = jnp.dot(context, dense_weight, preferred_element_type=jnp.float32).astype(bf)
    share, up_a, up_b = combined(
        [(functools.partial(mp_peers, chips), functools.partial(mp_sum_body, chips), 1, 1, 8)]
        + dp_split_parts(lines, RING),
        [partial.reshape(2, chips, 2, rows, -1), up_piece[:half], up_piece[half:]],
        [
            sd((rows, partial.shape[-1]), jnp.float32),
            sd((lines, RING, half, up_piece.shape[-1]), bf),
            sd((lines, RING, half, up_piece.shape[-1]), bf),
        ],
        mp_sum_scratch(chips, rows, partial.shape[-1], bf) + dp_split_scratch(lines, RING),
        2,
    )
    up_w = dp_split_join(up_a, up_b)
    stream_own = hidden_in.astype(jnp.float32) + share
    normed_two_own = layer_norm(stream_own).astype(bf)
    (normed_two,) = combined(
        [(functools.partial(mp_peers, chips), functools.partial(mp_gather_body, chips), 1, 1, 2)],
        [normed_two_own],
        [sd((2, chips, 2) + normed_two_own.shape, bf)],
        mp_gather_scratch(chips),
        3,
    )
    normed_two = normed_two.reshape(mp_count * rows, -1)
    upper = jnp.dot(normed_two, up_w, preferred_element_type=jnp.float32)
    activated = jax.nn.gelu(upper, approximate=True).astype(bf)
    return (stream_own.astype(bf), activated, cache)


def solution(mesh):
    placed = (
        P(("dp", "mp"), None),
        P("dp", None),
        P("dp", None),
        P(("dp", "mp"), None),
        P(("dp", "mp"), None),
        P("mp", None),
    )
    return jax.shard_map(
        local,
        mesh=mesh,
        in_specs=placed,
        out_specs=(P(("dp", "mp"), None), P("dp", "mp"), P("dp", None, "mp", None, None)),
        check_vma=False,
    )
```

```python
import functools

import jax
import jax.numpy as jnp
from jax import lax
from jax.experimental import pallas as pl
from jax.experimental.pallas import tpu as pltpu
from jax.sharding import PartitionSpec as P

H = 16
HD = 128
PAGE = 128
RING = 4
MESH = pl.DeviceIdType.MESH


def layer_norm(values):
    mean_val = jnp.mean(values, -1, keepdims=True)
    centered = values - mean_val
    variance = jnp.mean(centered * centered, -1, keepdims=True)
    return centered * lax.rsqrt(variance + 1e-05)


def _remote(src, dst, send_sem, recv_sem, axis, peer):
    return pltpu.make_async_remote_copy(
        src_ref=src,
        dst_ref=dst,
        send_sem=send_sem,
        recv_sem=recv_sem,
        device_id={axis: peer},
        device_id_type=MESH,
    )


def mp_places(chips):
    me = lax.axis_index("mp")
    per_half = chips * 2
    h, c, k = me // per_half, (me // 2) % chips, me % 2
    far = (1 - h) * per_half + c * 2 + k
    twin = h * per_half + c * 2 + (1 - k)
    mates = [h * per_half + ((c + j) % chips) * 2 + k for j in range(1, chips)]
    return h, c, k, far, twin, mates


def exchange_peers(n, axis):
    me = lax.axis_index(axis)
    return [(None, axis, lax.rem(me + step, n)) for step in range(1, n)]


def exchange_body(n, axis, ins, outs, scratch):
    send_sem, recv_sem, local_sem = scratch
    me = lax.axis_index(axis)
    copies, locals_ = [], []
    for a in range(len(ins)):
        for step in range(1, n):
            peer = lax.rem(me + step, n)
            slot = a * (n - 1) + step - 1
            copy = _remote(ins[a].at[peer], outs[a].at[me], send_sem.at[slot], recv_sem.at[slot], axis, peer)
            copy.start()
            copies.append(copy)
        own = pltpu.make_async_copy(ins[a].at[me], outs[a].at[me], local_sem.at[a])
        own.start()
        locals_.append(own)
    yield
    for own in locals_:
        own.wait()
    for copy in copies:
        copy.wait()


def exchange_scratch(n, count):
    return [
        pltpu.SemaphoreType.DMA((count * (n - 1),)),
        pltpu.SemaphoreType.DMA((count * (n - 1),)),
        pltpu.SemaphoreType.DMA((count,)),
    ]


def dp_peers(lines, ring):
    me = lax.axis_index("dp")
    z, y = me // ring, me % ring
    out = [(z > 0, "dp", me - ring), (z < lines - 1, "dp", me + ring)]
    return out + [(None, "dp", z * ring + (y + k) % ring) for k in range(1, ring)]


def dp_gather_body(lines, ring, ins, outs, scratch):
    (x_ref,), (o_ref,), (send_sem, recv_sem) = ins, outs, scratch
    me = lax.axis_index("dp")
    z, y = me // ring, me % ring
    has_left, has_right = z > 0, z < lines - 1
    sends = []

    def send(cond, src, src_z, peer):
        slot = src_z * ring + y
        copy = _remote(src, o_ref.at[src_z, y], send_sem.at[len(sends)], recv_sem.at[slot], "dp", peer)
        pl.when(cond)(copy.start)
        sends.append((cond, copy))

    def spread(cond, src, src_z):
        for k in range(1, ring):
            send(cond, src, src_z, z * ring + (y + k) % ring)

    def arrive(cond, src_z, peer):
        slot = src_z * ring + y
        copy = _remote(o_ref.at[src_z, y], o_ref.at[src_z, y], send_sem.at[0], recv_sem.at[slot], "dp", peer)
        pl.when(cond)(copy.wait_recv)

    send(has_right, x_ref, z, me + ring)
    send(has_left, x_ref, z, me - ring)
    spread(z >= 0, x_ref, z)
    o_ref[z, y] = x_ref[...]
    yield
    for s in range(1, lines):
        from_left = z - s >= 0
        src_l = jnp.maximum(z - s, 0)
        arrive(from_left, src_l, me - ring)
        send(from_left & has_right, o_ref.at[src_l, y], src_l, me + ring)
        spread(from_left, o_ref.at[src_l, y], src_l)
        from_right = z + s <= lines - 1
        src_r = jnp.minimum(z + s, lines - 1)
        arrive(from_right, src_r, me + ring)
        send(from_right & has_left, o_ref.at[src_r, y], src_r, me - ring)
        spread(from_right, o_ref.at[src_r, y], src_r)
        yield
    for k in range(1, ring):
        yy = (y + k) % ring
        for zz in range(lines):
            slot = zz * ring + yy
            copy = _remote(o_ref.at[zz, yy], o_ref.at[zz, yy], send_sem.at[0], recv_sem.at[slot], "dp", z * ring + yy)
            copy.wait_recv()
    for cond, copy in sends:
        pl.when(cond)(copy.wait_send)


def dp_scratch(lines, ring):
    return [
        pltpu.SemaphoreType.DMA((1 + ring + (lines - 1) * 2 * ring,)),
        pltpu.SemaphoreType.DMA((lines * ring,)),
    ]


def dp_direct_peers(lines, ring):
    me = lax.axis_index("dp")
    z, y = me // ring, me % ring
    out = []
    for d in range(1, lines):
        out += [(z + d < lines, "dp", me + d * ring), (z - d >= 0, "dp", me - d * ring)]
    return out + [(None, "dp", z * ring + (y + k) % ring) for k in range(1, ring)]


def dp_direct_body(lines, ring, ins, outs, scratch):
    (x_ref,), (o_ref,), (send_sem, recv_sem) = ins, outs, scratch
    me = lax.axis_index("dp")
    z, y = me // ring, me % ring
    sends = []

    def send(cond, src, src_z, peer):
        slot = src_z * ring + y
        copy = _remote(src, o_ref.at[src_z, y], send_sem.at[len(sends)], recv_sem.at[slot], "dp", peer)
        pl.when(cond)(copy.start)
        sends.append((cond, copy))

    def spread(cond, src, src_z):
        for k in range(1, ring):
            send(cond, src, src_z, z * ring + (y + k) % ring)

    def arrive(cond, src_z, peer):
        slot = src_z * ring + y
        copy = _remote(o_ref.at[src_z, y], o_ref.at[src_z, y], send_sem.at[0], recv_sem.at[slot], "dp", peer)
        pl.when(cond)(copy.wait_recv)

    always = z >= 0
    spread(always, x_ref, z)
    for d in range(1, lines):
        send(z + d < lines, x_ref, z, me + d * ring)
        send(z - d >= 0, x_ref, z, me - d * ring)
    o_ref[z, y] = x_ref[...]
    yield
    for d in range(1, lines):
        for sign in (1, -1):
            cond = (z + sign * d < lines) & (z + sign * d >= 0)
            src_z = jnp.clip(z + sign * d, 0, lines - 1)
            arrive(cond, src_z, src_z * ring + y)
            spread(cond, o_ref.at[src_z, y], src_z)
        yield
    for k in range(1, ring):
        yy = (y + k) % ring
        for zz in range(lines):
            slot = zz * ring + yy
            copy = _remote(o_ref.at[zz, yy], o_ref.at[zz, yy], send_sem.at[0], recv_sem.at[slot], "dp", z * ring + yy)
            copy.wait_recv()
    for cond, copy in sends:
        pl.when(cond)(copy.wait_send)


def dp_direct_scratch(lines, ring):
    return [
        pltpu.SemaphoreType.DMA((ring - 1 + 2 * (lines - 1) * ring,)),
        pltpu.SemaphoreType.DMA((lines * ring,)),
    ]


def weights_peers(n, lines, ring):
    return exchange_peers(n, "mp") + dp_peers(lines, ring)


def weights_body(n, lines, ring, ins, outs, scratch):
    (qkv_t, up_t), (qkv_full, up_blk) = ins, outs
    ex_send, ex_recv, ex_local, qkv_blk, qkv_rows, dp_send, dp_recv = scratch
    yield from exchange_body(n, "mp", [qkv_t, up_t], [qkv_blk, up_blk], (ex_send, ex_recv, ex_local))
    per = qkv_blk.shape[1]
    for m in range(n):
        qkv_rows[m * per:(m + 1) * per, :] = qkv_blk[m]
    yield from dp_gather_body(lines, ring, [qkv_rows], [qkv_full], (dp_send, dp_recv))


def mp_peers(chips):
    _, _, _, far, twin, mates = mp_places(chips)
    return [(None, "mp", peer) for peer in [far, twin] + mates]


def mp_gather_body(chips, ins, outs, scratch):
    (x_ref,), (o_ref,), (send_sem, recv_sem) = ins, outs, scratch
    h, c, k, far, twin, mates = mp_places(chips)
    sends = []

    def send(src, hh, cc, kk, peer):
        slot = (hh * chips + cc) * 2 + kk
        copy = _remote(src, o_ref.at[hh, cc, kk], send_sem.at[len(sends)], recv_sem.at[slot], "mp", peer)
        copy.start()
        sends.append(copy)

    def arrive(hh, cc, kk, peer):
        slot = (hh * chips + cc) * 2 + kk
        copy = _remote(o_ref.at[hh, cc, kk], o_ref.at[hh, cc, kk], send_sem.at[0], recv_sem.at[slot], "mp", peer)
        copy.wait_recv()

    send(x_ref, h, c, k, far)
    for peer in mates:
        send(x_ref, h, c, k, peer)
    send(x_ref, h, c, k, twin)
    o_ref[h, c, k] = x_ref[...]
    yield
    arrive(1 - h, c, k, far)
    for peer in mates:
        send(o_ref.at[1 - h, c, k], 1 - h, c, k, peer)
    send(o_ref.at[1 - h, c, k], 1 - h, c, k, twin)
    yield
    for j in range(1, chips):
        cc = (c + j) % chips
        for hh in (h, 1 - h):
            arrive(hh, cc, k, mates[j - 1])
            send(o_ref.at[hh, cc, k], hh, cc, k, twin)
    yield
    for hh in range(2):
        for cc in range(chips):
            arrive(hh, cc, 1 - k, twin)
    for copy in sends:
        copy.wait_send()


def mp_gather_scratch(chips):
    return [pltpu.SemaphoreType.DMA((4 * chips,)), pltpu.SemaphoreType.DMA((4 * chips,))]


def mp_sum_body(chips, ins, outs, scratch):
    (p_ref,), (o_ref,) = ins, outs
    twin_in, pair, mate_in, far_out, far_in, acc, send_sem, recv_sem = scratch
    h, c, k, far, twin, mates = mp_places(chips)
    sends = []

    def send(src, dst, slot, peer):
        copy = _remote(src, dst, send_sem.at[len(sends)], recv_sem.at[slot], "mp", peer)
        copy.start()
        sends.append(copy)

    def arrive(dst, slot, peer):
        _remote(dst, dst, send_sem.at[0], recv_sem.at[slot], "mp", peer).wait_recv()

    for hh in range(2):
        for cc in range(chips):
            send(p_ref.at[hh, cc, 1 - k], twin_in.at[hh, cc], hh * chips + cc, twin)
    yield
    for j in range(1, chips):
        cc = (c + j) % chips
        for hh in range(2):
            arrive(twin_in.at[hh, cc], hh * chips + cc, twin)
            pair[hh, cc] = (
                p_ref[hh, cc, k].astype(jnp.float32) + twin_in[hh, cc].astype(jnp.float32)
            ).astype(pair.dtype)
            send(pair.at[hh, cc], mate_in.at[c, hh], 2 * chips + c * 2 + hh, mates[j - 1])
    for hh in range(2):
        arrive(twin_in.at[hh, c], hh * chips + c, twin)
        acc[hh] = p_ref[hh, c, k].astype(jnp.float32) + twin_in[hh, c].astype(jnp.float32)
    yield
    for j in range(1, chips):
        cc = (c + j) % chips
        for hh in range(2):
            arrive(mate_in.at[cc, hh], 2 * chips + cc * 2 + hh, mates[j - 1])
            acc[hh] = acc[hh] + mate_in[cc, hh].astype(jnp.float32)
    far_out[...] = acc[1 - h].astype(far_out.dtype)
    send(far_out, far_in, 4 * chips, far)
    yield
    arrive(far_in, 4 * chips, far)
    o_ref[...] = acc[h] + far_in[...].astype(jnp.float32)
    for copy in sends:
        copy.wait_send()


def mp_sum_scratch(chips, rows, cols, dt):
    return [
        pltpu.VMEM((2, chips, rows, cols), dt),
        pltpu.VMEM((2, chips, rows, cols), dt),
        pltpu.VMEM((chips, 2, rows, cols), dt),
        pltpu.VMEM((rows, cols), dt),
        pltpu.VMEM((rows, cols), dt),
        pltpu.VMEM((2, rows, cols), jnp.float32),
        pltpu.SemaphoreType.DMA((4 * chips + 1,)),
        pltpu.SemaphoreType.DMA((4 * chips + 1,)),
    ]


def combined_kernel(parts, *refs):
    n_in = sum(p[2] for p in parts)
    n_out = sum(p[3] for p in parts)
    ins, outs, scratch = refs[:n_in], refs[n_in:n_in + n_out], refs[n_in + n_out:]
    barrier = pltpu.get_barrier_semaphore()
    total = 0
    for peers, _, _, _, _ in parts:
        for cond, axis, peer in peers():
            def signal(axis=axis, peer=peer):
                pl.semaphore_signal(barrier, inc=1, device_id={axis: peer}, device_id_type=MESH)
            if cond is None:
                signal()
                total = total + 1
            else:
                pl.when(cond)(signal)
                total = total + cond.astype(jnp.int32)
    pl.semaphore_wait(barrier, total)
    gens = []
    for _, body, pi, po, ps in parts:
        gens.append(body(ins[:pi], outs[:po], scratch[:ps]))
        ins, outs, scratch = ins[pi:], outs[po:], scratch[ps:]
    while gens:
        for gen in list(gens):
            try:
                next(gen)
            except StopIteration:
                gens.remove(gen)


def combined(parts, inputs, out_shapes, scratch_shapes, cid):
    return pl.pallas_call(
        functools.partial(combined_kernel, parts),
        out_shape=out_shapes,
        in_specs=[pl.BlockSpec(memory_space=pltpu.VMEM)] * len(inputs),
        out_specs=[pl.BlockSpec(memory_space=pltpu.VMEM)] * len(out_shapes),
        scratch_shapes=scratch_shapes,
        compiler_params=pltpu.CompilerParams(collective_id=cid, has_side_effects=True),
    )(*inputs)


def attend(normed, qkv_w, segment, table, mp_index):
    group_rows = normed.shape[0]
    heads_dev = qkv_w.shape[1] // (3 * HD)
    joined = jnp.dot(normed, qkv_w, preferred_element_type=jnp.float32).astype(jnp.bfloat16)
    joined = joined.reshape(group_rows, heads_dev, 3, HD)
    query = joined[:, :, 0]
    keys = joined[:, :, 1]
    vals = joined[:, :, 2]
    head_ids = mp_index * heads_dev + jnp.arange(heads_dev)
    slopes = jnp.exp2(-8.0 * (head_ids + 1).astype(jnp.float32) / H)
    positions = jnp.arange(group_rows)
    distance = (positions[:, None] - positions[None, :]).astype(jnp.float32)
    allowed = (segment[:, None] == segment[None, :]) & (distance >= 0)
    scores = jnp.einsum("thd,shd->hts", query, keys, preferred_element_type=jnp.float32) / jnp.sqrt(
        jnp.float32(HD)
    )
    scores = scores - slopes[:, None, None] * distance[None]
    scores = jnp.where(allowed[None], scores, -jnp.inf)
    probs = jax.nn.softmax(scores, axis=-1).astype(jnp.bfloat16)
    context = jnp.einsum("hts,shd->thd", probs, vals, preferred_element_type=jnp.float32).astype(
        jnp.bfloat16
    )
    context = context.reshape(group_rows, heads_dev * HD)
    key_vals = jnp.stack([keys, vals], 1)
    pages_here = group_rows // PAGE
    key_vals = key_vals.reshape(pages_here, PAGE, 2, heads_dev, HD).transpose(0, 2, 3, 1, 4)
    cache = jnp.zeros((pages_here, 2, heads_dev, PAGE, HD), jnp.bfloat16).at[table].set(key_vals)
    return (context, cache)


def local(hidden_in, segment_ids, page_table, qkv_master, up_master, dense_weight):
    mp_count = lax.axis_size("mp")
    dp_count = lax.axis_size("dp")
    mp_index = lax.axis_index("mp")
    chips = mp_count // 4
    lines = dp_count // RING
    rows = hidden_in.shape[0]
    rows_w = qkv_master.shape[0]
    bf = jnp.bfloat16
    qkv_t = qkv_master.astype(bf).reshape(rows_w, mp_count, -1).transpose(1, 0, 2)
    up_t = up_master.astype(bf).reshape(rows_w, mp_count, -1).transpose(1, 0, 2)
    normed_own = layer_norm(hidden_in.astype(jnp.float32)).astype(bf)
    sd = jax.ShapeDtypeStruct
    qkv_rows = sd((mp_count * rows_w, qkv_t.shape[-1]), bf)
    qkv_w, up_blk, normed = combined(
        [
            (
                functools.partial(weights_peers, mp_count, lines, RING),
                functools.partial(weights_body, mp_count, lines, RING),
                2, 2, 7,
            ),
            (functools.partial(mp_peers, chips), functools.partial(mp_gather_body, chips), 1, 1, 2),
        ],
        [qkv_t, up_t, normed_own],
        [
            sd((lines, RING) + qkv_rows.shape, bf),
            sd(up_t.shape, bf),
            sd((2, chips, 2) + normed_own.shape, bf),
        ],
        exchange_scratch(mp_count, 2)
        + [pltpu.VMEM(qkv_t.shape, bf), pltpu.VMEM(qkv_rows.shape, bf)]
        + dp_scratch(lines, RING)
        + mp_gather_scratch(chips),
        1,
    )
    normed = normed.reshape(mp_count * rows, -1)
    qkv_w = qkv_w.reshape(-1, qkv_t.shape[-1])
    up_piece = up_blk.reshape(mp_count * rows_w, -1)
    context, cache = attend(normed, qkv_w, segment_ids[0], page_table[0], mp_index)
    partial = jnp.dot(context, dense_weight, preferred_element_type=jnp.float32).astype(bf)
    share, up_w = combined(
        [
            (functools.partial(mp_peers, chips), functools.partial(mp_sum_body, chips), 1, 1, 8),
            (functools.partial(dp_peers, lines, RING), functools.partial(dp_gather_body, lines, RING), 1, 1, 2),
        ],
        [partial.reshape(2, chips, 2, rows, -1), up_piece],
        [sd((rows, partial.shape[-1]), jnp.float32), sd((lines, RING) + up_piece.shape, bf)],
        mp_sum_scratch(chips, rows, partial.shape[-1], bf) + dp_scratch(lines, RING),
        2,
    )
    up_w = up_w.reshape(-1, up_piece.shape[-1])
    stream_own = hidden_in.astype(jnp.float32) + share
    normed_two_own = layer_norm(stream_own).astype(bf)
    (normed_two,) = combined(
        [(functools.partial(mp_peers, chips), functools.partial(mp_gather_body, chips), 1, 1, 2)],
        [normed_two_own],
        [sd((2, chips, 2) + normed_two_own.shape, bf)],
        mp_gather_scratch(chips),
        3,
    )
    normed_two = normed_two.reshape(mp_count * rows, -1)
    upper = jnp.dot(normed_two, up_w, preferred_element_type=jnp.float32)
    activated = jax.nn.gelu(upper, approximate=True).astype(bf)
    return (stream_own.astype(bf), activated, cache)


def solution(mesh):
    placed = (
        P(("dp", "mp"), None),
        P("dp", None),
        P("dp", None),
        P(("dp", "mp"), None),
        P(("dp", "mp"), None),
        P("mp", None),
    )
    return jax.shard_map(
        local,
        mesh=mesh,
        in_specs=placed,
        out_specs=(P(("dp", "mp"), None), P("dp", "mp"), P("dp", None, "mp", None, None)),
        check_vma=False,
    )
```

```python
import functools

import jax
import jax.numpy as jnp
from jax import lax
from jax.experimental import pallas as pl
from jax.experimental.pallas import tpu as pltpu
from jax.sharding import PartitionSpec as P

H = 16
HD = 128
PAGE = 128
RING = 4
MESH = pl.DeviceIdType.MESH


def layer_norm(values):
    mean_val = jnp.mean(values, -1, keepdims=True)
    centered = values - mean_val
    variance = jnp.mean(centered * centered, -1, keepdims=True)
    return centered * lax.rsqrt(variance + 1e-05)


def _remote(src, dst, send_sem, recv_sem, axis, peer):
    return pltpu.make_async_remote_copy(
        src_ref=src,
        dst_ref=dst,
        send_sem=send_sem,
        recv_sem=recv_sem,
        device_id={axis: peer},
        device_id_type=MESH,
    )


def mp_places(chips):
    me = lax.axis_index("mp")
    per_half = chips * 2
    h, c, k = me // per_half, (me // 2) % chips, me % 2
    far = (1 - h) * per_half + c * 2 + k
    twin = h * per_half + c * 2 + (1 - k)
    mates = [h * per_half + ((c + j) % chips) * 2 + k for j in range(1, chips)]
    return h, c, k, far, twin, mates


def exchange_peers(n, axis):
    me = lax.axis_index(axis)
    return [(None, axis, lax.rem(me + step, n)) for step in range(1, n)]


def exchange_body(n, axis, ins, outs, scratch):
    send_sem, recv_sem, local_sem = scratch
    me = lax.axis_index(axis)
    copies, locals_ = [], []
    for a in range(len(ins)):
        for step in range(1, n):
            peer = lax.rem(me + step, n)
            slot = a * (n - 1) + step - 1
            copy = _remote(ins[a].at[peer], outs[a].at[me], send_sem.at[slot], recv_sem.at[slot], axis, peer)
            copy.start()
            copies.append(copy)
        own = pltpu.make_async_copy(ins[a].at[me], outs[a].at[me], local_sem.at[a])
        own.start()
        locals_.append(own)
    yield
    for own in locals_:
        own.wait()
    for copy in copies:
        copy.wait()


def exchange_scratch(n, count):
    return [
        pltpu.SemaphoreType.DMA((count * (n - 1),)),
        pltpu.SemaphoreType.DMA((count * (n - 1),)),
        pltpu.SemaphoreType.DMA((count,)),
    ]


def dp_peers(lines, ring):
    me = lax.axis_index("dp")
    z, y = me // ring, me % ring
    out = [(z > 0, "dp", me - ring), (z < lines - 1, "dp", me + ring)]
    return out + [(None, "dp", z * ring + (y + k) % ring) for k in range(1, ring)]


def dp_gather_body(lines, ring, ins, outs, scratch):
    (x_ref,), (o_ref,), (send_sem, recv_sem) = ins, outs, scratch
    me = lax.axis_index("dp")
    z, y = me // ring, me % ring
    has_left, has_right = z > 0, z < lines - 1
    sends = []

    def send(cond, src, src_z, peer):
        slot = src_z * ring + y
        copy = _remote(src, o_ref.at[src_z, y], send_sem.at[len(sends)], recv_sem.at[slot], "dp", peer)
        pl.when(cond)(copy.start)
        sends.append((cond, copy))

    def spread(cond, src, src_z):
        for k in range(1, ring):
            send(cond, src, src_z, z * ring + (y + k) % ring)

    def arrive(cond, src_z, peer):
        slot = src_z * ring + y
        copy = _remote(o_ref.at[src_z, y], o_ref.at[src_z, y], send_sem.at[0], recv_sem.at[slot], "dp", peer)
        pl.when(cond)(copy.wait_recv)

    send(has_right, x_ref, z, me + ring)
    send(has_left, x_ref, z, me - ring)
    spread(z >= 0, x_ref, z)
    o_ref[z, y] = x_ref[...]
    yield
    for s in range(1, lines):
        from_left = z - s >= 0
        src_l = jnp.maximum(z - s, 0)
        arrive(from_left, src_l, me - ring)
        send(from_left & has_right, o_ref.at[src_l, y], src_l, me + ring)
        spread(from_left, o_ref.at[src_l, y], src_l)
        from_right = z + s <= lines - 1
        src_r = jnp.minimum(z + s, lines - 1)
        arrive(from_right, src_r, me + ring)
        send(from_right & has_left, o_ref.at[src_r, y], src_r, me - ring)
        spread(from_right, o_ref.at[src_r, y], src_r)
        yield
    for k in range(1, ring):
        yy = (y + k) % ring
        for zz in range(lines):
            slot = zz * ring + yy
            copy = _remote(o_ref.at[zz, yy], o_ref.at[zz, yy], send_sem.at[0], recv_sem.at[slot], "dp", z * ring + yy)
            copy.wait_recv()
    for cond, copy in sends:
        pl.when(cond)(copy.wait_send)


def dp_scratch(lines, ring):
    return [
        pltpu.SemaphoreType.DMA((1 + ring + (lines - 1) * 2 * ring,)),
        pltpu.SemaphoreType.DMA((lines * ring,)),
    ]


def dp_direct_peers(lines, ring):
    me = lax.axis_index("dp")
    z, y = me // ring, me % ring
    out = []
    for d in range(1, lines):
        out += [(z + d < lines, "dp", me + d * ring), (z - d >= 0, "dp", me - d * ring)]
    return out + [(None, "dp", z * ring + (y + k) % ring) for k in range(1, ring)]


def dp_direct_body(lines, ring, ins, outs, scratch):
    (x_ref,), (o_ref,), (send_sem, recv_sem) = ins, outs, scratch
    me = lax.axis_index("dp")
    z, y = me // ring, me % ring
    sends = []

    def send(cond, src, src_z, peer):
        slot = src_z * ring + y
        copy = _remote(src, o_ref.at[src_z, y], send_sem.at[len(sends)], recv_sem.at[slot], "dp", peer)
        pl.when(cond)(copy.start)
        sends.append((cond, copy))

    def spread(cond, src, src_z):
        for k in range(1, ring):
            send(cond, src, src_z, z * ring + (y + k) % ring)

    def arrive(cond, src_z, peer):
        slot = src_z * ring + y
        copy = _remote(o_ref.at[src_z, y], o_ref.at[src_z, y], send_sem.at[0], recv_sem.at[slot], "dp", peer)
        pl.when(cond)(copy.wait_recv)

    always = z >= 0
    spread(always, x_ref, z)
    for d in range(1, lines):
        send(z + d < lines, x_ref, z, me + d * ring)
        send(z - d >= 0, x_ref, z, me - d * ring)
    o_ref[z, y] = x_ref[...]
    yield
    for d in range(1, lines):
        for sign in (1, -1):
            cond = (z + sign * d < lines) & (z + sign * d >= 0)
            src_z = jnp.clip(z + sign * d, 0, lines - 1)
            arrive(cond, src_z, src_z * ring + y)
            spread(cond, o_ref.at[src_z, y], src_z)
        yield
    for k in range(1, ring):
        yy = (y + k) % ring
        for zz in range(lines):
            slot = zz * ring + yy
            copy = _remote(o_ref.at[zz, yy], o_ref.at[zz, yy], send_sem.at[0], recv_sem.at[slot], "dp", z * ring + yy)
            copy.wait_recv()
    for cond, copy in sends:
        pl.when(cond)(copy.wait_send)


def dp_direct_scratch(lines, ring):
    return [
        pltpu.SemaphoreType.DMA((ring - 1 + 2 * (lines - 1) * ring,)),
        pltpu.SemaphoreType.DMA((lines * ring,)),
    ]


def weights_peers(n, lines, ring):
    return exchange_peers(n, "mp") + dp_peers(lines, ring)


def weights_body(n, lines, ring, ins, outs, scratch):
    (qkv_t, up_t), (qkv_full, up_blk) = ins, outs
    ex_send, ex_recv, ex_local, qkv_blk, qkv_rows, dp_send, dp_recv = scratch
    yield from exchange_body(n, "mp", [qkv_t, up_t], [qkv_blk, up_blk], (ex_send, ex_recv, ex_local))
    per = qkv_blk.shape[1]
    for m in range(n):
        qkv_rows[m * per:(m + 1) * per, :] = qkv_blk[m]
    yield from dp_gather_body(lines, ring, [qkv_rows], [qkv_full], (dp_send, dp_recv))


def tail_peers(chips):
    return mp_peers(chips) + mp_peers(chips)


def tail_body(chips, ins, outs, scratch):
    (p_ref, h_ref), (hidden_ref, normed_ref) = ins, outs
    sum_scratch, (share, own), gather_scratch = scratch[:8], scratch[8:10], scratch[10:]
    yield from mp_sum_body(chips, [p_ref], [share], sum_scratch)
    stream = h_ref[...].astype(jnp.float32) + share[...]
    hidden_ref[...] = stream.astype(hidden_ref.dtype)
    own[...] = layer_norm(stream).astype(own.dtype)
    yield from mp_gather_body(chips, [own], [normed_ref], gather_scratch)


def mp_peers(chips):
    _, _, _, far, twin, mates = mp_places(chips)
    return [(None, "mp", peer) for peer in [far, twin] + mates]


def mp_gather_body(chips, ins, outs, scratch):
    (x_ref,), (o_ref,), (send_sem, recv_sem) = ins, outs, scratch
    h, c, k, far, twin, mates = mp_places(chips)
    sends = []

    def send(src, hh, cc, kk, peer):
        slot = (hh * chips + cc) * 2 + kk
        copy = _remote(src, o_ref.at[hh, cc, kk], send_sem.at[len(sends)], recv_sem.at[slot], "mp", peer)
        copy.start()
        sends.append(copy)

    def arrive(hh, cc, kk, peer):
        slot = (hh * chips + cc) * 2 + kk
        copy = _remote(o_ref.at[hh, cc, kk], o_ref.at[hh, cc, kk], send_sem.at[0], recv_sem.at[slot], "mp", peer)
        copy.wait_recv()

    send(x_ref, h, c, k, far)
    for peer in mates:
        send(x_ref, h, c, k, peer)
    send(x_ref, h, c, k, twin)
    o_ref[h, c, k] = x_ref[...]
    yield
    arrive(1 - h, c, k, far)
    for peer in mates:
        send(o_ref.at[1 - h, c, k], 1 - h, c, k, peer)
    send(o_ref.at[1 - h, c, k], 1 - h, c, k, twin)
    yield
    for j in range(1, chips):
        cc = (c + j) % chips
        for hh in (h, 1 - h):
            arrive(hh, cc, k, mates[j - 1])
            send(o_ref.at[hh, cc, k], hh, cc, k, twin)
    yield
    for hh in range(2):
        for cc in range(chips):
            arrive(hh, cc, 1 - k, twin)
    for copy in sends:
        copy.wait_send()


def mp_gather_scratch(chips):
    return [pltpu.SemaphoreType.DMA((4 * chips,)), pltpu.SemaphoreType.DMA((4 * chips,))]


def mp_sum_body(chips, ins, outs, scratch):
    (p_ref,), (o_ref,) = ins, outs
    twin_in, pair, mate_in, far_out, far_in, acc, send_sem, recv_sem = scratch
    h, c, k, far, twin, mates = mp_places(chips)
    sends = []

    def send(src, dst, slot, peer):
        copy = _remote(src, dst, send_sem.at[len(sends)], recv_sem.at[slot], "mp", peer)
        copy.start()
        sends.append(copy)

    def arrive(dst, slot, peer):
        _remote(dst, dst, send_sem.at[0], recv_sem.at[slot], "mp", peer).wait_recv()

    for hh in range(2):
        for cc in range(chips):
            send(p_ref.at[hh, cc, 1 - k], twin_in.at[hh, cc], hh * chips + cc, twin)
    yield
    for j in range(1, chips):
        cc = (c + j) % chips
        for hh in range(2):
            arrive(twin_in.at[hh, cc], hh * chips + cc, twin)
            pair[hh, cc] = (
                p_ref[hh, cc, k].astype(jnp.float32) + twin_in[hh, cc].astype(jnp.float32)
            ).astype(pair.dtype)
            send(pair.at[hh, cc], mate_in.at[c, hh], 2 * chips + c * 2 + hh, mates[j - 1])
    for hh in range(2):
        arrive(twin_in.at[hh, c], hh * chips + c, twin)
        acc[hh] = p_ref[hh, c, k].astype(jnp.float32) + twin_in[hh, c].astype(jnp.float32)
    yield
    for j in range(1, chips):
        cc = (c + j) % chips
        for hh in range(2):
            arrive(mate_in.at[cc, hh], 2 * chips + cc * 2 + hh, mates[j - 1])
            acc[hh] = acc[hh] + mate_in[cc, hh].astype(jnp.float32)
    far_out[...] = acc[1 - h].astype(far_out.dtype)
    send(far_out, far_in, 4 * chips, far)
    yield
    arrive(far_in, 4 * chips, far)
    o_ref[...] = acc[h] + far_in[...].astype(jnp.float32)
    for copy in sends:
        copy.wait_send()


def mp_sum_scratch(chips, rows, cols, dt):
    return [
        pltpu.VMEM((2, chips, rows, cols), dt),
        pltpu.VMEM((2, chips, rows, cols), dt),
        pltpu.VMEM((chips, 2, rows, cols), dt),
        pltpu.VMEM((rows, cols), dt),
        pltpu.VMEM((rows, cols), dt),
        pltpu.VMEM((2, rows, cols), jnp.float32),
        pltpu.SemaphoreType.DMA((4 * chips + 1,)),
        pltpu.SemaphoreType.DMA((4 * chips + 1,)),
    ]


def combined_kernel(parts, *refs):
    n_in = sum(p[2] for p in parts)
    n_out = sum(p[3] for p in parts)
    ins, outs, scratch = refs[:n_in], refs[n_in:n_in + n_out], refs[n_in + n_out:]
    barrier = pltpu.get_barrier_semaphore()
    total = 0
    for peers, _, _, _, _ in parts:
        for cond, axis, peer in peers():
            def signal(axis=axis, peer=peer):
                pl.semaphore_signal(barrier, inc=1, device_id={axis: peer}, device_id_type=MESH)
            if cond is None:
                signal()
                total = total + 1
            else:
                pl.when(cond)(signal)
                total = total + cond.astype(jnp.int32)
    pl.semaphore_wait(barrier, total)
    gens = []
    for _, body, pi, po, ps in parts:
        gens.append(body(ins[:pi], outs[:po], scratch[:ps]))
        ins, outs, scratch = ins[pi:], outs[po:], scratch[ps:]
    while gens:
        for gen in list(gens):
            try:
                next(gen)
            except StopIteration:
                gens.remove(gen)


def combined(parts, inputs, out_shapes, scratch_shapes, cid):
    return pl.pallas_call(
        functools.partial(combined_kernel, parts),
        out_shape=out_shapes,
        in_specs=[pl.BlockSpec(memory_space=pltpu.VMEM)] * len(inputs),
        out_specs=[pl.BlockSpec(memory_space=pltpu.VMEM)] * len(out_shapes),
        scratch_shapes=scratch_shapes,
        compiler_params=pltpu.CompilerParams(collective_id=cid, has_side_effects=True),
    )(*inputs)


def attend(normed, qkv_w, segment, table, mp_index):
    group_rows = normed.shape[0]
    heads_dev = qkv_w.shape[1] // (3 * HD)
    joined = jnp.dot(normed, qkv_w, preferred_element_type=jnp.float32).astype(jnp.bfloat16)
    joined = joined.reshape(group_rows, heads_dev, 3, HD)
    query = joined[:, :, 0]
    keys = joined[:, :, 1]
    vals = joined[:, :, 2]
    head_ids = mp_index * heads_dev + jnp.arange(heads_dev)
    slopes = jnp.exp2(-8.0 * (head_ids + 1).astype(jnp.float32) / H)
    positions = jnp.arange(group_rows)
    distance = (positions[:, None] - positions[None, :]).astype(jnp.float32)
    allowed = (segment[:, None] == segment[None, :]) & (distance >= 0)
    scores = jnp.einsum("thd,shd->hts", query, keys, preferred_element_type=jnp.float32) / jnp.sqrt(
        jnp.float32(HD)
    )
    scores = scores - slopes[:, None, None] * distance[None]
    scores = jnp.where(allowed[None], scores, -jnp.inf)
    probs = jax.nn.softmax(scores, axis=-1).astype(jnp.bfloat16)
    context = jnp.einsum("hts,shd->thd", probs, vals, preferred_element_type=jnp.float32).astype(
        jnp.bfloat16
    )
    context = context.reshape(group_rows, heads_dev * HD)
    key_vals = jnp.stack([keys, vals], 1)
    pages_here = group_rows // PAGE
    key_vals = key_vals.reshape(pages_here, PAGE, 2, heads_dev, HD).transpose(0, 2, 3, 1, 4)
    cache = jnp.zeros((pages_here, 2, heads_dev, PAGE, HD), jnp.bfloat16).at[table].set(key_vals)
    return (context, cache)


def local(hidden_in, segment_ids, page_table, qkv_master, up_master, dense_weight):
    mp_count = lax.axis_size("mp")
    dp_count = lax.axis_size("dp")
    mp_index = lax.axis_index("mp")
    chips = mp_count // 4
    lines = dp_count // RING
    rows = hidden_in.shape[0]
    rows_w = qkv_master.shape[0]
    bf = jnp.bfloat16
    qkv_t = qkv_master.astype(bf).reshape(rows_w, mp_count, -1).transpose(1, 0, 2)
    up_t = up_master.astype(bf).reshape(rows_w, mp_count, -1).transpose(1, 0, 2)
    normed_own = layer_norm(hidden_in.astype(jnp.float32)).astype(bf)
    sd = jax.ShapeDtypeStruct
    qkv_rows = sd((mp_count * rows_w, qkv_t.shape[-1]), bf)
    qkv_w, up_blk, normed = combined(
        [
            (
                functools.partial(weights_peers, mp_count, lines, RING),
                functools.partial(weights_body, mp_count, lines, RING),
                2, 2, 7,
            ),
            (functools.partial(mp_peers, chips), functools.partial(mp_gather_body, chips), 1, 1, 2),
        ],
        [qkv_t, up_t, normed_own],
        [
            sd((lines, RING) + qkv_rows.shape, bf),
            sd(up_t.shape, bf),
            sd((2, chips, 2) + normed_own.shape, bf),
        ],
        exchange_scratch(mp_count, 2)
        + [pltpu.VMEM(qkv_t.shape, bf), pltpu.VMEM(qkv_rows.shape, bf)]
        + dp_scratch(lines, RING)
        + mp_gather_scratch(chips),
        1,
    )
    normed = normed.reshape(mp_count * rows, -1)
    qkv_w = qkv_w.reshape(-1, qkv_t.shape[-1])
    up_piece = up_blk.reshape(mp_count * rows_w, -1)
    context, cache = attend(normed, qkv_w, segment_ids[0], page_table[0], mp_index)
    partial = jnp.dot(context, dense_weight, preferred_element_type=jnp.float32).astype(bf)
    cols = partial.shape[-1]
    hidden_out, normed_two, up_w = combined(
        [
            (functools.partial(tail_peers, chips), functools.partial(tail_body, chips), 2, 2, 12),
            (functools.partial(dp_peers, lines, RING), functools.partial(dp_gather_body, lines, RING), 1, 1, 2),
        ],
        [partial.reshape(2, chips, 2, rows, -1), hidden_in, up_piece],
        [
            sd((rows, cols), bf),
            sd((2, chips, 2, rows, cols), bf),
            sd((lines, RING) + up_piece.shape, bf),
        ],
        mp_sum_scratch(chips, rows, cols, bf)
        + [pltpu.VMEM((rows, cols), jnp.float32), pltpu.VMEM((rows, cols), bf)]
        + mp_gather_scratch(chips)
        + dp_scratch(lines, RING),
        2,
    )
    up_w = up_w.reshape(-1, up_piece.shape[-1])
    normed_two = normed_two.reshape(mp_count * rows, -1)
    upper = jnp.dot(normed_two, up_w, preferred_element_type=jnp.float32)
    activated = jax.nn.gelu(upper, approximate=True).astype(bf)
    return (hidden_out, activated, cache)


def solution(mesh):
    placed = (
        P(("dp", "mp"), None),
        P("dp", None),
        P("dp", None),
        P(("dp", "mp"), None),
        P(("dp", "mp"), None),
        P("mp", None),
    )
    return jax.shard_map(
        local,
        mesh=mesh,
        in_specs=placed,
        out_specs=(P(("dp", "mp"), None), P("dp", "mp"), P("dp", None, "mp", None, None)),
        check_vma=False,
    )
```

```python
import functools

import jax
import jax.numpy as jnp
from jax import lax
from jax.experimental import pallas as pl
from jax.experimental.pallas import tpu as pltpu
from jax.sharding import PartitionSpec as P

H = 16
HD = 128
PAGE = 128
RING = 4
MESH = pl.DeviceIdType.MESH


def layer_norm(values):
    mean_val = jnp.mean(values, -1, keepdims=True)
    centered = values - mean_val
    variance = jnp.mean(centered * centered, -1, keepdims=True)
    return centered * lax.rsqrt(variance + 1e-05)


def _remote(src, dst, send_sem, recv_sem, axis, peer):
    return pltpu.make_async_remote_copy(
        src_ref=src,
        dst_ref=dst,
        send_sem=send_sem,
        recv_sem=recv_sem,
        device_id={axis: peer},
        device_id_type=MESH,
    )


def mp_places(chips):
    me = lax.axis_index("mp")
    per_half = chips * 2
    h, c, k = me // per_half, (me // 2) % chips, me % 2
    far = (1 - h) * per_half + c * 2 + k
    twin = h * per_half + c * 2 + (1 - k)
    mates = [h * per_half + ((c + j) % chips) * 2 + k for j in range(1, chips)]
    return h, c, k, far, twin, mates


def exchange_peers(n, axis):
    me = lax.axis_index(axis)
    return [(None, axis, lax.rem(me + step, n)) for step in range(1, n)]


def exchange_body(n, axis, ins, outs, scratch):
    send_sem, recv_sem, local_sem = scratch
    me = lax.axis_index(axis)
    copies, locals_ = [], []
    for a in range(len(ins)):
        for step in range(1, n):
            peer = lax.rem(me + step, n)
            slot = a * (n - 1) + step - 1
            copy = _remote(ins[a].at[peer], outs[a].at[me], send_sem.at[slot], recv_sem.at[slot], axis, peer)
            copy.start()
            copies.append(copy)
        own = pltpu.make_async_copy(ins[a].at[me], outs[a].at[me], local_sem.at[a])
        own.start()
        locals_.append(own)
    yield
    for own in locals_:
        own.wait()
    for copy in copies:
        copy.wait()


def exchange_scratch(n, count):
    return [
        pltpu.SemaphoreType.DMA((count * (n - 1),)),
        pltpu.SemaphoreType.DMA((count * (n - 1),)),
        pltpu.SemaphoreType.DMA((count,)),
    ]


def dp_peers(lines, ring):
    me = lax.axis_index("dp")
    z, y = me // ring, me % ring
    out = [(z > 0, "dp", me - ring), (z < lines - 1, "dp", me + ring)]
    return out + [(None, "dp", z * ring + (y + k) % ring) for k in range(1, ring)]


def dp_gather_body(lines, ring, ins, outs, scratch):
    (x_ref,), (o_ref,), (send_sem, recv_sem) = ins, outs, scratch
    me = lax.axis_index("dp")
    z, y = me // ring, me % ring
    has_left, has_right = z > 0, z < lines - 1
    sends = []

    def send(cond, src, src_z, peer):
        slot = src_z * ring + y
        copy = _remote(src, o_ref.at[src_z, y], send_sem.at[len(sends)], recv_sem.at[slot], "dp", peer)
        pl.when(cond)(copy.start)
        sends.append((cond, copy))

    def spread(cond, src, src_z):
        for k in range(1, ring):
            send(cond, src, src_z, z * ring + (y + k) % ring)

    def arrive(cond, src_z, peer):
        slot = src_z * ring + y
        copy = _remote(o_ref.at[src_z, y], o_ref.at[src_z, y], send_sem.at[0], recv_sem.at[slot], "dp", peer)
        pl.when(cond)(copy.wait_recv)

    send(has_right, x_ref, z, me + ring)
    send(has_left, x_ref, z, me - ring)
    spread(z >= 0, x_ref, z)
    o_ref[z, y] = x_ref[...]
    yield
    for s in range(1, lines):
        from_left = z - s >= 0
        src_l = jnp.maximum(z - s, 0)
        arrive(from_left, src_l, me - ring)
        send(from_left & has_right, o_ref.at[src_l, y], src_l, me + ring)
        spread(from_left, o_ref.at[src_l, y], src_l)
        from_right = z + s <= lines - 1
        src_r = jnp.minimum(z + s, lines - 1)
        arrive(from_right, src_r, me + ring)
        send(from_right & has_left, o_ref.at[src_r, y], src_r, me - ring)
        spread(from_right, o_ref.at[src_r, y], src_r)
        yield
    for k in range(1, ring):
        yy = (y + k) % ring
        for zz in range(lines):
            slot = zz * ring + yy
            copy = _remote(o_ref.at[zz, yy], o_ref.at[zz, yy], send_sem.at[0], recv_sem.at[slot], "dp", z * ring + yy)
            copy.wait_recv()
    for cond, copy in sends:
        pl.when(cond)(copy.wait_send)


def dp_scratch(lines, ring):
    return [
        pltpu.SemaphoreType.DMA((1 + ring + (lines - 1) * 2 * ring,)),
        pltpu.SemaphoreType.DMA((lines * ring,)),
    ]


def dp_direct_peers(lines, ring):
    me = lax.axis_index("dp")
    z, y = me // ring, me % ring
    out = []
    for d in range(1, lines):
        out += [(z + d < lines, "dp", me + d * ring), (z - d >= 0, "dp", me - d * ring)]
    return out + [(None, "dp", z * ring + (y + k) % ring) for k in range(1, ring)]


def dp_direct_body(lines, ring, ins, outs, scratch):
    (x_ref,), (o_ref,), (send_sem, recv_sem) = ins, outs, scratch
    me = lax.axis_index("dp")
    z, y = me // ring, me % ring
    sends = []

    def send(cond, src, src_z, peer):
        slot = src_z * ring + y
        copy = _remote(src, o_ref.at[src_z, y], send_sem.at[len(sends)], recv_sem.at[slot], "dp", peer)
        pl.when(cond)(copy.start)
        sends.append((cond, copy))

    def spread(cond, src, src_z):
        for k in range(1, ring):
            send(cond, src, src_z, z * ring + (y + k) % ring)

    def arrive(cond, src_z, peer):
        slot = src_z * ring + y
        copy = _remote(o_ref.at[src_z, y], o_ref.at[src_z, y], send_sem.at[0], recv_sem.at[slot], "dp", peer)
        pl.when(cond)(copy.wait_recv)

    always = z >= 0
    spread(always, x_ref, z)
    for d in range(1, lines):
        send(z + d < lines, x_ref, z, me + d * ring)
        send(z - d >= 0, x_ref, z, me - d * ring)
    o_ref[z, y] = x_ref[...]
    yield
    for d in range(1, lines):
        for sign in (1, -1):
            cond = (z + sign * d < lines) & (z + sign * d >= 0)
            src_z = jnp.clip(z + sign * d, 0, lines - 1)
            arrive(cond, src_z, src_z * ring + y)
            spread(cond, o_ref.at[src_z, y], src_z)
        yield
    for k in range(1, ring):
        yy = (y + k) % ring
        for zz in range(lines):
            slot = zz * ring + yy
            copy = _remote(o_ref.at[zz, yy], o_ref.at[zz, yy], send_sem.at[0], recv_sem.at[slot], "dp", z * ring + yy)
            copy.wait_recv()
    for cond, copy in sends:
        pl.when(cond)(copy.wait_send)


def dp_direct_scratch(lines, ring):
    return [
        pltpu.SemaphoreType.DMA((ring - 1 + 2 * (lines - 1) * ring,)),
        pltpu.SemaphoreType.DMA((lines * ring,)),
    ]


def weights_peers(n, lines, ring):
    return exchange_peers(n, "mp") + dp_peers(lines, ring)


def weights_body(n, lines, ring, ins, outs, scratch):
    (qkv_t, up_t), (qkv_full, up_blk) = ins, outs
    ex_send, ex_recv, ex_local, qkv_blk, qkv_rows, dp_send, dp_recv = scratch
    yield from exchange_body(n, "mp", [qkv_t, up_t], [qkv_blk, up_blk], (ex_send, ex_recv, ex_local))
    per = qkv_blk.shape[1]
    for m in range(n):
        qkv_rows[m * per:(m + 1) * per, :] = qkv_blk[m]
    yield from dp_gather_body(lines, ring, [qkv_rows], [qkv_full], (dp_send, dp_recv))


def tail_peers(chips):
    return mp_peers(chips) + mp_peers(chips)


def tail_body(chips, ins, outs, scratch):
    (p_ref, h_ref), (hidden_ref, normed_ref) = ins, outs
    sum_scratch, (share, own), gather_scratch = scratch[:8], scratch[8:10], scratch[10:]
    yield from mp_sum_body(chips, [p_ref], [share], sum_scratch)
    stream = h_ref[...].astype(jnp.float32) + share[...]
    hidden_ref[...] = stream.astype(hidden_ref.dtype)
    own[...] = layer_norm(stream).astype(own.dtype)
    yield from mp_gather_body(chips, [own], [normed_ref], gather_scratch)


def normed_gather_body(chips, ins, outs, scratch):
    (h_ref,), (normed_ref,) = ins, outs
    own, gather_scratch = scratch[0], scratch[1:]
    own[...] = layer_norm(h_ref[...].astype(jnp.float32)).astype(own.dtype)
    yield from mp_gather_body(chips, [own], [normed_ref], gather_scratch)


def mp_peers(chips):
    _, _, _, far, twin, mates = mp_places(chips)
    return [(None, "mp", peer) for peer in [far, twin] + mates]


def mp_gather_body(chips, ins, outs, scratch):
    (x_ref,), (o_ref,), (send_sem, recv_sem) = ins, outs, scratch
    h, c, k, far, twin, mates = mp_places(chips)
    sends = []

    def send(src, hh, cc, kk, peer):
        slot = (hh * chips + cc) * 2 + kk
        copy = _remote(src, o_ref.at[hh, cc, kk], send_sem.at[len(sends)], recv_sem.at[slot], "mp", peer)
        copy.start()
        sends.append(copy)

    def arrive(hh, cc, kk, peer):
        slot = (hh * chips + cc) * 2 + kk
        copy = _remote(o_ref.at[hh, cc, kk], o_ref.at[hh, cc, kk], send_sem.at[0], recv_sem.at[slot], "mp", peer)
        copy.wait_recv()

    send(x_ref, h, c, k, far)
    for peer in mates:
        send(x_ref, h, c, k, peer)
    send(x_ref, h, c, k, twin)
    o_ref[h, c, k] = x_ref[...]
    yield
    arrive(1 - h, c, k, far)
    for peer in mates:
        send(o_ref.at[1 - h, c, k], 1 - h, c, k, peer)
    send(o_ref.at[1 - h, c, k], 1 - h, c, k, twin)
    yield
    for j in range(1, chips):
        cc = (c + j) % chips
        for hh in (h, 1 - h):
            arrive(hh, cc, k, mates[j - 1])
            send(o_ref.at[hh, cc, k], hh, cc, k, twin)
    yield
    for hh in range(2):
        for cc in range(chips):
            arrive(hh, cc, 1 - k, twin)
    for copy in sends:
        copy.wait_send()


def mp_gather_scratch(chips):
    return [pltpu.SemaphoreType.DMA((4 * chips,)), pltpu.SemaphoreType.DMA((4 * chips,))]


def mp_sum_body(chips, ins, outs, scratch):
    (p_ref,), (o_ref,) = ins, outs
    twin_in, pair, mate_in, far_out, far_in, acc, send_sem, recv_sem = scratch
    h, c, k, far, twin, mates = mp_places(chips)
    sends = []

    def send(src, dst, slot, peer):
        copy = _remote(src, dst, send_sem.at[len(sends)], recv_sem.at[slot], "mp", peer)
        copy.start()
        sends.append(copy)

    def arrive(dst, slot, peer):
        _remote(dst, dst, send_sem.at[0], recv_sem.at[slot], "mp", peer).wait_recv()

    for hh in range(2):
        for cc in range(chips):
            send(p_ref.at[hh, cc, 1 - k], twin_in.at[hh, cc], hh * chips + cc, twin)
    yield
    for j in range(1, chips):
        cc = (c + j) % chips
        for hh in range(2):
            arrive(twin_in.at[hh, cc], hh * chips + cc, twin)
            pair[hh, cc] = (
                p_ref[hh, cc, k].astype(jnp.float32) + twin_in[hh, cc].astype(jnp.float32)
            ).astype(pair.dtype)
            send(pair.at[hh, cc], mate_in.at[c, hh], 2 * chips + c * 2 + hh, mates[j - 1])
    for hh in range(2):
        arrive(twin_in.at[hh, c], hh * chips + c, twin)
        acc[hh] = p_ref[hh, c, k].astype(jnp.float32) + twin_in[hh, c].astype(jnp.float32)
    yield
    for j in range(1, chips):
        cc = (c + j) % chips
        for hh in range(2):
            arrive(mate_in.at[cc, hh], 2 * chips + cc * 2 + hh, mates[j - 1])
            acc[hh] = acc[hh] + mate_in[cc, hh].astype(jnp.float32)
    far_out[...] = acc[1 - h].astype(far_out.dtype)
    send(far_out, far_in, 4 * chips, far)
    yield
    arrive(far_in, 4 * chips, far)
    o_ref[...] = acc[h] + far_in[...].astype(jnp.float32)
    for copy in sends:
        copy.wait_send()


def mp_sum_scratch(chips, rows, cols, dt):
    return [
        pltpu.VMEM((2, chips, rows, cols), dt),
        pltpu.VMEM((2, chips, rows, cols), dt),
        pltpu.VMEM((chips, 2, rows, cols), dt),
        pltpu.VMEM((rows, cols), dt),
        pltpu.VMEM((rows, cols), dt),
        pltpu.VMEM((2, rows, cols), jnp.float32),
        pltpu.SemaphoreType.DMA((4 * chips + 1,)),
        pltpu.SemaphoreType.DMA((4 * chips + 1,)),
    ]


def combined_kernel(parts, *refs):
    n_in = sum(p[2] for p in parts)
    n_out = sum(p[3] for p in parts)
    ins, outs, scratch = refs[:n_in], refs[n_in:n_in + n_out], refs[n_in + n_out:]
    barrier = pltpu.get_barrier_semaphore()
    total = 0
    for peers, _, _, _, _ in parts:
        for cond, axis, peer in peers():
            def signal(axis=axis, peer=peer):
                pl.semaphore_signal(barrier, inc=1, device_id={axis: peer}, device_id_type=MESH)
            if cond is None:
                signal()
                total = total + 1
            else:
                pl.when(cond)(signal)
                total = total + cond.astype(jnp.int32)
    pl.semaphore_wait(barrier, total)
    gens = []
    for _, body, pi, po, ps in parts:
        gens.append(body(ins[:pi], outs[:po], scratch[:ps]))
        ins, outs, scratch = ins[pi:], outs[po:], scratch[ps:]
    while gens:
        for gen in list(gens):
            try:
                next(gen)
            except StopIteration:
                gens.remove(gen)


def combined(parts, inputs, out_shapes, scratch_shapes, cid):
    return pl.pallas_call(
        functools.partial(combined_kernel, parts),
        out_shape=out_shapes,
        in_specs=[pl.BlockSpec(memory_space=pltpu.VMEM)] * len(inputs),
        out_specs=[pl.BlockSpec(memory_space=pltpu.VMEM)] * len(out_shapes),
        scratch_shapes=scratch_shapes,
        compiler_params=pltpu.CompilerParams(collective_id=cid, has_side_effects=True),
    )(*inputs)


def attend(normed, qkv_w, segment, table, mp_index):
    group_rows = normed.shape[0]
    heads_dev = qkv_w.shape[1] // (3 * HD)
    joined = jnp.dot(normed, qkv_w, preferred_element_type=jnp.float32).astype(jnp.bfloat16)
    joined = joined.reshape(group_rows, heads_dev, 3, HD)
    query = joined[:, :, 0]
    keys = joined[:, :, 1]
    vals = joined[:, :, 2]
    head_ids = mp_index * heads_dev + jnp.arange(heads_dev)
    slopes = jnp.exp2(-8.0 * (head_ids + 1).astype(jnp.float32) / H)
    positions = jnp.arange(group_rows)
    distance = (positions[:, None] - positions[None, :]).astype(jnp.float32)
    allowed = (segment[:, None] == segment[None, :]) & (distance >= 0)
    scores = jnp.einsum("thd,shd->hts", query, keys, preferred_element_type=jnp.float32) / jnp.sqrt(
        jnp.float32(HD)
    )
    scores = scores - slopes[:, None, None] * distance[None]
    scores = jnp.where(allowed[None], scores, -jnp.inf)
    probs = jax.nn.softmax(scores, axis=-1).astype(jnp.bfloat16)
    context = jnp.einsum("hts,shd->thd", probs, vals, preferred_element_type=jnp.float32).astype(
        jnp.bfloat16
    )
    context = context.reshape(group_rows, heads_dev * HD)
    key_vals = jnp.stack([keys, vals], 1)
    pages_here = group_rows // PAGE
    key_vals = key_vals.reshape(pages_here, PAGE, 2, heads_dev, HD).transpose(0, 2, 3, 1, 4)
    cache = jnp.zeros((pages_here, 2, heads_dev, PAGE, HD), jnp.bfloat16).at[table].set(key_vals)
    return (context, cache)


def local(hidden_in, segment_ids, page_table, qkv_master, up_master, dense_weight):
    mp_count = lax.axis_size("mp")
    dp_count = lax.axis_size("dp")
    mp_index = lax.axis_index("mp")
    chips = mp_count // 4
    lines = dp_count // RING
    rows = hidden_in.shape[0]
    rows_w = qkv_master.shape[0]
    bf = jnp.bfloat16
    qkv_t = qkv_master.astype(bf).reshape(rows_w, mp_count, -1).transpose(1, 0, 2)
    up_t = up_master.astype(bf).reshape(rows_w, mp_count, -1).transpose(1, 0, 2)
    sd = jax.ShapeDtypeStruct
    qkv_rows = sd((mp_count * rows_w, qkv_t.shape[-1]), bf)
    qkv_w, up_blk, normed = combined(
        [
            (
                functools.partial(weights_peers, mp_count, lines, RING),
                functools.partial(weights_body, mp_count, lines, RING),
                2, 2, 7,
            ),
            (functools.partial(mp_peers, chips), functools.partial(normed_gather_body, chips), 1, 1, 3),
        ],
        [qkv_t, up_t, hidden_in],
        [
            sd((lines, RING) + qkv_rows.shape, bf),
            sd(up_t.shape, bf),
            sd((2, chips, 2) + hidden_in.shape, bf),
        ],
        exchange_scratch(mp_count, 2)
        + [pltpu.VMEM(qkv_t.shape, bf), pltpu.VMEM(qkv_rows.shape, bf)]
        + dp_scratch(lines, RING)
        + [pltpu.VMEM((rows, hidden_in.shape[-1]), bf)]
        + mp_gather_scratch(chips),
        1,
    )
    normed = normed.reshape(mp_count * rows, -1)
    qkv_w = qkv_w.reshape(-1, qkv_t.shape[-1])
    up_piece = up_blk.reshape(mp_count * rows_w, -1)
    context, cache = attend(normed, qkv_w, segment_ids[0], page_table[0], mp_index)
    partial = jnp.dot(context, dense_weight, preferred_element_type=jnp.float32).astype(bf)
    cols = partial.shape[-1]
    hidden_out, normed_two, up_w = combined(
        [
            (functools.partial(tail_peers, chips), functools.partial(tail_body, chips), 2, 2, 12),
            (functools.partial(dp_peers, lines, RING), functools.partial(dp_gather_body, lines, RING), 1, 1, 2),
        ],
        [partial.reshape(2, chips, 2, rows, -1), hidden_in, up_piece],
        [
            sd((rows, cols), bf),
            sd((2, chips, 2, rows, cols), bf),
            sd((lines, RING) + up_piece.shape, bf),
        ],
        mp_sum_scratch(chips, rows, cols, bf)
        + [pltpu.VMEM((rows, cols), jnp.float32), pltpu.VMEM((rows, cols), bf)]
        + mp_gather_scratch(chips)
        + dp_scratch(lines, RING),
        2,
    )
    up_w = up_w.reshape(-1, up_piece.shape[-1])
    normed_two = normed_two.reshape(mp_count * rows, -1)
    upper = jnp.dot(normed_two, up_w, preferred_element_type=jnp.float32)
    activated = jax.nn.gelu(upper, approximate=True).astype(bf)
    return (hidden_out, activated, cache)


def solution(mesh):
    placed = (
        P(("dp", "mp"), None),
        P("dp", None),
        P("dp", None),
        P(("dp", "mp"), None),
        P(("dp", "mp"), None),
        P("mp", None),
    )
    return jax.shard_map(
        local,
        mesh=mesh,
        in_specs=placed,
        out_specs=(P(("dp", "mp"), None), P("dp", "mp"), P("dp", None, "mp", None, None)),
        check_vma=False,
    )
```

```python
import functools

import jax
import jax.numpy as jnp
from jax import lax
from jax.experimental import pallas as pl
from jax.experimental.pallas import tpu as pltpu
from jax.sharding import PartitionSpec as P

H = 16
HD = 128
PAGE = 128
RING = 4
MESH = pl.DeviceIdType.MESH


def layer_norm(values):
    mean_val = jnp.mean(values, -1, keepdims=True)
    centered = values - mean_val
    variance = jnp.mean(centered * centered, -1, keepdims=True)
    return centered * lax.rsqrt(variance + 1e-05)


def _remote(src, dst, send_sem, recv_sem, axis, peer):
    return pltpu.make_async_remote_copy(
        src_ref=src,
        dst_ref=dst,
        send_sem=send_sem,
        recv_sem=recv_sem,
        device_id={axis: peer},
        device_id_type=MESH,
    )


def mp_places(chips):
    me = lax.axis_index("mp")
    per_half = chips * 2
    h, c, k = me // per_half, (me // 2) % chips, me % 2
    far = (1 - h) * per_half + c * 2 + k
    twin = h * per_half + c * 2 + (1 - k)
    mates = [h * per_half + ((c + j) % chips) * 2 + k for j in range(1, chips)]
    return h, c, k, far, twin, mates


def exchange_peers(n, axis):
    me = lax.axis_index(axis)
    return [(None, axis, lax.rem(me + step, n)) for step in range(1, n)]


def exchange_body(n, axis, ins, outs, scratch):
    send_sem, recv_sem, local_sem = scratch
    me = lax.axis_index(axis)
    copies, locals_ = [], []
    for a in range(len(ins)):
        for step in range(1, n):
            peer = lax.rem(me + step, n)
            slot = a * (n - 1) + step - 1
            copy = _remote(ins[a].at[peer], outs[a].at[me], send_sem.at[slot], recv_sem.at[slot], axis, peer)
            copy.start()
            copies.append(copy)
        own = pltpu.make_async_copy(ins[a].at[me], outs[a].at[me], local_sem.at[a])
        own.start()
        locals_.append(own)
    yield
    for own in locals_:
        own.wait()
    for copy in copies:
        copy.wait()


def exchange_scratch(n, count):
    return [
        pltpu.SemaphoreType.DMA((count * (n - 1),)),
        pltpu.SemaphoreType.DMA((count * (n - 1),)),
        pltpu.SemaphoreType.DMA((count,)),
    ]


def dp_peers(lines, ring):
    me = lax.axis_index("dp")
    z, y = me // ring, me % ring
    out = [(z > 0, "dp", me - ring), (z < lines - 1, "dp", me + ring)]
    return out + [(None, "dp", z * ring + (y + k) % ring) for k in range(1, ring)]


def dp_gather_body(lines, ring, ins, outs, scratch):
    (x_ref,), (o_ref,), (send_sem, recv_sem) = ins, outs, scratch
    me = lax.axis_index("dp")
    z, y = me // ring, me % ring
    has_left, has_right = z > 0, z < lines - 1
    sends = []

    def send(cond, src, src_z, peer):
        slot = src_z * ring + y
        copy = _remote(src, o_ref.at[src_z, y], send_sem.at[len(sends)], recv_sem.at[slot], "dp", peer)
        pl.when(cond)(copy.start)
        sends.append((cond, copy))

    def spread(cond, src, src_z):
        for k in range(1, ring):
            send(cond, src, src_z, z * ring + (y + k) % ring)

    def arrive(cond, src_z, peer):
        slot = src_z * ring + y
        copy = _remote(o_ref.at[src_z, y], o_ref.at[src_z, y], send_sem.at[0], recv_sem.at[slot], "dp", peer)
        pl.when(cond)(copy.wait_recv)

    send(has_right, x_ref, z, me + ring)
    send(has_left, x_ref, z, me - ring)
    spread(z >= 0, x_ref, z)
    o_ref[z, y] = x_ref[...]
    yield
    for s in range(1, lines):
        from_left = z - s >= 0
        src_l = jnp.maximum(z - s, 0)
        arrive(from_left, src_l, me - ring)
        send(from_left & has_right, o_ref.at[src_l, y], src_l, me + ring)
        spread(from_left, o_ref.at[src_l, y], src_l)
        from_right = z + s <= lines - 1
        src_r = jnp.minimum(z + s, lines - 1)
        arrive(from_right, src_r, me + ring)
        send(from_right & has_left, o_ref.at[src_r, y], src_r, me - ring)
        spread(from_right, o_ref.at[src_r, y], src_r)
        yield
    for k in range(1, ring):
        yy = (y + k) % ring
        for zz in range(lines):
            slot = zz * ring + yy
            copy = _remote(o_ref.at[zz, yy], o_ref.at[zz, yy], send_sem.at[0], recv_sem.at[slot], "dp", z * ring + yy)
            copy.wait_recv()
    for cond, copy in sends:
        pl.when(cond)(copy.wait_send)


def dp_scratch(lines, ring):
    return [
        pltpu.SemaphoreType.DMA((1 + ring + (lines - 1) * 2 * ring,)),
        pltpu.SemaphoreType.DMA((lines * ring,)),
    ]


def dp_direct_peers(lines, ring):
    me = lax.axis_index("dp")
    z, y = me // ring, me % ring
    out = []
    for d in range(1, lines):
        out += [(z + d < lines, "dp", me + d * ring), (z - d >= 0, "dp", me - d * ring)]
    return out + [(None, "dp", z * ring + (y + k) % ring) for k in range(1, ring)]


def dp_direct_body(lines, ring, ins, outs, scratch):
    (x_ref,), (o_ref,), (send_sem, recv_sem) = ins, outs, scratch
    me = lax.axis_index("dp")
    z, y = me // ring, me % ring
    sends = []

    def send(cond, src, src_z, peer):
        slot = src_z * ring + y
        copy = _remote(src, o_ref.at[src_z, y], send_sem.at[len(sends)], recv_sem.at[slot], "dp", peer)
        pl.when(cond)(copy.start)
        sends.append((cond, copy))

    def spread(cond, src, src_z):
        for k in range(1, ring):
            send(cond, src, src_z, z * ring + (y + k) % ring)

    def arrive(cond, src_z, peer):
        slot = src_z * ring + y
        copy = _remote(o_ref.at[src_z, y], o_ref.at[src_z, y], send_sem.at[0], recv_sem.at[slot], "dp", peer)
        pl.when(cond)(copy.wait_recv)

    always = z >= 0
    spread(always, x_ref, z)
    for d in range(1, lines):
        send(z + d < lines, x_ref, z, me + d * ring)
        send(z - d >= 0, x_ref, z, me - d * ring)
    o_ref[z, y] = x_ref[...]
    yield
    for d in range(1, lines):
        for sign in (1, -1):
            cond = (z + sign * d < lines) & (z + sign * d >= 0)
            src_z = jnp.clip(z + sign * d, 0, lines - 1)
            arrive(cond, src_z, src_z * ring + y)
            spread(cond, o_ref.at[src_z, y], src_z)
        yield
    for k in range(1, ring):
        yy = (y + k) % ring
        for zz in range(lines):
            slot = zz * ring + yy
            copy = _remote(o_ref.at[zz, yy], o_ref.at[zz, yy], send_sem.at[0], recv_sem.at[slot], "dp", z * ring + yy)
            copy.wait_recv()
    for cond, copy in sends:
        pl.when(cond)(copy.wait_send)


def dp_direct_scratch(lines, ring):
    return [
        pltpu.SemaphoreType.DMA((ring - 1 + 2 * (lines - 1) * ring,)),
        pltpu.SemaphoreType.DMA((lines * ring,)),
    ]


def weights_peers(n, lines, ring):
    return exchange_peers(n, "mp") + dp_peers(lines, ring)


def weights_body(n, lines, ring, ins, outs, scratch):
    (qkv_m, up_m), (qkv_full, up_blk) = ins, outs
    ex_send, ex_recv, ex_local, qkv_blk, qkv_rows, dp_send, dp_recv, qkv_t, up_t = scratch
    for master, cast in ((qkv_m, qkv_t), (up_m, up_t)):
        width = cast.shape[-1]
        for m in range(n):
            cast[m] = master[:, m * width:(m + 1) * width].astype(cast.dtype)
    yield from exchange_body(n, "mp", [qkv_t, up_t], [qkv_blk, up_blk], (ex_send, ex_recv, ex_local))
    per = qkv_blk.shape[1]
    for m in range(n):
        qkv_rows[m * per:(m + 1) * per, :] = qkv_blk[m]
    yield from dp_gather_body(lines, ring, [qkv_rows], [qkv_full], (dp_send, dp_recv))


def tail_peers(chips):
    return mp_peers(chips) + mp_peers(chips)


def tail_body(chips, ins, outs, scratch):
    (p_ref, h_ref), (hidden_ref, normed_ref) = ins, outs
    sum_scratch, (share, own), gather_scratch = scratch[:8], scratch[8:10], scratch[10:]
    yield from mp_sum_body(chips, [p_ref], [share], sum_scratch)
    stream = h_ref[...].astype(jnp.float32) + share[...]
    hidden_ref[...] = stream.astype(hidden_ref.dtype)
    own[...] = layer_norm(stream).astype(own.dtype)
    yield from mp_gather_body(chips, [own], [normed_ref], gather_scratch)


def normed_gather_body(chips, ins, outs, scratch):
    (h_ref,), (normed_ref,) = ins, outs
    own, gather_scratch = scratch[0], scratch[1:]
    own[...] = layer_norm(h_ref[...].astype(jnp.float32)).astype(own.dtype)
    yield from mp_gather_body(chips, [own], [normed_ref], gather_scratch)


def mp_peers(chips):
    _, _, _, far, twin, mates = mp_places(chips)
    return [(None, "mp", peer) for peer in [far, twin] + mates]


def mp_gather_body(chips, ins, outs, scratch):
    (x_ref,), (o_ref,), (send_sem, recv_sem) = ins, outs, scratch
    h, c, k, far, twin, mates = mp_places(chips)
    sends = []

    def send(src, hh, cc, kk, peer):
        slot = (hh * chips + cc) * 2 + kk
        copy = _remote(src, o_ref.at[hh, cc, kk], send_sem.at[len(sends)], recv_sem.at[slot], "mp", peer)
        copy.start()
        sends.append(copy)

    def arrive(hh, cc, kk, peer):
        slot = (hh * chips + cc) * 2 + kk
        copy = _remote(o_ref.at[hh, cc, kk], o_ref.at[hh, cc, kk], send_sem.at[0], recv_sem.at[slot], "mp", peer)
        copy.wait_recv()

    send(x_ref, h, c, k, far)
    for peer in mates:
        send(x_ref, h, c, k, peer)
    send(x_ref, h, c, k, twin)
    o_ref[h, c, k] = x_ref[...]
    yield
    arrive(1 - h, c, k, far)
    for peer in mates:
        send(o_ref.at[1 - h, c, k], 1 - h, c, k, peer)
    send(o_ref.at[1 - h, c, k], 1 - h, c, k, twin)
    yield
    for j in range(1, chips):
        cc = (c + j) % chips
        for hh in (h, 1 - h):
            arrive(hh, cc, k, mates[j - 1])
            send(o_ref.at[hh, cc, k], hh, cc, k, twin)
    yield
    for hh in range(2):
        for cc in range(chips):
            arrive(hh, cc, 1 - k, twin)
    for copy in sends:
        copy.wait_send()


def mp_gather_scratch(chips):
    return [pltpu.SemaphoreType.DMA((4 * chips,)), pltpu.SemaphoreType.DMA((4 * chips,))]


def mp_sum_body(chips, ins, outs, scratch):
    (p_ref,), (o_ref,) = ins, outs
    twin_in, pair, mate_in, far_out, far_in, acc, send_sem, recv_sem = scratch
    h, c, k, far, twin, mates = mp_places(chips)
    sends = []

    def send(src, dst, slot, peer):
        copy = _remote(src, dst, send_sem.at[len(sends)], recv_sem.at[slot], "mp", peer)
        copy.start()
        sends.append(copy)

    def arrive(dst, slot, peer):
        _remote(dst, dst, send_sem.at[0], recv_sem.at[slot], "mp", peer).wait_recv()

    for hh in range(2):
        for cc in range(chips):
            send(p_ref.at[hh, cc, 1 - k], twin_in.at[hh, cc], hh * chips + cc, twin)
    yield
    for j in range(1, chips):
        cc = (c + j) % chips
        for hh in range(2):
            arrive(twin_in.at[hh, cc], hh * chips + cc, twin)
            pair[hh, cc] = (
                p_ref[hh, cc, k].astype(jnp.float32) + twin_in[hh, cc].astype(jnp.float32)
            ).astype(pair.dtype)
            send(pair.at[hh, cc], mate_in.at[c, hh], 2 * chips + c * 2 + hh, mates[j - 1])
    for hh in range(2):
        arrive(twin_in.at[hh, c], hh * chips + c, twin)
        acc[hh] = p_ref[hh, c, k].astype(jnp.float32) + twin_in[hh, c].astype(jnp.float32)
    yield
    for j in range(1, chips):
        cc = (c + j) % chips
        for hh in range(2):
            arrive(mate_in.at[cc, hh], 2 * chips + cc * 2 + hh, mates[j - 1])
            acc[hh] = acc[hh] + mate_in[cc, hh].astype(jnp.float32)
    far_out[...] = acc[1 - h].astype(far_out.dtype)
    send(far_out, far_in, 4 * chips, far)
    yield
    arrive(far_in, 4 * chips, far)
    o_ref[...] = acc[h] + far_in[...].astype(jnp.float32)
    for copy in sends:
        copy.wait_send()


def mp_sum_scratch(chips, rows, cols, dt):
    return [
        pltpu.VMEM((2, chips, rows, cols), dt),
        pltpu.VMEM((2, chips, rows, cols), dt),
        pltpu.VMEM((chips, 2, rows, cols), dt),
        pltpu.VMEM((rows, cols), dt),
        pltpu.VMEM((rows, cols), dt),
        pltpu.VMEM((2, rows, cols), jnp.float32),
        pltpu.SemaphoreType.DMA((4 * chips + 1,)),
        pltpu.SemaphoreType.DMA((4 * chips + 1,)),
    ]


def combined_kernel(parts, *refs):
    n_in = sum(p[2] for p in parts)
    n_out = sum(p[3] for p in parts)
    ins, outs, scratch = refs[:n_in], refs[n_in:n_in + n_out], refs[n_in + n_out:]
    barrier = pltpu.get_barrier_semaphore()
    total = 0
    for peers, _, _, _, _ in parts:
        for cond, axis, peer in peers():
            def signal(axis=axis, peer=peer):
                pl.semaphore_signal(barrier, inc=1, device_id={axis: peer}, device_id_type=MESH)
            if cond is None:
                signal()
                total = total + 1
            else:
                pl.when(cond)(signal)
                total = total + cond.astype(jnp.int32)
    pl.semaphore_wait(barrier, total)
    gens = []
    for _, body, pi, po, ps in parts:
        gens.append(body(ins[:pi], outs[:po], scratch[:ps]))
        ins, outs, scratch = ins[pi:], outs[po:], scratch[ps:]
    while gens:
        for gen in list(gens):
            try:
                next(gen)
            except StopIteration:
                gens.remove(gen)


def combined(parts, inputs, out_shapes, scratch_shapes, cid):
    return pl.pallas_call(
        functools.partial(combined_kernel, parts),
        out_shape=out_shapes,
        in_specs=[pl.BlockSpec(memory_space=pltpu.VMEM)] * len(inputs),
        out_specs=[pl.BlockSpec(memory_space=pltpu.VMEM)] * len(out_shapes),
        scratch_shapes=scratch_shapes,
        compiler_params=pltpu.CompilerParams(collective_id=cid, has_side_effects=True),
    )(*inputs)


def attend(normed, qkv_w, segment, table, mp_index):
    group_rows = normed.shape[0]
    heads_dev = qkv_w.shape[1] // (3 * HD)
    joined = jnp.dot(normed, qkv_w, preferred_element_type=jnp.float32).astype(jnp.bfloat16)
    joined = joined.reshape(group_rows, heads_dev, 3, HD)
    query = joined[:, :, 0]
    keys = joined[:, :, 1]
    vals = joined[:, :, 2]
    head_ids = mp_index * heads_dev + jnp.arange(heads_dev)
    slopes = jnp.exp2(-8.0 * (head_ids + 1).astype(jnp.float32) / H)
    positions = jnp.arange(group_rows)
    distance = (positions[:, None] - positions[None, :]).astype(jnp.float32)
    allowed = (segment[:, None] == segment[None, :]) & (distance >= 0)
    scores = jnp.einsum("thd,shd->hts", query, keys, preferred_element_type=jnp.float32) / jnp.sqrt(
        jnp.float32(HD)
    )
    scores = scores - slopes[:, None, None] * distance[None]
    scores = jnp.where(allowed[None], scores, -jnp.inf)
    probs = jax.nn.softmax(scores, axis=-1).astype(jnp.bfloat16)
    context = jnp.einsum("hts,shd->thd", probs, vals, preferred_element_type=jnp.float32).astype(
        jnp.bfloat16
    )
    context = context.reshape(group_rows, heads_dev * HD)
    key_vals = jnp.stack([keys, vals], 1)
    pages_here = group_rows // PAGE
    key_vals = key_vals.reshape(pages_here, PAGE, 2, heads_dev, HD).transpose(0, 2, 3, 1, 4)
    cache = jnp.zeros((pages_here, 2, heads_dev, PAGE, HD), jnp.bfloat16).at[table].set(key_vals)
    return (context, cache)


def local(hidden_in, segment_ids, page_table, qkv_master, up_master, dense_weight):
    mp_count = lax.axis_size("mp")
    dp_count = lax.axis_size("dp")
    mp_index = lax.axis_index("mp")
    chips = mp_count // 4
    lines = dp_count // RING
    rows = hidden_in.shape[0]
    rows_w = qkv_master.shape[0]
    bf = jnp.bfloat16
    sd = jax.ShapeDtypeStruct
    qkv_t = sd((mp_count, rows_w, qkv_master.shape[-1] // mp_count), bf)
    up_t = sd((mp_count, rows_w, up_master.shape[-1] // mp_count), bf)
    qkv_rows = sd((mp_count * rows_w, qkv_t.shape[-1]), bf)
    qkv_w, up_blk, normed = combined(
        [
            (
                functools.partial(weights_peers, mp_count, lines, RING),
                functools.partial(weights_body, mp_count, lines, RING),
                2, 2, 9,
            ),
            (functools.partial(mp_peers, chips), functools.partial(normed_gather_body, chips), 1, 1, 3),
        ],
        [qkv_master, up_master, hidden_in],
        [
            sd((lines, RING) + qkv_rows.shape, bf),
            sd(up_t.shape, bf),
            sd((2, chips, 2) + hidden_in.shape, bf),
        ],
        exchange_scratch(mp_count, 2)
        + [pltpu.VMEM(qkv_t.shape, bf), pltpu.VMEM(qkv_rows.shape, bf)]
        + dp_scratch(lines, RING)
        + [pltpu.VMEM(qkv_t.shape, bf), pltpu.VMEM(up_t.shape, bf)]
        + [pltpu.VMEM((rows, hidden_in.shape[-1]), bf)]
        + mp_gather_scratch(chips),
        1,
    )
    normed = normed.reshape(mp_count * rows, -1)
    qkv_w = qkv_w.reshape(-1, qkv_t.shape[-1])
    up_piece = up_blk.reshape(mp_count * rows_w, -1)
    context, cache = attend(normed, qkv_w, segment_ids[0], page_table[0], mp_index)
    partial = jnp.dot(context, dense_weight, preferred_element_type=jnp.float32).astype(bf)
    cols = partial.shape[-1]
    hidden_out, normed_two, up_w = combined(
        [
            (functools.partial(tail_peers, chips), functools.partial(tail_body, chips), 2, 2, 12),
            (functools.partial(dp_peers, lines, RING), functools.partial(dp_gather_body, lines, RING), 1, 1, 2),
        ],
        [partial.reshape(2, chips, 2, rows, -1), hidden_in, up_piece],
        [
            sd((rows, cols), bf),
            sd((2, chips, 2, rows, cols), bf),
            sd((lines, RING) + up_piece.shape, bf),
        ],
        mp_sum_scratch(chips, rows, cols, bf)
        + [pltpu.VMEM((rows, cols), jnp.float32), pltpu.VMEM((rows, cols), bf)]
        + mp_gather_scratch(chips)
        + dp_scratch(lines, RING),
        2,
    )
    up_w = up_w.reshape(-1, up_piece.shape[-1])
    normed_two = normed_two.reshape(mp_count * rows, -1)
    upper = jnp.dot(normed_two, up_w, preferred_element_type=jnp.float32)
    activated = jax.nn.gelu(upper, approximate=True).astype(bf)
    return (hidden_out, activated, cache)


def solution(mesh):
    placed = (
        P(("dp", "mp"), None),
        P("dp", None),
        P("dp", None),
        P(("dp", "mp"), None),
        P(("dp", "mp"), None),
        P("mp", None),
    )
    return jax.shard_map(
        local,
        mesh=mesh,
        in_specs=placed,
        out_specs=(P(("dp", "mp"), None), P("dp", "mp"), P("dp", None, "mp", None, None)),
        check_vma=False,
    )
```

```python
import functools

import jax
import jax.numpy as jnp
from jax import lax
from jax.experimental import pallas as pl
from jax.experimental.pallas import tpu as pltpu
from jax.sharding import PartitionSpec as P

H = 16
HD = 128
PAGE = 128
RING = 4
MESH = pl.DeviceIdType.MESH


def layer_norm(values):
    mean_val = jnp.mean(values, -1, keepdims=True)
    centered = values - mean_val
    variance = jnp.mean(centered * centered, -1, keepdims=True)
    return centered * lax.rsqrt(variance + 1e-05)


def _remote(src, dst, send_sem, recv_sem, axis, peer):
    return pltpu.make_async_remote_copy(
        src_ref=src,
        dst_ref=dst,
        send_sem=send_sem,
        recv_sem=recv_sem,
        device_id={axis: peer},
        device_id_type=MESH,
    )


def mp_places(chips):
    me = lax.axis_index("mp")
    per_half = chips * 2
    h, c, k = me // per_half, (me // 2) % chips, me % 2
    far = (1 - h) * per_half + c * 2 + k
    twin = h * per_half + c * 2 + (1 - k)
    mates = [h * per_half + ((c + j) % chips) * 2 + k for j in range(1, chips)]
    return h, c, k, far, twin, mates


def exchange_peers(n, axis):
    me = lax.axis_index(axis)
    return [(None, axis, lax.rem(me + step, n)) for step in range(1, n)]


def exchange_body(n, axis, ins, outs, scratch):
    send_sem, recv_sem, local_sem = scratch
    me = lax.axis_index(axis)
    copies, locals_ = [], []
    for a in range(len(ins)):
        for step in range(1, n):
            peer = lax.rem(me + step, n)
            slot = a * (n - 1) + step - 1
            copy = _remote(ins[a].at[peer], outs[a].at[me], send_sem.at[slot], recv_sem.at[slot], axis, peer)
            copy.start()
            copies.append(copy)
        own = pltpu.make_async_copy(ins[a].at[me], outs[a].at[me], local_sem.at[a])
        own.start()
        locals_.append(own)
    yield
    for own in locals_:
        own.wait()
    for copy in copies:
        copy.wait()


def exchange_scratch(n, count):
    return [
        pltpu.SemaphoreType.DMA((count * (n - 1),)),
        pltpu.SemaphoreType.DMA((count * (n - 1),)),
        pltpu.SemaphoreType.DMA((count,)),
    ]


def dp_peers(lines, ring):
    me = lax.axis_index("dp")
    z, y = me // ring, me % ring
    out = [(z > 0, "dp", me - ring), (z < lines - 1, "dp", me + ring)]
    return out + [(None, "dp", z * ring + (y + k) % ring) for k in range(1, ring)]


def dp_gather_body(lines, ring, ins, outs, scratch):
    (x_ref,), (o_ref,), (send_sem, recv_sem) = ins, outs, scratch
    me = lax.axis_index("dp")
    z, y = me // ring, me % ring
    has_left, has_right = z > 0, z < lines - 1
    sends = []

    def send(cond, src, src_z, peer):
        slot = src_z * ring + y
        copy = _remote(src, o_ref.at[src_z, y], send_sem.at[len(sends)], recv_sem.at[slot], "dp", peer)
        pl.when(cond)(copy.start)
        sends.append((cond, copy))

    def spread(cond, src, src_z):
        for k in range(1, ring):
            send(cond, src, src_z, z * ring + (y + k) % ring)

    def arrive(cond, src_z, peer):
        slot = src_z * ring + y
        copy = _remote(o_ref.at[src_z, y], o_ref.at[src_z, y], send_sem.at[0], recv_sem.at[slot], "dp", peer)
        pl.when(cond)(copy.wait_recv)

    send(has_right, x_ref, z, me + ring)
    send(has_left, x_ref, z, me - ring)
    spread(z >= 0, x_ref, z)
    o_ref[z, y] = x_ref[...]
    yield
    for s in range(1, lines):
        from_left = z - s >= 0
        src_l = jnp.maximum(z - s, 0)
        arrive(from_left, src_l, me - ring)
        send(from_left & has_right, o_ref.at[src_l, y], src_l, me + ring)
        spread(from_left, o_ref.at[src_l, y], src_l)
        from_right = z + s <= lines - 1
        src_r = jnp.minimum(z + s, lines - 1)
        arrive(from_right, src_r, me + ring)
        send(from_right & has_left, o_ref.at[src_r, y], src_r, me - ring)
        spread(from_right, o_ref.at[src_r, y], src_r)
        yield
    for k in range(1, ring):
        yy = (y + k) % ring
        for zz in range(lines):
            slot = zz * ring + yy
            copy = _remote(o_ref.at[zz, yy], o_ref.at[zz, yy], send_sem.at[0], recv_sem.at[slot], "dp", z * ring + yy)
            copy.wait_recv()
    for cond, copy in sends:
        pl.when(cond)(copy.wait_send)


def dp_scratch(lines, ring):
    return [
        pltpu.SemaphoreType.DMA((1 + ring + (lines - 1) * 2 * ring,)),
        pltpu.SemaphoreType.DMA((lines * ring,)),
    ]


def dp_direct_peers(lines, ring):
    me = lax.axis_index("dp")
    z, y = me // ring, me % ring
    out = []
    for d in range(1, lines):
        out += [(z + d < lines, "dp", me + d * ring), (z - d >= 0, "dp", me - d * ring)]
    return out + [(None, "dp", z * ring + (y + k) % ring) for k in range(1, ring)]


def dp_direct_body(lines, ring, ins, outs, scratch):
    (x_ref,), (o_ref,), (send_sem, recv_sem) = ins, outs, scratch
    me = lax.axis_index("dp")
    z, y = me // ring, me % ring
    sends = []

    def send(cond, src, src_z, peer):
        slot = src_z * ring + y
        copy = _remote(src, o_ref.at[src_z, y], send_sem.at[len(sends)], recv_sem.at[slot], "dp", peer)
        pl.when(cond)(copy.start)
        sends.append((cond, copy))

    def spread(cond, src, src_z):
        for k in range(1, ring):
            send(cond, src, src_z, z * ring + (y + k) % ring)

    def arrive(cond, src_z, peer):
        slot = src_z * ring + y
        copy = _remote(o_ref.at[src_z, y], o_ref.at[src_z, y], send_sem.at[0], recv_sem.at[slot], "dp", peer)
        pl.when(cond)(copy.wait_recv)

    always = z >= 0
    spread(always, x_ref, z)
    for d in range(1, lines):
        send(z + d < lines, x_ref, z, me + d * ring)
        send(z - d >= 0, x_ref, z, me - d * ring)
    o_ref[z, y] = x_ref[...]
    yield
    for d in range(1, lines):
        for sign in (1, -1):
            cond = (z + sign * d < lines) & (z + sign * d >= 0)
            src_z = jnp.clip(z + sign * d, 0, lines - 1)
            arrive(cond, src_z, src_z * ring + y)
            spread(cond, o_ref.at[src_z, y], src_z)
        yield
    for k in range(1, ring):
        yy = (y + k) % ring
        for zz in range(lines):
            slot = zz * ring + yy
            copy = _remote(o_ref.at[zz, yy], o_ref.at[zz, yy], send_sem.at[0], recv_sem.at[slot], "dp", z * ring + yy)
            copy.wait_recv()
    for cond, copy in sends:
        pl.when(cond)(copy.wait_send)


def dp_direct_scratch(lines, ring):
    return [
        pltpu.SemaphoreType.DMA((ring - 1 + 2 * (lines - 1) * ring,)),
        pltpu.SemaphoreType.DMA((lines * ring,)),
    ]


def weights_peers(n, lines, ring):
    return exchange_peers(n, "mp") + dp_peers(lines, ring)


def weights_body(n, lines, ring, ins, outs, scratch):
    (qkv_m, up_m), (qkv_full, up_full) = ins, outs
    ex_send, ex_recv, ex_local, qkv_t, up_t, qkv_blk, up_blk, qkv_rows, up_rows = scratch[:9]
    dp_qkv, dp_up = scratch[9:11], scratch[11:13]
    for master, cast in ((qkv_m, qkv_t), (up_m, up_t)):
        width = cast.shape[-1]
        for m in range(n):
            cast[m] = master[:, m * width:(m + 1) * width].astype(cast.dtype)
    yield from exchange_body(n, "mp", [qkv_t, up_t], [qkv_blk, up_blk], (ex_send, ex_recv, ex_local))
    for blk, rows_buf in ((qkv_blk, qkv_rows), (up_blk, up_rows)):
        per = blk.shape[1]
        for m in range(n):
            rows_buf[m * per:(m + 1) * per, :] = blk[m]
    gens = [
        dp_gather_body(lines, ring, [qkv_rows], [qkv_full], dp_qkv),
        dp_gather_body(lines, ring, [up_rows], [up_full], dp_up),
    ]
    while gens:
        for gen in list(gens):
            try:
                next(gen)
            except StopIteration:
                gens.remove(gen)
        yield


def tail_peers(chips):
    return mp_peers(chips) + mp_peers(chips)


def tail_body(chips, ins, outs, scratch):
    (p_ref, h_ref), (hidden_ref, normed_ref) = ins, outs
    sum_scratch, (share, own), gather_scratch = scratch[:8], scratch[8:10], scratch[10:]
    yield from mp_sum_body(chips, [p_ref], [share], sum_scratch)
    stream = h_ref[...].astype(jnp.float32) + share[...]
    hidden_ref[...] = stream.astype(hidden_ref.dtype)
    own[...] = layer_norm(stream).astype(own.dtype)
    yield from mp_gather_body(chips, [own], [normed_ref], gather_scratch)


def normed_gather_body(chips, ins, outs, scratch):
    (h_ref,), (normed_ref,) = ins, outs
    own, gather_scratch = scratch[0], scratch[1:]
    own[...] = layer_norm(h_ref[...].astype(jnp.float32)).astype(own.dtype)
    yield from mp_gather_body(chips, [own], [normed_ref], gather_scratch)


def mp_peers(chips):
    _, _, _, far, twin, mates = mp_places(chips)
    return [(None, "mp", peer) for peer in [far, twin] + mates]


def mp_gather_body(chips, ins, outs, scratch):
    (x_ref,), (o_ref,), (send_sem, recv_sem) = ins, outs, scratch
    h, c, k, far, twin, mates = mp_places(chips)
    sends = []

    def send(src, hh, cc, kk, peer):
        slot = (hh * chips + cc) * 2 + kk
        copy = _remote(src, o_ref.at[hh, cc, kk], send_sem.at[len(sends)], recv_sem.at[slot], "mp", peer)
        copy.start()
        sends.append(copy)

    def arrive(hh, cc, kk, peer):
        slot = (hh * chips + cc) * 2 + kk
        copy = _remote(o_ref.at[hh, cc, kk], o_ref.at[hh, cc, kk], send_sem.at[0], recv_sem.at[slot], "mp", peer)
        copy.wait_recv()

    send(x_ref, h, c, k, far)
    for peer in mates:
        send(x_ref, h, c, k, peer)
    send(x_ref, h, c, k, twin)
    o_ref[h, c, k] = x_ref[...]
    yield
    arrive(1 - h, c, k, far)
    for peer in mates:
        send(o_ref.at[1 - h, c, k], 1 - h, c, k, peer)
    send(o_ref.at[1 - h, c, k], 1 - h, c, k, twin)
    yield
    for j in range(1, chips):
        cc = (c + j) % chips
        for hh in (h, 1 - h):
            arrive(hh, cc, k, mates[j - 1])
            send(o_ref.at[hh, cc, k], hh, cc, k, twin)
    yield
    for hh in range(2):
        for cc in range(chips):
            arrive(hh, cc, 1 - k, twin)
    for copy in sends:
        copy.wait_send()


def mp_gather_scratch(chips):
    return [pltpu.SemaphoreType.DMA((4 * chips,)), pltpu.SemaphoreType.DMA((4 * chips,))]


def mp_sum_body(chips, ins, outs, scratch):
    (p_ref,), (o_ref,) = ins, outs
    twin_in, pair, mate_in, far_out, far_in, acc, send_sem, recv_sem = scratch
    h, c, k, far, twin, mates = mp_places(chips)
    sends = []

    def send(src, dst, slot, peer):
        copy = _remote(src, dst, send_sem.at[len(sends)], recv_sem.at[slot], "mp", peer)
        copy.start()
        sends.append(copy)

    def arrive(dst, slot, peer):
        _remote(dst, dst, send_sem.at[0], recv_sem.at[slot], "mp", peer).wait_recv()

    for hh in range(2):
        for cc in range(chips):
            send(p_ref.at[hh, cc, 1 - k], twin_in.at[hh, cc], hh * chips + cc, twin)
    yield
    for j in range(1, chips):
        cc = (c + j) % chips
        for hh in range(2):
            arrive(twin_in.at[hh, cc], hh * chips + cc, twin)
            pair[hh, cc] = (
                p_ref[hh, cc, k].astype(jnp.float32) + twin_in[hh, cc].astype(jnp.float32)
            ).astype(pair.dtype)
            send(pair.at[hh, cc], mate_in.at[c, hh], 2 * chips + c * 2 + hh, mates[j - 1])
    for hh in range(2):
        arrive(twin_in.at[hh, c], hh * chips + c, twin)
        acc[hh] = p_ref[hh, c, k].astype(jnp.float32) + twin_in[hh, c].astype(jnp.float32)
    yield
    for j in range(1, chips):
        cc = (c + j) % chips
        for hh in range(2):
            arrive(mate_in.at[cc, hh], 2 * chips + cc * 2 + hh, mates[j - 1])
            acc[hh] = acc[hh] + mate_in[cc, hh].astype(jnp.float32)
    far_out[...] = acc[1 - h].astype(far_out.dtype)
    send(far_out, far_in, 4 * chips, far)
    yield
    arrive(far_in, 4 * chips, far)
    o_ref[...] = acc[h] + far_in[...].astype(jnp.float32)
    for copy in sends:
        copy.wait_send()


def mp_sum_scratch(chips, rows, cols, dt):
    return [
        pltpu.VMEM((2, chips, rows, cols), dt),
        pltpu.VMEM((2, chips, rows, cols), dt),
        pltpu.VMEM((chips, 2, rows, cols), dt),
        pltpu.VMEM((rows, cols), dt),
        pltpu.VMEM((rows, cols), dt),
        pltpu.VMEM((2, rows, cols), jnp.float32),
        pltpu.SemaphoreType.DMA((4 * chips + 1,)),
        pltpu.SemaphoreType.DMA((4 * chips + 1,)),
    ]


def combined_kernel(parts, *refs):
    n_in = sum(p[2] for p in parts)
    n_out = sum(p[3] for p in parts)
    ins, outs, scratch = refs[:n_in], refs[n_in:n_in + n_out], refs[n_in + n_out:]
    barrier = pltpu.get_barrier_semaphore()
    total = 0
    for peers, _, _, _, _ in parts:
        for cond, axis, peer in peers():
            def signal(axis=axis, peer=peer):
                pl.semaphore_signal(barrier, inc=1, device_id={axis: peer}, device_id_type=MESH)
            if cond is None:
                signal()
                total = total + 1
            else:
                pl.when(cond)(signal)
                total = total + cond.astype(jnp.int32)
    pl.semaphore_wait(barrier, total)
    gens = []
    for _, body, pi, po, ps in parts:
        gens.append(body(ins[:pi], outs[:po], scratch[:ps]))
        ins, outs, scratch = ins[pi:], outs[po:], scratch[ps:]
    while gens:
        for gen in list(gens):
            try:
                next(gen)
            except StopIteration:
                gens.remove(gen)


def combined(parts, inputs, out_shapes, scratch_shapes, cid):
    return pl.pallas_call(
        functools.partial(combined_kernel, parts),
        out_shape=out_shapes,
        in_specs=[pl.BlockSpec(memory_space=pltpu.VMEM)] * len(inputs),
        out_specs=[pl.BlockSpec(memory_space=pltpu.VMEM)] * len(out_shapes),
        scratch_shapes=scratch_shapes,
        compiler_params=pltpu.CompilerParams(collective_id=cid, has_side_effects=True),
    )(*inputs)


def attend(normed, qkv_w, segment, table, mp_index):
    group_rows = normed.shape[0]
    heads_dev = qkv_w.shape[1] // (3 * HD)
    joined = jnp.dot(normed, qkv_w, preferred_element_type=jnp.float32).astype(jnp.bfloat16)
    joined = joined.reshape(group_rows, heads_dev, 3, HD)
    query = joined[:, :, 0]
    keys = joined[:, :, 1]
    vals = joined[:, :, 2]
    head_ids = mp_index * heads_dev + jnp.arange(heads_dev)
    slopes = jnp.exp2(-8.0 * (head_ids + 1).astype(jnp.float32) / H)
    positions = jnp.arange(group_rows)
    distance = (positions[:, None] - positions[None, :]).astype(jnp.float32)
    allowed = (segment[:, None] == segment[None, :]) & (distance >= 0)
    scores = jnp.einsum("thd,shd->hts", query, keys, preferred_element_type=jnp.float32) / jnp.sqrt(
        jnp.float32(HD)
    )
    scores = scores - slopes[:, None, None] * distance[None]
    scores = jnp.where(allowed[None], scores, -jnp.inf)
    probs = jax.nn.softmax(scores, axis=-1).astype(jnp.bfloat16)
    context = jnp.einsum("hts,shd->thd", probs, vals, preferred_element_type=jnp.float32).astype(
        jnp.bfloat16
    )
    context = context.reshape(group_rows, heads_dev * HD)
    key_vals = jnp.stack([keys, vals], 1)
    pages_here = group_rows // PAGE
    key_vals = key_vals.reshape(pages_here, PAGE, 2, heads_dev, HD).transpose(0, 2, 3, 1, 4)
    cache = jnp.zeros((pages_here, 2, heads_dev, PAGE, HD), jnp.bfloat16).at[table].set(key_vals)
    return (context, cache)


def local(hidden_in, segment_ids, page_table, qkv_master, up_master, dense_weight):
    mp_count = lax.axis_size("mp")
    dp_count = lax.axis_size("dp")
    mp_index = lax.axis_index("mp")
    chips = mp_count // 4
    lines = dp_count // RING
    rows = hidden_in.shape[0]
    rows_w = qkv_master.shape[0]
    bf = jnp.bfloat16
    sd = jax.ShapeDtypeStruct
    qkv_t = sd((mp_count, rows_w, qkv_master.shape[-1] // mp_count), bf)
    up_t = sd((mp_count, rows_w, up_master.shape[-1] // mp_count), bf)
    qkv_rows = sd((mp_count * rows_w, qkv_t.shape[-1]), bf)
    up_rows = sd((mp_count * rows_w, up_t.shape[-1]), bf)
    qkv_w, up_w, normed = combined(
        [
            (
                functools.partial(weights_peers, mp_count, lines, RING),
                functools.partial(weights_body, mp_count, lines, RING),
                2, 2, 13,
            ),
            (functools.partial(mp_peers, chips), functools.partial(normed_gather_body, chips), 1, 1, 3),
        ],
        [qkv_master, up_master, hidden_in],
        [
            sd((lines, RING) + qkv_rows.shape, bf),
            sd((lines, RING) + up_rows.shape, bf),
            sd((2, chips, 2) + hidden_in.shape, bf),
        ],
        exchange_scratch(mp_count, 2)
        + [pltpu.VMEM(x.shape, bf) for x in (qkv_t, up_t, qkv_t, up_t, qkv_rows, up_rows)]
        + dp_scratch(lines, RING)
        + dp_scratch(lines, RING)
        + [pltpu.VMEM((rows, hidden_in.shape[-1]), bf)]
        + mp_gather_scratch(chips),
        1,
    )
    normed = normed.reshape(mp_count * rows, -1)
    qkv_w = qkv_w.reshape(-1, qkv_t.shape[-1])
    up_w = up_w.reshape(-1, up_t.shape[-1])
    context, cache = attend(normed, qkv_w, segment_ids[0], page_table[0], mp_index)
    partial = jnp.dot(context, dense_weight, preferred_element_type=jnp.float32).astype(bf)
    cols = partial.shape[-1]
    hidden_out, normed_two = combined(
        [(functools.partial(tail_peers, chips), functools.partial(tail_body, chips), 2, 2, 12)],
        [partial.reshape(2, chips, 2, rows, -1), hidden_in],
        [sd((rows, cols), bf), sd((2, chips, 2, rows, cols), bf)],
        mp_sum_scratch(chips, rows, cols, bf)
        + [pltpu.VMEM((rows, cols), jnp.float32), pltpu.VMEM((rows, cols), bf)]
        + mp_gather_scratch(chips),
        2,
    )
    normed_two = normed_two.reshape(mp_count * rows, -1)
    upper = jnp.dot(normed_two, up_w, preferred_element_type=jnp.float32)
    activated = jax.nn.gelu(upper, approximate=True).astype(bf)
    return (hidden_out, activated, cache)


def solution(mesh):
    placed = (
        P(("dp", "mp"), None),
        P("dp", None),
        P("dp", None),
        P(("dp", "mp"), None),
        P(("dp", "mp"), None),
        P("mp", None),
    )
    return jax.shard_map(
        local,
        mesh=mesh,
        in_specs=placed,
        out_specs=(P(("dp", "mp"), None), P("dp", "mp"), P("dp", None, "mp", None, None)),
        check_vma=False,
    )
```

```python
import functools

import jax
import jax.numpy as jnp
from jax import lax
from jax.experimental import pallas as pl
from jax.experimental.pallas import tpu as pltpu
from jax.sharding import PartitionSpec as P

H = 16
HD = 128
PAGE = 128
RING = 4
MESH = pl.DeviceIdType.MESH


def layer_norm(values):
    mean_val = jnp.mean(values, -1, keepdims=True)
    centered = values - mean_val
    variance = jnp.mean(centered * centered, -1, keepdims=True)
    return centered * lax.rsqrt(variance + 1e-05)


def _remote(src, dst, send_sem, recv_sem, axis, peer):
    return pltpu.make_async_remote_copy(
        src_ref=src,
        dst_ref=dst,
        send_sem=send_sem,
        recv_sem=recv_sem,
        device_id={axis: peer},
        device_id_type=MESH,
    )


def mp_places(chips):
    me = lax.axis_index("mp")
    per_half = chips * 2
    h, c, k = me // per_half, (me // 2) % chips, me % 2
    far = (1 - h) * per_half + c * 2 + k
    twin = h * per_half + c * 2 + (1 - k)
    mates = [h * per_half + ((c + j) % chips) * 2 + k for j in range(1, chips)]
    return h, c, k, far, twin, mates


def exchange_peers(n, axis):
    me = lax.axis_index(axis)
    return [(None, axis, lax.rem(me + step, n)) for step in range(1, n)]


def exchange_body(n, axis, ins, outs, scratch):
    send_sem, recv_sem, local_sem = scratch
    me = lax.axis_index(axis)
    copies, locals_ = [], []
    for a in range(len(ins)):
        for step in range(1, n):
            peer = lax.rem(me + step, n)
            slot = a * (n - 1) + step - 1
            copy = _remote(ins[a].at[peer], outs[a].at[me], send_sem.at[slot], recv_sem.at[slot], axis, peer)
            copy.start()
            copies.append(copy)
        own = pltpu.make_async_copy(ins[a].at[me], outs[a].at[me], local_sem.at[a])
        own.start()
        locals_.append(own)
    yield
    for own in locals_:
        own.wait()
    for copy in copies:
        copy.wait()


def exchange_scratch(n, count):
    return [
        pltpu.SemaphoreType.DMA((count * (n - 1),)),
        pltpu.SemaphoreType.DMA((count * (n - 1),)),
        pltpu.SemaphoreType.DMA((count,)),
    ]


def dp_peers(lines, ring):
    me = lax.axis_index("dp")
    z, y = me // ring, me % ring
    out = [(z > 0, "dp", me - ring), (z < lines - 1, "dp", me + ring)]
    return out + [(None, "dp", z * ring + (y + k) % ring) for k in range(1, ring)]


def dp_gather_body(lines, ring, ins, outs, scratch):
    (x_ref,), (o_ref,), (send_sem, recv_sem) = ins, outs, scratch
    me = lax.axis_index("dp")
    z, y = me // ring, me % ring
    has_left, has_right = z > 0, z < lines - 1
    sends = []

    def send(cond, src, src_z, peer):
        slot = src_z * ring + y
        copy = _remote(src, o_ref.at[src_z, y], send_sem.at[len(sends)], recv_sem.at[slot], "dp", peer)
        pl.when(cond)(copy.start)
        sends.append((cond, copy))

    def spread(cond, src, src_z):
        for k in range(1, ring):
            send(cond, src, src_z, z * ring + (y + k) % ring)

    def arrive(cond, src_z, peer):
        slot = src_z * ring + y
        copy = _remote(o_ref.at[src_z, y], o_ref.at[src_z, y], send_sem.at[0], recv_sem.at[slot], "dp", peer)
        pl.when(cond)(copy.wait_recv)

    send(has_right, x_ref, z, me + ring)
    send(has_left, x_ref, z, me - ring)
    spread(z >= 0, x_ref, z)
    o_ref[z, y] = x_ref[...]
    yield
    for s in range(1, lines):
        from_left = z - s >= 0
        src_l = jnp.maximum(z - s, 0)
        arrive(from_left, src_l, me - ring)
        send(from_left & has_right, o_ref.at[src_l, y], src_l, me + ring)
        spread(from_left, o_ref.at[src_l, y], src_l)
        from_right = z + s <= lines - 1
        src_r = jnp.minimum(z + s, lines - 1)
        arrive(from_right, src_r, me + ring)
        send(from_right & has_left, o_ref.at[src_r, y], src_r, me - ring)
        spread(from_right, o_ref.at[src_r, y], src_r)
        yield
    for k in range(1, ring):
        yy = (y + k) % ring
        for zz in range(lines):
            slot = zz * ring + yy
            copy = _remote(o_ref.at[zz, yy], o_ref.at[zz, yy], send_sem.at[0], recv_sem.at[slot], "dp", z * ring + yy)
            copy.wait_recv()
    for cond, copy in sends:
        pl.when(cond)(copy.wait_send)


def dp_scratch(lines, ring):
    return [
        pltpu.SemaphoreType.DMA((1 + ring + (lines - 1) * 2 * ring,)),
        pltpu.SemaphoreType.DMA((lines * ring,)),
    ]


def dp_direct_peers(lines, ring):
    me = lax.axis_index("dp")
    z, y = me // ring, me % ring
    out = []
    for d in range(1, lines):
        out += [(z + d < lines, "dp", me + d * ring), (z - d >= 0, "dp", me - d * ring)]
    return out + [(None, "dp", z * ring + (y + k) % ring) for k in range(1, ring)]


def dp_direct_body(lines, ring, ins, outs, scratch):
    (x_ref,), (o_ref,), (send_sem, recv_sem) = ins, outs, scratch
    me = lax.axis_index("dp")
    z, y = me // ring, me % ring
    sends = []

    def send(cond, src, src_z, peer):
        slot = src_z * ring + y
        copy = _remote(src, o_ref.at[src_z, y], send_sem.at[len(sends)], recv_sem.at[slot], "dp", peer)
        pl.when(cond)(copy.start)
        sends.append((cond, copy))

    def spread(cond, src, src_z):
        for k in range(1, ring):
            send(cond, src, src_z, z * ring + (y + k) % ring)

    def arrive(cond, src_z, peer):
        slot = src_z * ring + y
        copy = _remote(o_ref.at[src_z, y], o_ref.at[src_z, y], send_sem.at[0], recv_sem.at[slot], "dp", peer)
        pl.when(cond)(copy.wait_recv)

    always = z >= 0
    spread(always, x_ref, z)
    for d in range(1, lines):
        send(z + d < lines, x_ref, z, me + d * ring)
        send(z - d >= 0, x_ref, z, me - d * ring)
    o_ref[z, y] = x_ref[...]
    yield
    for d in range(1, lines):
        for sign in (1, -1):
            cond = (z + sign * d < lines) & (z + sign * d >= 0)
            src_z = jnp.clip(z + sign * d, 0, lines - 1)
            arrive(cond, src_z, src_z * ring + y)
            spread(cond, o_ref.at[src_z, y], src_z)
        yield
    for k in range(1, ring):
        yy = (y + k) % ring
        for zz in range(lines):
            slot = zz * ring + yy
            copy = _remote(o_ref.at[zz, yy], o_ref.at[zz, yy], send_sem.at[0], recv_sem.at[slot], "dp", z * ring + yy)
            copy.wait_recv()
    for cond, copy in sends:
        pl.when(cond)(copy.wait_send)


def dp_direct_scratch(lines, ring):
    return [
        pltpu.SemaphoreType.DMA((ring - 1 + 2 * (lines - 1) * ring,)),
        pltpu.SemaphoreType.DMA((lines * ring,)),
    ]


def weights_peers(n, lines, ring):
    return exchange_peers(n, "mp") + dp_peers(lines, ring)


def weights_body(n, lines, ring, ins, outs, scratch):
    (qkv_m, up_m), (qkv_full, up_blk) = ins, outs
    ex_send, ex_recv, ex_local, qkv_blk, qkv_rows, dp_send, dp_recv, qkv_t, up_t = scratch
    for master, cast in ((qkv_m, qkv_t), (up_m, up_t)):
        width = cast.shape[-1]
        for m in range(n):
            cast[m] = master[:, m * width:(m + 1) * width].astype(cast.dtype)
    yield from exchange_body(n, "mp", [qkv_t, up_t], [qkv_blk, up_blk], (ex_send, ex_recv, ex_local))
    per = qkv_blk.shape[1]
    for m in range(n):
        qkv_rows[m * per:(m + 1) * per, :] = qkv_blk[m]
    yield from dp_gather_body(lines, ring, [qkv_rows], [qkv_full], (dp_send, dp_recv))


def tail_peers(chips):
    return mp_peers(chips) + mp_peers(chips)


def tail_body(chips, ins, outs, scratch):
    (p_ref, h_ref), (hidden_ref, normed_ref) = ins, outs
    sum_scratch, (share, own), gather_scratch = scratch[:8], scratch[8:10], scratch[10:]
    yield from mp_sum_body(chips, [p_ref], [share], sum_scratch)
    stream = h_ref[...].astype(jnp.float32) + share[...]
    hidden_ref[...] = stream.astype(hidden_ref.dtype)
    own[...] = layer_norm(stream).astype(own.dtype)
    yield from mp_gather_body(chips, [own], [normed_ref], gather_scratch)


def normed_gather_body(chips, ins, outs, scratch):
    (h_ref,), (normed_ref,) = ins, outs
    own, gather_scratch = scratch[0], scratch[1:]
    own[...] = layer_norm(h_ref[...].astype(jnp.float32)).astype(own.dtype)
    yield from mp_gather_body(chips, [own], [normed_ref], gather_scratch)


def mp_peers(chips):
    _, _, _, far, twin, mates = mp_places(chips)
    return [(None, "mp", peer) for peer in [far, twin] + mates]


def mp_gather_body(chips, ins, outs, scratch):
    (x_ref,), (o_ref,), (send_sem, recv_sem) = ins, outs, scratch
    h, c, k, far, twin, mates = mp_places(chips)
    sends = []

    def send(src, hh, cc, kk, peer):
        slot = (hh * chips + cc) * 2 + kk
        copy = _remote(src, o_ref.at[hh, cc, kk], send_sem.at[len(sends)], recv_sem.at[slot], "mp", peer)
        copy.start()
        sends.append(copy)

    def arrive(hh, cc, kk, peer):
        slot = (hh * chips + cc) * 2 + kk
        copy = _remote(o_ref.at[hh, cc, kk], o_ref.at[hh, cc, kk], send_sem.at[0], recv_sem.at[slot], "mp", peer)
        copy.wait_recv()

    send(x_ref, h, c, k, far)
    for peer in mates:
        send(x_ref, h, c, k, peer)
    send(x_ref, h, c, k, twin)
    o_ref[h, c, k] = x_ref[...]
    yield
    arrive(1 - h, c, k, far)
    for peer in mates:
        send(o_ref.at[1 - h, c, k], 1 - h, c, k, peer)
    send(o_ref.at[1 - h, c, k], 1 - h, c, k, twin)
    yield
    for j in range(1, chips):
        cc = (c + j) % chips
        for hh in (h, 1 - h):
            arrive(hh, cc, k, mates[j - 1])
            send(o_ref.at[hh, cc, k], hh, cc, k, twin)
    yield
    for hh in range(2):
        for cc in range(chips):
            arrive(hh, cc, 1 - k, twin)
    for copy in sends:
        copy.wait_send()


def mp_gather_scratch(chips):
    return [pltpu.SemaphoreType.DMA((4 * chips,)), pltpu.SemaphoreType.DMA((4 * chips,))]


def mp_sum_body(chips, ins, outs, scratch):
    (p_ref,), (o_ref,) = ins, outs
    twin_in, pair, mate_in, far_out, far_in, acc, send_sem, recv_sem = scratch
    h, c, k, far, twin, mates = mp_places(chips)
    sends = []

    def send(src, dst, slot, peer):
        copy = _remote(src, dst, send_sem.at[len(sends)], recv_sem.at[slot], "mp", peer)
        copy.start()
        sends.append(copy)

    def arrive(dst, slot, peer):
        _remote(dst, dst, send_sem.at[0], recv_sem.at[slot], "mp", peer).wait_recv()

    for hh in range(2):
        for cc in range(chips):
            send(p_ref.at[hh, cc, 1 - k], twin_in.at[hh, cc], hh * chips + cc, twin)
    yield
    for j in range(1, chips):
        cc = (c + j) % chips
        for hh in range(2):
            arrive(twin_in.at[hh, cc], hh * chips + cc, twin)
            pair[hh, cc] = (
                p_ref[hh, cc, k].astype(jnp.float32) + twin_in[hh, cc].astype(jnp.float32)
            ).astype(pair.dtype)
            send(pair.at[hh, cc], mate_in.at[c, hh], 2 * chips + c * 2 + hh, mates[j - 1])
    for hh in range(2):
        arrive(twin_in.at[hh, c], hh * chips + c, twin)
        acc[hh] = p_ref[hh, c, k].astype(jnp.float32) + twin_in[hh, c].astype(jnp.float32)
    yield
    for j in range(1, chips):
        cc = (c + j) % chips
        for hh in range(2):
            arrive(mate_in.at[cc, hh], 2 * chips + cc * 2 + hh, mates[j - 1])
            acc[hh] = acc[hh] + mate_in[cc, hh].astype(jnp.float32)
    far_out[...] = acc[1 - h].astype(far_out.dtype)
    send(far_out, far_in, 4 * chips, far)
    yield
    arrive(far_in, 4 * chips, far)
    o_ref[...] = acc[h] + far_in[...].astype(jnp.float32)
    for copy in sends:
        copy.wait_send()


def mp_sum_scratch(chips, rows, cols, dt):
    return [
        pltpu.VMEM((2, chips, rows, cols), dt),
        pltpu.VMEM((2, chips, rows, cols), dt),
        pltpu.VMEM((chips, 2, rows, cols), dt),
        pltpu.VMEM((rows, cols), dt),
        pltpu.VMEM((rows, cols), dt),
        pltpu.VMEM((2, rows, cols), jnp.float32),
        pltpu.SemaphoreType.DMA((4 * chips + 1,)),
        pltpu.SemaphoreType.DMA((4 * chips + 1,)),
    ]


def combined_kernel(parts, *refs):
    n_in = sum(p[2] for p in parts)
    n_out = sum(p[3] for p in parts)
    ins, outs, scratch = refs[:n_in], refs[n_in:n_in + n_out], refs[n_in + n_out:]
    barrier = pltpu.get_barrier_semaphore()
    total = 0
    for peers, _, _, _, _ in parts:
        for cond, axis, peer in peers():
            def signal(axis=axis, peer=peer):
                pl.semaphore_signal(barrier, inc=1, device_id={axis: peer}, device_id_type=MESH)
            if cond is None:
                signal()
                total = total + 1
            else:
                pl.when(cond)(signal)
                total = total + cond.astype(jnp.int32)
    pl.semaphore_wait(barrier, total)
    gens = []
    for _, body, pi, po, ps in parts:
        gens.append(body(ins[:pi], outs[:po], scratch[:ps]))
        ins, outs, scratch = ins[pi:], outs[po:], scratch[ps:]
    while gens:
        for gen in list(gens):
            try:
                next(gen)
            except StopIteration:
                gens.remove(gen)


def combined(parts, inputs, out_shapes, scratch_shapes, cid):
    return pl.pallas_call(
        functools.partial(combined_kernel, parts),
        out_shape=out_shapes,
        in_specs=[pl.BlockSpec(memory_space=pltpu.VMEM)] * len(inputs),
        out_specs=[pl.BlockSpec(memory_space=pltpu.VMEM)] * len(out_shapes),
        scratch_shapes=scratch_shapes,
        compiler_params=pltpu.CompilerParams(collective_id=cid, has_side_effects=True),
    )(*inputs)


def attend(normed, qkv_w, segment, table, mp_index):
    group_rows = normed.shape[0]
    heads_dev = qkv_w.shape[1] // (3 * HD)
    joined = jnp.dot(normed, qkv_w, preferred_element_type=jnp.float32).astype(jnp.bfloat16)
    joined = joined.reshape(group_rows, heads_dev, 3, HD)
    query = joined[:, :, 0]
    keys = joined[:, :, 1]
    vals = joined[:, :, 2]
    head_ids = mp_index * heads_dev + jnp.arange(heads_dev)
    slopes = jnp.exp2(-8.0 * (head_ids + 1).astype(jnp.float32) / H)
    positions = jnp.arange(group_rows)
    distance = (positions[:, None] - positions[None, :]).astype(jnp.float32)
    allowed = (segment[:, None] == segment[None, :]) & (distance >= 0)
    scores = jnp.einsum("thd,shd->hts", query, keys, preferred_element_type=jnp.float32) / jnp.sqrt(
        jnp.float32(HD)
    )
    scores = scores - slopes[:, None, None] * distance[None]
    scores = jnp.where(allowed[None], scores, -jnp.inf)
    probs = jax.nn.softmax(scores, axis=-1).astype(jnp.bfloat16)
    context = jnp.einsum("hts,shd->thd", probs, vals, preferred_element_type=jnp.float32).astype(
        jnp.bfloat16
    )
    context = context.reshape(group_rows, heads_dev * HD)
    key_vals = jnp.stack([keys, vals], 1)
    pages_here = group_rows // PAGE
    key_vals = key_vals.reshape(pages_here, PAGE, 2, heads_dev, HD).transpose(0, 2, 3, 1, 4)
    cache = jnp.zeros((pages_here, 2, heads_dev, PAGE, HD), jnp.bfloat16).at[table].set(key_vals)
    return (context, cache)


def local(hidden_in, segment_ids, page_table, qkv_master, up_master, dense_weight):
    mp_count = lax.axis_size("mp")
    dp_count = lax.axis_size("dp")
    mp_index = lax.axis_index("mp")
    chips = mp_count // 4
    lines = dp_count // RING
    rows = hidden_in.shape[0]
    rows_w = qkv_master.shape[0]
    bf = jnp.bfloat16
    sd = jax.ShapeDtypeStruct
    qkv_t = sd((mp_count, rows_w, qkv_master.shape[-1] // mp_count), bf)
    up_t = sd((mp_count, rows_w, up_master.shape[-1] // mp_count), bf)
    qkv_rows = sd((mp_count * rows_w, qkv_t.shape[-1]), bf)
    qkv_w, up_blk, normed = combined(
        [
            (
                functools.partial(weights_peers, mp_count, lines, RING),
                functools.partial(weights_body, mp_count, lines, RING),
                2, 2, 9,
            ),
            (functools.partial(mp_peers, chips), functools.partial(normed_gather_body, chips), 1, 1, 3),
        ],
        [qkv_master, up_master, hidden_in],
        [
            sd((lines, RING) + qkv_rows.shape, bf),
            sd(up_t.shape, bf),
            sd((2, chips, 2) + hidden_in.shape, bf),
        ],
        exchange_scratch(mp_count, 2)
        + [pltpu.VMEM(qkv_t.shape, bf), pltpu.VMEM(qkv_rows.shape, bf)]
        + dp_scratch(lines, RING)
        + [pltpu.VMEM(qkv_t.shape, bf), pltpu.VMEM(up_t.shape, bf)]
        + [pltpu.VMEM((rows, hidden_in.shape[-1]), bf)]
        + mp_gather_scratch(chips),
        1,
    )
    normed = normed.reshape(mp_count * rows, -1)
    qkv_w = qkv_w.reshape(-1, qkv_t.shape[-1])
    up_piece = up_blk.reshape(mp_count * rows_w, -1)
    context, cache = attend(normed, qkv_w, segment_ids[0], page_table[0], mp_index)
    partial = jnp.dot(context, dense_weight, preferred_element_type=jnp.float32).astype(bf)
    cols = partial.shape[-1]
    up_w, hidden_out, normed_two = combined(
        [
            (functools.partial(dp_peers, lines, RING), functools.partial(dp_gather_body, lines, RING), 1, 1, 2),
            (functools.partial(tail_peers, chips), functools.partial(tail_body, chips), 2, 2, 12),
        ],
        [up_piece, partial.reshape(2, chips, 2, rows, -1), hidden_in],
        [
            sd((lines, RING) + up_piece.shape, bf),
            sd((rows, cols), bf),
            sd((2, chips, 2, rows, cols), bf),
        ],
        dp_scratch(lines, RING)
        + mp_sum_scratch(chips, rows, cols, bf)
        + [pltpu.VMEM((rows, cols), jnp.float32), pltpu.VMEM((rows, cols), bf)]
        + mp_gather_scratch(chips),
        2,
    )
    up_w = up_w.reshape(-1, up_piece.shape[-1])
    normed_two = normed_two.reshape(mp_count * rows, -1)
    upper = jnp.dot(normed_two, up_w, preferred_element_type=jnp.float32)
    activated = jax.nn.gelu(upper, approximate=True).astype(bf)
    return (hidden_out, activated, cache)


def solution(mesh):
    placed = (
        P(("dp", "mp"), None),
        P("dp", None),
        P("dp", None),
        P(("dp", "mp"), None),
        P(("dp", "mp"), None),
        P("mp", None),
    )
    return jax.shard_map(
        local,
        mesh=mesh,
        in_specs=placed,
        out_specs=(P(("dp", "mp"), None), P("dp", "mp"), P("dp", None, "mp", None, None)),
        check_vma=False,
    )
```

```python
import functools

import jax
import jax.numpy as jnp
from jax import lax
from jax.experimental import pallas as pl
from jax.experimental.pallas import tpu as pltpu
from jax.sharding import PartitionSpec as P

H = 16
HD = 128
PAGE = 128
RING = 4
MESH = pl.DeviceIdType.MESH


def layer_norm(values):
    mean_val = jnp.mean(values, -1, keepdims=True)
    centered = values - mean_val
    variance = jnp.mean(centered * centered, -1, keepdims=True)
    return centered * lax.rsqrt(variance + 1e-05)


def _remote(src, dst, send_sem, recv_sem, axis, peer):
    return pltpu.make_async_remote_copy(
        src_ref=src,
        dst_ref=dst,
        send_sem=send_sem,
        recv_sem=recv_sem,
        device_id={axis: peer},
        device_id_type=MESH,
    )


def mp_places(chips):
    me = lax.axis_index("mp")
    per_half = chips * 2
    h, c, k = me // per_half, (me // 2) % chips, me % 2
    far = (1 - h) * per_half + c * 2 + k
    twin = h * per_half + c * 2 + (1 - k)
    mates = [h * per_half + ((c + j) % chips) * 2 + k for j in range(1, chips)]
    return h, c, k, far, twin, mates


def exchange_peers(n, axis):
    me = lax.axis_index(axis)
    return [(None, axis, lax.rem(me + step, n)) for step in range(1, n)]


def exchange_body(n, axis, ins, outs, scratch):
    send_sem, recv_sem, local_sem = scratch
    me = lax.axis_index(axis)
    copies, locals_ = [], []
    for a in range(len(ins)):
        for step in range(1, n):
            peer = lax.rem(me + step, n)
            slot = a * (n - 1) + step - 1
            copy = _remote(ins[a].at[peer], outs[a].at[me], send_sem.at[slot], recv_sem.at[slot], axis, peer)
            copy.start()
            copies.append(copy)
        own = pltpu.make_async_copy(ins[a].at[me], outs[a].at[me], local_sem.at[a])
        own.start()
        locals_.append(own)
    yield
    for own in locals_:
        own.wait()
    for copy in copies:
        copy.wait()


def exchange_scratch(n, count):
    return [
        pltpu.SemaphoreType.DMA((count * (n - 1),)),
        pltpu.SemaphoreType.DMA((count * (n - 1),)),
        pltpu.SemaphoreType.DMA((count,)),
    ]


def dp_peers(lines, ring):
    me = lax.axis_index("dp")
    z, y = me // ring, me % ring
    out = [(z > 0, "dp", me - ring), (z < lines - 1, "dp", me + ring)]
    return out + [(None, "dp", z * ring + (y + k) % ring) for k in range(1, ring)]


def dp_gather_body(lines, ring, ins, outs, scratch):
    (x_ref,), (o_ref,), (send_sem, recv_sem) = ins, outs, scratch
    me = lax.axis_index("dp")
    z, y = me // ring, me % ring
    has_left, has_right = z > 0, z < lines - 1
    sends = []

    def send(cond, src, src_z, peer):
        slot = src_z * ring + y
        copy = _remote(src, o_ref.at[src_z, y], send_sem.at[len(sends)], recv_sem.at[slot], "dp", peer)
        pl.when(cond)(copy.start)
        sends.append((cond, copy))

    def spread(cond, src, src_z):
        for k in range(1, ring):
            send(cond, src, src_z, z * ring + (y + k) % ring)

    def arrive(cond, src_z, peer):
        slot = src_z * ring + y
        copy = _remote(o_ref.at[src_z, y], o_ref.at[src_z, y], send_sem.at[0], recv_sem.at[slot], "dp", peer)
        pl.when(cond)(copy.wait_recv)

    send(has_right, x_ref, z, me + ring)
    send(has_left, x_ref, z, me - ring)
    spread(z >= 0, x_ref, z)
    o_ref[z, y] = x_ref[...]
    yield
    for s in range(1, lines):
        from_left = z - s >= 0
        src_l = jnp.maximum(z - s, 0)
        arrive(from_left, src_l, me - ring)
        send(from_left & has_right, o_ref.at[src_l, y], src_l, me + ring)
        spread(from_left, o_ref.at[src_l, y], src_l)
        from_right = z + s <= lines - 1
        src_r = jnp.minimum(z + s, lines - 1)
        arrive(from_right, src_r, me + ring)
        send(from_right & has_left, o_ref.at[src_r, y], src_r, me - ring)
        spread(from_right, o_ref.at[src_r, y], src_r)
        yield
    for k in range(1, ring):
        yy = (y + k) % ring
        for zz in range(lines):
            slot = zz * ring + yy
            copy = _remote(o_ref.at[zz, yy], o_ref.at[zz, yy], send_sem.at[0], recv_sem.at[slot], "dp", z * ring + yy)
            copy.wait_recv()
    for cond, copy in sends:
        pl.when(cond)(copy.wait_send)


def dp_scratch(lines, ring):
    return [
        pltpu.SemaphoreType.DMA((1 + ring + (lines - 1) * 2 * ring,)),
        pltpu.SemaphoreType.DMA((lines * ring,)),
    ]


def dp_direct_peers(lines, ring):
    me = lax.axis_index("dp")
    z, y = me // ring, me % ring
    out = []
    for d in range(1, lines):
        out += [(z + d < lines, "dp", me + d * ring), (z - d >= 0, "dp", me - d * ring)]
    return out + [(None, "dp", z * ring + (y + k) % ring) for k in range(1, ring)]


def dp_direct_body(lines, ring, ins, outs, scratch):
    (x_ref,), (o_ref,), (send_sem, recv_sem) = ins, outs, scratch
    me = lax.axis_index("dp")
    z, y = me // ring, me % ring
    sends = []

    def send(cond, src, src_z, peer):
        slot = src_z * ring + y
        copy = _remote(src, o_ref.at[src_z, y], send_sem.at[len(sends)], recv_sem.at[slot], "dp", peer)
        pl.when(cond)(copy.start)
        sends.append((cond, copy))

    def spread(cond, src, src_z):
        for k in range(1, ring):
            send(cond, src, src_z, z * ring + (y + k) % ring)

    def arrive(cond, src_z, peer):
        slot = src_z * ring + y
        copy = _remote(o_ref.at[src_z, y], o_ref.at[src_z, y], send_sem.at[0], recv_sem.at[slot], "dp", peer)
        pl.when(cond)(copy.wait_recv)

    always = z >= 0
    spread(always, x_ref, z)
    for d in range(1, lines):
        send(z + d < lines, x_ref, z, me + d * ring)
        send(z - d >= 0, x_ref, z, me - d * ring)
    o_ref[z, y] = x_ref[...]
    yield
    for d in range(1, lines):
        for sign in (1, -1):
            cond = (z + sign * d < lines) & (z + sign * d >= 0)
            src_z = jnp.clip(z + sign * d, 0, lines - 1)
            arrive(cond, src_z, src_z * ring + y)
            spread(cond, o_ref.at[src_z, y], src_z)
        yield
    for k in range(1, ring):
        yy = (y + k) % ring
        for zz in range(lines):
            slot = zz * ring + yy
            copy = _remote(o_ref.at[zz, yy], o_ref.at[zz, yy], send_sem.at[0], recv_sem.at[slot], "dp", z * ring + yy)
            copy.wait_recv()
    for cond, copy in sends:
        pl.when(cond)(copy.wait_send)


def dp_direct_scratch(lines, ring):
    return [
        pltpu.SemaphoreType.DMA((ring - 1 + 2 * (lines - 1) * ring,)),
        pltpu.SemaphoreType.DMA((lines * ring,)),
    ]


def weights_peers(n, lines, ring):
    return exchange_peers(n, "mp") + dp_peers(lines, ring)


def weights_body(n, lines, ring, ins, outs, scratch):
    (qkv_m, up_m), (qkv_full, up_rows) = ins, outs
    ex_send, ex_recv, ex_local, qkv_blk, qkv_rows, dp_send, dp_recv, qkv_t, up_t, up_blk = scratch
    for master, cast in ((qkv_m, qkv_t), (up_m, up_t)):
        width = cast.shape[-1]
        for m in range(n):
            cast[m] = master[:, m * width:(m + 1) * width].astype(cast.dtype)
    yield from exchange_body(n, "mp", [qkv_t, up_t], [qkv_blk, up_blk], (ex_send, ex_recv, ex_local))
    per = qkv_blk.shape[1]
    for m in range(n):
        qkv_rows[m * per:(m + 1) * per, :] = qkv_blk[m]
        up_rows[m * per:(m + 1) * per, :] = up_blk[m]
    yield from dp_gather_body(lines, ring, [qkv_rows], [qkv_full], (dp_send, dp_recv))


def tail_peers(chips):
    return mp_peers(chips) + mp_peers(chips)


def tail_body(chips, ins, outs, scratch):
    (p_ref, h_ref), (hidden_ref, normed_ref) = ins, outs
    sum_scratch, (share, own), gather_scratch = scratch[:8], scratch[8:10], scratch[10:]
    yield from mp_sum_body(chips, [p_ref], [share], sum_scratch)
    stream = h_ref[...].astype(jnp.float32) + share[...]
    hidden_ref[...] = stream.astype(hidden_ref.dtype)
    own[...] = layer_norm(stream).astype(own.dtype)
    yield from mp_gather_body(chips, [own], [normed_ref], gather_scratch)


def normed_gather_body(chips, ins, outs, scratch):
    (h_ref,), (normed_ref,) = ins, outs
    own, gather_scratch = scratch[0], scratch[1:]
    own[...] = layer_norm(h_ref[...].astype(jnp.float32)).astype(own.dtype)
    yield from mp_gather_body(chips, [own], [normed_ref], gather_scratch)


def mp_peers(chips):
    _, _, _, far, twin, mates = mp_places(chips)
    return [(None, "mp", peer) for peer in [far, twin] + mates]


def mp_gather_body(chips, ins, outs, scratch):
    (x_ref,), (o_ref,), (send_sem, recv_sem) = ins, outs, scratch
    h, c, k, far, twin, mates = mp_places(chips)
    sends = []

    def send(src, hh, cc, kk, peer):
        slot = (hh * chips + cc) * 2 + kk
        copy = _remote(src, o_ref.at[hh, cc, kk], send_sem.at[len(sends)], recv_sem.at[slot], "mp", peer)
        copy.start()
        sends.append(copy)

    def arrive(hh, cc, kk, peer):
        slot = (hh * chips + cc) * 2 + kk
        copy = _remote(o_ref.at[hh, cc, kk], o_ref.at[hh, cc, kk], send_sem.at[0], recv_sem.at[slot], "mp", peer)
        copy.wait_recv()

    send(x_ref, h, c, k, far)
    for peer in mates:
        send(x_ref, h, c, k, peer)
    send(x_ref, h, c, k, twin)
    o_ref[h, c, k] = x_ref[...]
    yield
    arrive(1 - h, c, k, far)
    for peer in mates:
        send(o_ref.at[1 - h, c, k], 1 - h, c, k, peer)
    send(o_ref.at[1 - h, c, k], 1 - h, c, k, twin)
    yield
    for j in range(1, chips):
        cc = (c + j) % chips
        for hh in (h, 1 - h):
            arrive(hh, cc, k, mates[j - 1])
            send(o_ref.at[hh, cc, k], hh, cc, k, twin)
    yield
    for hh in range(2):
        for cc in range(chips):
            arrive(hh, cc, 1 - k, twin)
    for copy in sends:
        copy.wait_send()


def mp_gather_scratch(chips):
    return [pltpu.SemaphoreType.DMA((4 * chips,)), pltpu.SemaphoreType.DMA((4 * chips,))]


def mp_sum_body(chips, ins, outs, scratch):
    (p_ref,), (o_ref,) = ins, outs
    twin_in, pair, mate_in, far_out, far_in, acc, send_sem, recv_sem = scratch
    h, c, k, far, twin, mates = mp_places(chips)
    sends = []

    def send(src, dst, slot, peer):
        copy = _remote(src, dst, send_sem.at[len(sends)], recv_sem.at[slot], "mp", peer)
        copy.start()
        sends.append(copy)

    def arrive(dst, slot, peer):
        _remote(dst, dst, send_sem.at[0], recv_sem.at[slot], "mp", peer).wait_recv()

    for hh in range(2):
        for cc in range(chips):
            send(p_ref.at[hh, cc, 1 - k], twin_in.at[hh, cc], hh * chips + cc, twin)
    yield
    for j in range(1, chips):
        cc = (c + j) % chips
        for hh in range(2):
            arrive(twin_in.at[hh, cc], hh * chips + cc, twin)
            pair[hh, cc] = (
                p_ref[hh, cc, k].astype(jnp.float32) + twin_in[hh, cc].astype(jnp.float32)
            ).astype(pair.dtype)
            send(pair.at[hh, cc], mate_in.at[c, hh], 2 * chips + c * 2 + hh, mates[j - 1])
    for hh in range(2):
        arrive(twin_in.at[hh, c], hh * chips + c, twin)
        acc[hh] = p_ref[hh, c, k].astype(jnp.float32) + twin_in[hh, c].astype(jnp.float32)
    yield
    for j in range(1, chips):
        cc = (c + j) % chips
        for hh in range(2):
            arrive(mate_in.at[cc, hh], 2 * chips + cc * 2 + hh, mates[j - 1])
            acc[hh] = acc[hh] + mate_in[cc, hh].astype(jnp.float32)
    far_out[...] = acc[1 - h].astype(far_out.dtype)
    send(far_out, far_in, 4 * chips, far)
    yield
    arrive(far_in, 4 * chips, far)
    o_ref[...] = acc[h] + far_in[...].astype(jnp.float32)
    for copy in sends:
        copy.wait_send()


def mp_sum_scratch(chips, rows, cols, dt):
    return [
        pltpu.VMEM((2, chips, rows, cols), dt),
        pltpu.VMEM((2, chips, rows, cols), dt),
        pltpu.VMEM((chips, 2, rows, cols), dt),
        pltpu.VMEM((rows, cols), dt),
        pltpu.VMEM((rows, cols), dt),
        pltpu.VMEM((2, rows, cols), jnp.float32),
        pltpu.SemaphoreType.DMA((4 * chips + 1,)),
        pltpu.SemaphoreType.DMA((4 * chips + 1,)),
    ]


def combined_kernel(parts, *refs):
    n_in = sum(p[2] for p in parts)
    n_out = sum(p[3] for p in parts)
    ins, outs, scratch = refs[:n_in], refs[n_in:n_in + n_out], refs[n_in + n_out:]
    barrier = pltpu.get_barrier_semaphore()
    total = 0
    for peers, _, _, _, _ in parts:
        for cond, axis, peer in peers():
            def signal(axis=axis, peer=peer):
                pl.semaphore_signal(barrier, inc=1, device_id={axis: peer}, device_id_type=MESH)
            if cond is None:
                signal()
                total = total + 1
            else:
                pl.when(cond)(signal)
                total = total + cond.astype(jnp.int32)
    pl.semaphore_wait(barrier, total)
    gens = []
    for _, body, pi, po, ps in parts:
        gens.append(body(ins[:pi], outs[:po], scratch[:ps]))
        ins, outs, scratch = ins[pi:], outs[po:], scratch[ps:]
    while gens:
        for gen in list(gens):
            try:
                next(gen)
            except StopIteration:
                gens.remove(gen)


def combined(parts, inputs, out_shapes, scratch_shapes, cid):
    return pl.pallas_call(
        functools.partial(combined_kernel, parts),
        out_shape=out_shapes,
        in_specs=[pl.BlockSpec(memory_space=pltpu.VMEM)] * len(inputs),
        out_specs=[pl.BlockSpec(memory_space=pltpu.VMEM)] * len(out_shapes),
        scratch_shapes=scratch_shapes,
        compiler_params=pltpu.CompilerParams(collective_id=cid, has_side_effects=True),
    )(*inputs)


def attend(normed, qkv_w, segment, table, mp_index):
    group_rows = normed.shape[0]
    heads_dev = qkv_w.shape[1] // (3 * HD)
    joined = jnp.dot(normed, qkv_w, preferred_element_type=jnp.float32).astype(jnp.bfloat16)
    joined = joined.reshape(group_rows, heads_dev, 3, HD)
    query = joined[:, :, 0]
    keys = joined[:, :, 1]
    vals = joined[:, :, 2]
    head_ids = mp_index * heads_dev + jnp.arange(heads_dev)
    slopes = jnp.exp2(-8.0 * (head_ids + 1).astype(jnp.float32) / H)
    positions = jnp.arange(group_rows)
    distance = (positions[:, None] - positions[None, :]).astype(jnp.float32)
    allowed = (segment[:, None] == segment[None, :]) & (distance >= 0)
    scores = jnp.einsum("thd,shd->hts", query, keys, preferred_element_type=jnp.float32) / jnp.sqrt(
        jnp.float32(HD)
    )
    scores = scores - slopes[:, None, None] * distance[None]
    scores = jnp.where(allowed[None], scores, -jnp.inf)
    probs = jax.nn.softmax(scores, axis=-1).astype(jnp.bfloat16)
    context = jnp.einsum("hts,shd->thd", probs, vals, preferred_element_type=jnp.float32).astype(
        jnp.bfloat16
    )
    context = context.reshape(group_rows, heads_dev * HD)
    key_vals = jnp.stack([keys, vals], 1)
    pages_here = group_rows // PAGE
    key_vals = key_vals.reshape(pages_here, PAGE, 2, heads_dev, HD).transpose(0, 2, 3, 1, 4)
    cache = jnp.zeros((pages_here, 2, heads_dev, PAGE, HD), jnp.bfloat16).at[table].set(key_vals)
    return (context, cache)


def local(hidden_in, segment_ids, page_table, qkv_master, up_master, dense_weight):
    mp_count = lax.axis_size("mp")
    dp_count = lax.axis_size("dp")
    mp_index = lax.axis_index("mp")
    chips = mp_count // 4
    lines = dp_count // RING
    rows = hidden_in.shape[0]
    rows_w = qkv_master.shape[0]
    bf = jnp.bfloat16
    sd = jax.ShapeDtypeStruct
    qkv_t = sd((mp_count, rows_w, qkv_master.shape[-1] // mp_count), bf)
    up_t = sd((mp_count, rows_w, up_master.shape[-1] // mp_count), bf)
    qkv_rows = sd((mp_count * rows_w, qkv_t.shape[-1]), bf)
    qkv_w, up_blk, normed = combined(
        [
            (
                functools.partial(weights_peers, mp_count, lines, RING),
                functools.partial(weights_body, mp_count, lines, RING),
                2, 2, 10,
            ),
            (functools.partial(mp_peers, chips), functools.partial(normed_gather_body, chips), 1, 1, 3),
        ],
        [qkv_master, up_master, hidden_in],
        [
            sd((lines, RING) + qkv_rows.shape, bf),
            sd((mp_count * rows_w, up_t.shape[-1]), bf),
            sd((2, chips, 2) + hidden_in.shape, bf),
        ],
        exchange_scratch(mp_count, 2)
        + [pltpu.VMEM(qkv_t.shape, bf), pltpu.VMEM(qkv_rows.shape, bf)]
        + dp_scratch(lines, RING)
        + [pltpu.VMEM(qkv_t.shape, bf), pltpu.VMEM(up_t.shape, bf), pltpu.VMEM(up_t.shape, bf)]
        + [pltpu.VMEM((rows, hidden_in.shape[-1]), bf)]
        + mp_gather_scratch(chips),
        1,
    )
    normed = normed.reshape(mp_count * rows, -1)
    qkv_w = qkv_w.reshape(-1, qkv_t.shape[-1])
    up_piece = up_blk
    context, cache = attend(normed, qkv_w, segment_ids[0], page_table[0], mp_index)
    partial = jnp.dot(context, dense_weight, preferred_element_type=jnp.float32).astype(bf)
    cols = partial.shape[-1]
    up_w, hidden_out, normed_two = combined(
        [
            (functools.partial(dp_peers, lines, RING), functools.partial(dp_gather_body, lines, RING), 1, 1, 2),
            (functools.partial(tail_peers, chips), functools.partial(tail_body, chips), 2, 2, 12),
        ],
        [up_piece, partial.reshape(2, chips, 2, rows, -1), hidden_in],
        [
            sd((lines, RING) + up_piece.shape, bf),
            sd((rows, cols), bf),
            sd((2, chips, 2, rows, cols), bf),
        ],
        dp_scratch(lines, RING)
        + mp_sum_scratch(chips, rows, cols, bf)
        + [pltpu.VMEM((rows, cols), jnp.float32), pltpu.VMEM((rows, cols), bf)]
        + mp_gather_scratch(chips),
        2,
    )
    up_w = up_w.reshape(-1, up_piece.shape[-1])
    normed_two = normed_two.reshape(mp_count * rows, -1)
    upper = jnp.dot(normed_two, up_w, preferred_element_type=jnp.float32)
    activated = jax.nn.gelu(upper, approximate=True).astype(bf)
    return (hidden_out, activated, cache)


def solution(mesh):
    placed = (
        P(("dp", "mp"), None),
        P("dp", None),
        P("dp", None),
        P(("dp", "mp"), None),
        P(("dp", "mp"), None),
        P("mp", None),
    )
    return jax.shard_map(
        local,
        mesh=mesh,
        in_specs=placed,
        out_specs=(P(("dp", "mp"), None), P("dp", "mp"), P("dp", None, "mp", None, None)),
        check_vma=False,
    )
```

```python
import functools

import jax
import jax.numpy as jnp
from jax import lax
from jax.experimental import pallas as pl
from jax.experimental.pallas import tpu as pltpu
from jax.sharding import PartitionSpec as P

H = 16
HD = 128
PAGE = 128
RING = 4
MESH = pl.DeviceIdType.MESH


def layer_norm(values):
    mean_val = jnp.mean(values, -1, keepdims=True)
    centered = values - mean_val
    variance = jnp.mean(centered * centered, -1, keepdims=True)
    return centered * lax.rsqrt(variance + 1e-05)


def _remote(src, dst, send_sem, recv_sem, axis, peer):
    return pltpu.make_async_remote_copy(
        src_ref=src,
        dst_ref=dst,
        send_sem=send_sem,
        recv_sem=recv_sem,
        device_id={axis: peer},
        device_id_type=MESH,
    )


def mp_places(chips):
    me = lax.axis_index("mp")
    per_half = chips * 2
    h, c, k = me // per_half, (me // 2) % chips, me % 2
    far = (1 - h) * per_half + c * 2 + k
    twin = h * per_half + c * 2 + (1 - k)
    mates = [h * per_half + ((c + j) % chips) * 2 + k for j in range(1, chips)]
    return h, c, k, far, twin, mates


def exchange_peers(n, axis):
    me = lax.axis_index(axis)
    return [(None, axis, lax.rem(me + step, n)) for step in range(1, n)]


def exchange_body(n, axis, ins, outs, scratch):
    send_sem, recv_sem, local_sem = scratch
    me = lax.axis_index(axis)
    copies, locals_ = [], []
    for a in range(len(ins)):
        for step in range(1, n):
            peer = lax.rem(me + step, n)
            slot = a * (n - 1) + step - 1
            copy = _remote(ins[a].at[peer], outs[a].at[me], send_sem.at[slot], recv_sem.at[slot], axis, peer)
            copy.start()
            copies.append(copy)
        own = pltpu.make_async_copy(ins[a].at[me], outs[a].at[me], local_sem.at[a])
        own.start()
        locals_.append(own)
    yield
    for own in locals_:
        own.wait()
    for copy in copies:
        copy.wait()


def exchange_scratch(n, count):
    return [
        pltpu.SemaphoreType.DMA((count * (n - 1),)),
        pltpu.SemaphoreType.DMA((count * (n - 1),)),
        pltpu.SemaphoreType.DMA((count,)),
    ]


def dp_peers(lines, ring):
    me = lax.axis_index("dp")
    z, y = me // ring, me % ring
    out = [(z > 0, "dp", me - ring), (z < lines - 1, "dp", me + ring)]
    return out + [(None, "dp", z * ring + (y + k) % ring) for k in range(1, ring)]


def dp_gather_body(lines, ring, ins, outs, scratch):
    (x_ref,), (o_ref,), (send_sem, recv_sem) = ins, outs, scratch
    me = lax.axis_index("dp")
    z, y = me // ring, me % ring
    has_left, has_right = z > 0, z < lines - 1
    sends = []

    def send(cond, src, src_z, peer):
        slot = src_z * ring + y
        copy = _remote(src, o_ref.at[src_z, y], send_sem.at[len(sends)], recv_sem.at[slot], "dp", peer)
        pl.when(cond)(copy.start)
        sends.append((cond, copy))

    def spread(cond, src, src_z):
        for k in range(1, ring):
            send(cond, src, src_z, z * ring + (y + k) % ring)

    def arrive(cond, src_z, peer):
        slot = src_z * ring + y
        copy = _remote(o_ref.at[src_z, y], o_ref.at[src_z, y], send_sem.at[0], recv_sem.at[slot], "dp", peer)
        pl.when(cond)(copy.wait_recv)

    send(has_right, x_ref, z, me + ring)
    send(has_left, x_ref, z, me - ring)
    spread(z >= 0, x_ref, z)
    o_ref[z, y] = x_ref[...]
    yield
    for s in range(1, lines):
        from_left = z - s >= 0
        src_l = jnp.maximum(z - s, 0)
        arrive(from_left, src_l, me - ring)
        send(from_left & has_right, o_ref.at[src_l, y], src_l, me + ring)
        spread(from_left, o_ref.at[src_l, y], src_l)
        from_right = z + s <= lines - 1
        src_r = jnp.minimum(z + s, lines - 1)
        arrive(from_right, src_r, me + ring)
        send(from_right & has_left, o_ref.at[src_r, y], src_r, me - ring)
        spread(from_right, o_ref.at[src_r, y], src_r)
        yield
    for k in range(1, ring):
        yy = (y + k) % ring
        for zz in range(lines):
            slot = zz * ring + yy
            copy = _remote(o_ref.at[zz, yy], o_ref.at[zz, yy], send_sem.at[0], recv_sem.at[slot], "dp", z * ring + yy)
            copy.wait_recv()
    for cond, copy in sends:
        pl.when(cond)(copy.wait_send)


def dp_scratch(lines, ring):
    return [
        pltpu.SemaphoreType.DMA((1 + ring + (lines - 1) * 2 * ring,)),
        pltpu.SemaphoreType.DMA((lines * ring,)),
    ]


def dp_direct_peers(lines, ring):
    me = lax.axis_index("dp")
    z, y = me // ring, me % ring
    out = []
    for d in range(1, lines):
        out += [(z + d < lines, "dp", me + d * ring), (z - d >= 0, "dp", me - d * ring)]
    return out + [(None, "dp", z * ring + (y + k) % ring) for k in range(1, ring)]


def dp_direct_body(lines, ring, ins, outs, scratch):
    (x_ref,), (o_ref,), (send_sem, recv_sem) = ins, outs, scratch
    me = lax.axis_index("dp")
    z, y = me // ring, me % ring
    sends = []

    def send(cond, src, src_z, peer):
        slot = src_z * ring + y
        copy = _remote(src, o_ref.at[src_z, y], send_sem.at[len(sends)], recv_sem.at[slot], "dp", peer)
        pl.when(cond)(copy.start)
        sends.append((cond, copy))

    def spread(cond, src, src_z):
        for k in range(1, ring):
            send(cond, src, src_z, z * ring + (y + k) % ring)

    def arrive(cond, src_z, peer):
        slot = src_z * ring + y
        copy = _remote(o_ref.at[src_z, y], o_ref.at[src_z, y], send_sem.at[0], recv_sem.at[slot], "dp", peer)
        pl.when(cond)(copy.wait_recv)

    always = z >= 0
    spread(always, x_ref, z)
    for d in range(1, lines):
        send(z + d < lines, x_ref, z, me + d * ring)
        send(z - d >= 0, x_ref, z, me - d * ring)
    o_ref[z, y] = x_ref[...]
    yield
    for d in range(1, lines):
        for sign in (1, -1):
            cond = (z + sign * d < lines) & (z + sign * d >= 0)
            src_z = jnp.clip(z + sign * d, 0, lines - 1)
            arrive(cond, src_z, src_z * ring + y)
            spread(cond, o_ref.at[src_z, y], src_z)
        yield
    for k in range(1, ring):
        yy = (y + k) % ring
        for zz in range(lines):
            slot = zz * ring + yy
            copy = _remote(o_ref.at[zz, yy], o_ref.at[zz, yy], send_sem.at[0], recv_sem.at[slot], "dp", z * ring + yy)
            copy.wait_recv()
    for cond, copy in sends:
        pl.when(cond)(copy.wait_send)


def dp_direct_scratch(lines, ring):
    return [
        pltpu.SemaphoreType.DMA((ring - 1 + 2 * (lines - 1) * ring,)),
        pltpu.SemaphoreType.DMA((lines * ring,)),
    ]


def weights_peers(n, lines, ring):
    return exchange_peers(n, "mp") + dp_peers(lines, ring)


def weights_body(n, lines, ring, ins, outs, scratch):
    (qkv_m, up_m), (qkv_full, up_rows) = ins, outs
    ex_send, ex_recv, ex_local, qkv_blk, qkv_rows, dp_send, dp_recv, qkv_t, up_t, up_blk = scratch
    for master, cast in ((qkv_m, qkv_t), (up_m, up_t)):
        width = cast.shape[-1]
        for m in range(n):
            cast[m] = master[:, m * width:(m + 1) * width].astype(cast.dtype)
    yield from exchange_body(n, "mp", [qkv_t, up_t], [qkv_blk, up_blk], (ex_send, ex_recv, ex_local))
    per = qkv_blk.shape[1]
    for m in range(n):
        qkv_rows[m * per:(m + 1) * per, :] = qkv_blk[m]
        up_rows[m * per:(m + 1) * per, :] = up_blk[m]
    yield from dp_gather_body(lines, ring, [qkv_rows], [qkv_full], (dp_send, dp_recv))


def tail_peers(chips):
    return mp_peers(chips) + mp_peers(chips)


def tail_body(chips, ins, outs, scratch):
    (p_ref, h_ref), (hidden_ref, normed_ref) = ins, outs
    sum_scratch, (share, own), gather_scratch = scratch[:8], scratch[8:10], scratch[10:]
    yield from mp_sum_body(chips, [p_ref], [share], sum_scratch)
    stream = h_ref[...].astype(jnp.float32) + share[...]
    hidden_ref[...] = stream
    own[...] = layer_norm(stream).astype(own.dtype)
    yield from mp_gather_body(chips, [own], [normed_ref], gather_scratch)


def normed_gather_body(chips, ins, outs, scratch):
    (h_ref,), (normed_ref,) = ins, outs
    own, gather_scratch = scratch[0], scratch[1:]
    own[...] = layer_norm(h_ref[...].astype(jnp.float32)).astype(own.dtype)
    yield from mp_gather_body(chips, [own], [normed_ref], gather_scratch)


def mp_peers(chips):
    _, _, _, far, twin, mates = mp_places(chips)
    return [(None, "mp", peer) for peer in [far, twin] + mates]


def mp_gather_body(chips, ins, outs, scratch):
    (x_ref,), (o_ref,), (send_sem, recv_sem) = ins, outs, scratch
    h, c, k, far, twin, mates = mp_places(chips)
    rows = x_ref.shape[0]
    sends = []

    def view(hh, cc, kk):
        return o_ref.at[pl.ds(((hh * chips + cc) * 2 + kk) * rows, rows)]

    def send(src, hh, cc, kk, peer):
        slot = (hh * chips + cc) * 2 + kk
        copy = _remote(src, view(hh, cc, kk), send_sem.at[len(sends)], recv_sem.at[slot], "mp", peer)
        copy.start()
        sends.append(copy)

    def arrive(hh, cc, kk, peer):
        slot = (hh * chips + cc) * 2 + kk
        copy = _remote(view(hh, cc, kk), view(hh, cc, kk), send_sem.at[0], recv_sem.at[slot], "mp", peer)
        copy.wait_recv()

    send(x_ref, h, c, k, far)
    for peer in mates:
        send(x_ref, h, c, k, peer)
    send(x_ref, h, c, k, twin)
    o_ref[pl.ds(((h * chips + c) * 2 + k) * rows, rows), :] = x_ref[...]
    yield
    arrive(1 - h, c, k, far)
    for peer in mates:
        send(view(1 - h, c, k), 1 - h, c, k, peer)
    send(view(1 - h, c, k), 1 - h, c, k, twin)
    yield
    for j in range(1, chips):
        cc = (c + j) % chips
        for hh in (h, 1 - h):
            arrive(hh, cc, k, mates[j - 1])
            send(view(hh, cc, k), hh, cc, k, twin)
    yield
    for hh in range(2):
        for cc in range(chips):
            arrive(hh, cc, 1 - k, twin)
    for copy in sends:
        copy.wait_send()


def mp_gather_scratch(chips):
    return [pltpu.SemaphoreType.DMA((4 * chips,)), pltpu.SemaphoreType.DMA((4 * chips,))]


def mp_sum_body(chips, ins, outs, scratch):
    (p_ref,), (o_ref,) = ins, outs
    twin_in, pair, mate_in, far_out, far_in, acc, send_sem, recv_sem = scratch
    h, c, k, far, twin, mates = mp_places(chips)
    sends = []

    def send(src, dst, slot, peer):
        copy = _remote(src, dst, send_sem.at[len(sends)], recv_sem.at[slot], "mp", peer)
        copy.start()
        sends.append(copy)

    def arrive(dst, slot, peer):
        _remote(dst, dst, send_sem.at[0], recv_sem.at[slot], "mp", peer).wait_recv()

    for hh in range(2):
        for cc in range(chips):
            send(p_ref.at[hh, cc, 1 - k], twin_in.at[hh, cc], hh * chips + cc, twin)
    yield
    for j in range(1, chips):
        cc = (c + j) % chips
        for hh in range(2):
            arrive(twin_in.at[hh, cc], hh * chips + cc, twin)
            pair[hh, cc] = (
                p_ref[hh, cc, k].astype(jnp.float32) + twin_in[hh, cc].astype(jnp.float32)
            ).astype(pair.dtype)
            send(pair.at[hh, cc], mate_in.at[c, hh], 2 * chips + c * 2 + hh, mates[j - 1])
    for hh in range(2):
        arrive(twin_in.at[hh, c], hh * chips + c, twin)
        acc[hh] = p_ref[hh, c, k].astype(jnp.float32) + twin_in[hh, c].astype(jnp.float32)
    yield
    for j in range(1, chips):
        cc = (c + j) % chips
        for hh in range(2):
            arrive(mate_in.at[cc, hh], 2 * chips + cc * 2 + hh, mates[j - 1])
            acc[hh] = acc[hh] + mate_in[cc, hh].astype(jnp.float32)
    far_out[...] = acc[1 - h].astype(far_out.dtype)
    send(far_out, far_in, 4 * chips, far)
    yield
    arrive(far_in, 4 * chips, far)
    o_ref[...] = acc[h] + far_in[...].astype(jnp.float32)
    for copy in sends:
        copy.wait_send()


def mp_sum_scratch(chips, rows, cols, dt):
    return [
        pltpu.VMEM((2, chips, rows, cols), dt),
        pltpu.VMEM((2, chips, rows, cols), dt),
        pltpu.VMEM((chips, 2, rows, cols), dt),
        pltpu.VMEM((rows, cols), dt),
        pltpu.VMEM((rows, cols), dt),
        pltpu.VMEM((2, rows, cols), jnp.float32),
        pltpu.SemaphoreType.DMA((4 * chips + 1,)),
        pltpu.SemaphoreType.DMA((4 * chips + 1,)),
    ]


def combined_kernel(parts, *refs):
    n_in = sum(p[2] for p in parts)
    n_out = sum(p[3] for p in parts)
    ins, outs, scratch = refs[:n_in], refs[n_in:n_in + n_out], refs[n_in + n_out:]
    barrier = pltpu.get_barrier_semaphore()
    total = 0
    for peers, _, _, _, _ in parts:
        for cond, axis, peer in peers():
            def signal(axis=axis, peer=peer):
                pl.semaphore_signal(barrier, inc=1, device_id={axis: peer}, device_id_type=MESH)
            if cond is None:
                signal()
                total = total + 1
            else:
                pl.when(cond)(signal)
                total = total + cond.astype(jnp.int32)
    pl.semaphore_wait(barrier, total)
    gens = []
    for _, body, pi, po, ps in parts:
        gens.append(body(ins[:pi], outs[:po], scratch[:ps]))
        ins, outs, scratch = ins[pi:], outs[po:], scratch[ps:]
    while gens:
        for gen in list(gens):
            try:
                next(gen)
            except StopIteration:
                gens.remove(gen)


def combined(parts, inputs, out_shapes, scratch_shapes, cid):
    return pl.pallas_call(
        functools.partial(combined_kernel, parts),
        out_shape=out_shapes,
        in_specs=[pl.BlockSpec(memory_space=pltpu.VMEM)] * len(inputs),
        out_specs=[pl.BlockSpec(memory_space=pltpu.VMEM)] * len(out_shapes),
        scratch_shapes=scratch_shapes,
        compiler_params=pltpu.CompilerParams(collective_id=cid, has_side_effects=True),
    )(*inputs)


def attend(normed, qkv_w, segment, table, mp_index):
    group_rows = normed.shape[0]
    heads_dev = qkv_w.shape[1] // (3 * HD)
    joined = jnp.dot(normed, qkv_w, preferred_element_type=jnp.float32).astype(jnp.bfloat16)
    joined = joined.reshape(group_rows, heads_dev, 3, HD)
    query = joined[:, :, 0]
    keys = joined[:, :, 1]
    vals = joined[:, :, 2]
    head_ids = mp_index * heads_dev + jnp.arange(heads_dev)
    slopes = jnp.exp2(-8.0 * (head_ids + 1).astype(jnp.float32) / H)
    positions = jnp.arange(group_rows)
    distance = (positions[:, None] - positions[None, :]).astype(jnp.float32)
    allowed = (segment[:, None] == segment[None, :]) & (distance >= 0)
    scores = jnp.einsum("thd,shd->hts", query, keys, preferred_element_type=jnp.float32) / jnp.sqrt(
        jnp.float32(HD)
    )
    scores = scores - slopes[:, None, None] * distance[None]
    scores = jnp.where(allowed[None], scores, -jnp.inf)
    probs = jax.nn.softmax(scores, axis=-1).astype(jnp.bfloat16)
    context = jnp.einsum("hts,shd->thd", probs, vals, preferred_element_type=jnp.float32).astype(
        jnp.bfloat16
    )
    context = context.reshape(group_rows, heads_dev * HD)
    key_vals = jnp.stack([keys, vals], 1)
    pages_here = group_rows // PAGE
    key_vals = key_vals.reshape(pages_here, PAGE, 2, heads_dev, HD).transpose(0, 2, 3, 1, 4)
    slots = jnp.arange(pages_here)
    owner = jnp.sum(slots[None, :] * (table[None, :] == slots[:, None]), axis=1)
    cache = key_vals[owner]
    return (context, cache)


def local(hidden_in, segment_ids, page_table, qkv_master, up_master, dense_weight):
    mp_count = lax.axis_size("mp")
    dp_count = lax.axis_size("dp")
    mp_index = lax.axis_index("mp")
    chips = mp_count // 4
    lines = dp_count // RING
    rows = hidden_in.shape[0]
    rows_w = qkv_master.shape[0]
    bf = jnp.bfloat16
    sd = jax.ShapeDtypeStruct
    qkv_t = sd((mp_count, rows_w, qkv_master.shape[-1] // mp_count), bf)
    up_t = sd((mp_count, rows_w, up_master.shape[-1] // mp_count), bf)
    qkv_rows = sd((mp_count * rows_w, qkv_t.shape[-1]), bf)
    qkv_w, up_blk, normed = combined(
        [
            (
                functools.partial(weights_peers, mp_count, lines, RING),
                functools.partial(weights_body, mp_count, lines, RING),
                2, 2, 10,
            ),
            (functools.partial(mp_peers, chips), functools.partial(normed_gather_body, chips), 1, 1, 3),
        ],
        [qkv_master, up_master, hidden_in],
        [
            sd((lines, RING) + qkv_rows.shape, bf),
            sd((mp_count * rows_w, up_t.shape[-1]), bf),
            sd((mp_count * rows, hidden_in.shape[-1]), bf),
        ],
        exchange_scratch(mp_count, 2)
        + [pltpu.VMEM(qkv_t.shape, bf), pltpu.VMEM(qkv_rows.shape, bf)]
        + dp_scratch(lines, RING)
        + [pltpu.VMEM(qkv_t.shape, bf), pltpu.VMEM(up_t.shape, bf), pltpu.VMEM(up_t.shape, bf)]
        + [pltpu.VMEM((rows, hidden_in.shape[-1]), bf)]
        + mp_gather_scratch(chips),
        1,
    )
    normed = normed.reshape(mp_count * rows, -1)
    qkv_w = qkv_w.reshape(-1, qkv_t.shape[-1])
    up_piece = up_blk
    context, cache = attend(normed, qkv_w, segment_ids[0], page_table[0], mp_index)
    partial = jnp.dot(context, dense_weight, preferred_element_type=jnp.float32).astype(bf)
    cols = partial.shape[-1]
    up_w, hidden_out, normed_two = combined(
        [
            (functools.partial(dp_peers, lines, RING), functools.partial(dp_gather_body, lines, RING), 1, 1, 2),
            (functools.partial(tail_peers, chips), functools.partial(tail_body, chips), 2, 2, 12),
        ],
        [up_piece, partial.reshape(2, chips, 2, rows, -1), hidden_in],
        [
            sd((lines, RING) + up_piece.shape, bf),
            sd((rows, cols), jnp.float32),
            sd((mp_count * rows, cols), bf),
        ],
        dp_scratch(lines, RING)
        + mp_sum_scratch(chips, rows, cols, bf)
        + [pltpu.VMEM((rows, cols), jnp.float32), pltpu.VMEM((rows, cols), bf)]
        + mp_gather_scratch(chips),
        2,
    )
    up_w = up_w.reshape(-1, up_piece.shape[-1])
    normed_two = normed_two.reshape(mp_count * rows, -1)
    upper = jnp.dot(normed_two, up_w, preferred_element_type=jnp.float32)
    activated = jax.nn.gelu(upper, approximate=True).astype(bf)
    return (hidden_out.astype(bf), activated, cache)


def solution(mesh):
    placed = (
        P(("dp", "mp"), None),
        P("dp", None),
        P("dp", None),
        P(("dp", "mp"), None),
        P(("dp", "mp"), None),
        P("mp", None),
    )
    return jax.shard_map(
        local,
        mesh=mesh,
        in_specs=placed,
        out_specs=(P(("dp", "mp"), None), P("dp", "mp"), P("dp", None, "mp", None, None)),
        check_vma=False,
    )
```
